32 devices in a mesh: beam: 4 (over x, core), det: 2 (over y), slab: 4 (over z).
Axes of the slice: x: 2, y: 2, z: 4, core: 2. Of those that a mesh axis runs over, the one named last changes fastest.
Arguments:
- concentration: float32 [4, 32, 1024, 256], P(None, 'slab', 'beam', 'det'), may hold values from 0.1 to 1
- cross_section: float32 [4, 16], replicated, may hold values from 0.2 to 2
- line_attenuation: float32 [4], replicated, may hold values from 0.5 to 2
- energy_index: int32 [4], replicated, may hold values from 0 to 15
- fan_offset: int32 [256], replicated, may hold values from 0 to 28
- fan_weight: int32 [256, 4], replicated, may hold values from 1 to 3
- measured: float32 [4, 256, 256], P(None, None, 'det'), may hold values from 0 to 6
Outputs:
- voxel_grad: float32 [4, 32, 1024, 256], P(None, 'slab', 'beam', 'det')
- residual: float32 [4, 256, 256], P(None, ('beam', 'slab'), 'det')
The draws below stay inside these ranges and needn't reach their ends.
All inputs are finite; a program needn't handle non-finite values.
Results may differ from the reference program's by a relative error of at most 0.00013.
Values sent between devices are 32-bit elements; how exact they have to be, the bound alone decides.
No kernel may reach another device: no remote copies, remote signals or barrier semaphores. Data moves between devices by JAX's collectives and lax.ppermute only.
A program may use at most 128 MiB of HBM per device.

```python
import math
import jax
import jax.numpy as jnp
from jax import lax

S = 4
ENERGIES = 16
E_WIN = 4
K = 256
FAN = 4
NX = 1024
NY = 256
NZ = 32


def place_ends(drawn, own_key, smallest, largest):
    spot = [jax.random.randint(jax.random.fold_in(own_key, axis), (), 0, length) for axis, length in enumerate(drawn.shape)]
    main_axis = drawn.shape.index(max(drawn.shape))
    neighbour = spot[:main_axis] + [(spot[main_axis] + 1) % drawn.shape[main_axis]] + spot[main_axis + 1:]
    return drawn.at[tuple(spot)].set(smallest).at[tuple(neighbour)].set(largest)


def level_of(stream_key, shape, cuts, low, high):
    level, own = 1.0, jax.random.fold_in(stream_key, 6)
    for position, parts in cuts:
        draws = jnp.exp(jax.random.uniform(jax.random.fold_in(own, position), (parts,), jnp.float32, low / len(cuts), high / len(cuts)))
        level = level * jnp.repeat(draws, shape[position] // parts).reshape([-1 if axis == position else 1 for axis in range(len(shape))])
    return level


def setup_inputs(seed: int = 0) -> dict:
    seeds = jax.random.split(jax.random.key(seed), 8)
    return {
        "concentration": jnp.clip(jnp.exp(math.log(1.0) - 2.3025851 * jax.random.uniform(seeds[0], (S, NZ, NX, NY), jnp.float32) ** level_of(seeds[0], (S, NZ, NX, NY), ((1, 4), (2, 4), (3, 2)), -0.2, 0.2)), 0.1, 1.0),
        "cross_section": jnp.clip(jnp.exp(jax.random.uniform(seeds[1], (S, ENERGIES), jnp.float32, math.log(0.2), math.log(2.0))), 0.2, 2.0),
        "line_attenuation": jnp.clip(jnp.exp(jax.random.uniform(seeds[2], (S,), jnp.float32, math.log(0.5), math.log(2.0))), 0.5, 2.0),
        "energy_index": place_ends(jax.random.randint(seeds[3], (E_WIN,), 0, ENERGIES), jax.random.fold_in(seeds[3], 1), 0, ENERGIES - 1).astype(jnp.int32),
        "fan_offset": place_ends(jax.random.randint(seeds[4], (K,), 0, NZ - FAN + 1), jax.random.fold_in(seeds[4], 1), 0, NZ - FAN).astype(jnp.int32),
        "fan_weight": place_ends(jax.random.randint(seeds[5], (K, FAN), 1, 4), jax.random.fold_in(seeds[5], 1), 1, 3).astype(jnp.int32),
        "measured": jnp.clip(6.0 * jax.random.uniform(seeds[6], (E_WIN, K, NY), jnp.float32) ** level_of(seeds[6], (E_WIN, K, NY), ((2, 2),), -0.2, 0.2), 0.0, 6.0),
    }


def fan_matrix(fan_offset, fan_weight, slices):
    taps = fan_offset[:, None] + jnp.arange(fan_weight.shape[1], dtype=jnp.int32)[None, :]
    match = (taps[:, :, None] == slices[None, None, :]).astype(jnp.float32)
    return jnp.sum(fan_weight.astype(jnp.float32)[:, :, None] * match, axis=1)


def attenuate(conc_slice, sigma_sel, line_attenuation):
    emission = sigma_sel[0][:, None, None] * conc_slice[0][None]
    absorber = line_attenuation[0] * conc_slice[0]
    for species in range(1, S):
        emission = emission + sigma_sel[species][:, None, None] * conc_slice[species][None]
        absorber = absorber + line_attenuation[species] * conc_slice[species]
    path_in = jnp.cumsum(emission, axis=1) - emission
    incident = jnp.exp(-(1.5 / NX) * path_in)
    path_out = jnp.sum(absorber, axis=1, keepdims=True) - jnp.cumsum(absorber, axis=1)
    escape = jnp.exp(-(1.5 / NY) * path_out)
    return emission, incident, escape


def reference(concentration, cross_section, line_attenuation, energy_index, fan_offset, fan_weight, measured):
    hi = lax.Precision.HIGHEST
    sigma_sel = cross_section[:, energy_index]
    weights = fan_matrix(fan_offset, fan_weight, jnp.arange(NZ, dtype=jnp.int32))

    def forward(slice_index):
        conc_slice = concentration[:, slice_index]
        emission, incident, escape = attenuate(conc_slice, sigma_sel, line_attenuation)
        return jnp.sum(emission * incident * escape[None], axis=1)

    line_sums = lax.map(forward, jnp.arange(NZ, dtype=jnp.int32))
    signal = jnp.einsum("kz,zey->eky", weights, line_sums, precision=hi) / NX
    residual = signal - measured
    back = jnp.einsum("kz,eky->zey", weights, residual, precision=hi)

    def backward(slice_index):
        conc_slice = concentration[:, slice_index]
        emission, incident, escape = attenuate(conc_slice, sigma_sel, line_attenuation)
        fluor = emission * incident * escape[None]
        back_z = back[slice_index]
        heavy = back_z[:, None, :] * fluor
        after_x = jnp.sum(heavy, axis=1, keepdims=True) - jnp.cumsum(heavy, axis=1)
        summed = jnp.sum(heavy, axis=0)
        before_y = jnp.cumsum(summed, axis=1) - summed
        term = back_z[:, None, :] * incident * escape[None] - (1.5 / NX) * after_x
        result = []
        for species in range(S):
            acc = sigma_sel[species, 0] * term[0]
            for energy in range(1, E_WIN):
                acc = acc + sigma_sel[species, energy] * term[energy]
            result.append(acc - line_attenuation[species] * (1.5 / NY) * before_y)
        return jnp.stack(result)

    grads = lax.map(backward, jnp.arange(NZ, dtype=jnp.int32))
    return jnp.moveaxis(grads, 0, 1), residual
```

```python
import functools
import math

import jax
import jax.numpy as jnp
from jax import lax
from jax.experimental import pallas as pl
from jax.experimental.pallas import tpu as pltpu
from jax.sharding import PartitionSpec as P

VMEM, SMEM, HBM = pltpu.VMEM, pltpu.SMEM, pltpu.HBM
F32, BF16 = jnp.float32, jnp.bfloat16
LANES = 128
CHUNK = 32
STEP = 16
LN2 = math.log(2.0)
LOG2E = 1.0 / LN2


def call(body, name, out_shape, out_spaces, in_spaces, scratch=(), limit=8, cost=None):
    flops, exps, size = cost
    return pl.pallas_call(
        body,
        out_shape=out_shape,
        in_specs=[pl.BlockSpec(memory_space=s) for s in in_spaces],
        out_specs=[pl.BlockSpec(memory_space=s) for s in out_spaces],
        scratch_shapes=list(scratch),
        compiler_params=pltpu.CompilerParams(vmem_limit_bytes=limit << 20),
        cost_estimate=pl.CostEstimate(flops=flops, transcendentals=exps, bytes_accessed=size),
        name=name,
    )


def plain(*shape):
    return jax.ShapeDtypeStruct(shape, F32)


def split(value):
    high = value.astype(BF16)
    low = (value - high.astype(F32)).astype(BF16)
    return jnp.concatenate([high, low], axis=1)


def lane_sums(width, beyond):
    row = lax.broadcasted_iota(jnp.int32, (width, 2 * width), 0)
    col = lax.broadcasted_iota(jnp.int32, (width, 2 * width), 1)
    part = (row > col) if beyond else (row < col)
    ones = jnp.where(part | (col >= width), 1.0, 0.0).astype(BF16)
    return jnp.concatenate([ones, ones], axis=0)


def selected(cross_ref, index_ref):
    n_energy = index_ref.shape[0]
    columns = [index_ref[e] for e in range(n_energy)]
    return [[cross_ref[s, columns[e]] for e in range(n_energy)] for s in range(cross_ref.shape[0])]


def weighted(weights, values):
    total = weights[0] * values[0]
    for weight, value in zip(weights[1:], values[1:]):
        total = total + weight * value
    return total


def load_body(scale, line_hbm, conc_hbm, conc_ref, beyond_ref, total_ref, line_ref, line_sem, sems):
    n_species, depth, rows, width = conc_hbm.shape

    def copies(chunk):
        span = pl.ds(chunk * CHUNK, CHUNK)
        return [
            pltpu.make_async_copy(conc_hbm.at[:, z, span, :], conc_ref.at[:, span, z, :], sems.at[chunk])
            for z in range(depth)
        ]

    line_copy = pltpu.make_async_copy(line_hbm, line_ref, line_sem)
    line_copy.start()

    for chunk in range(rows // CHUNK):
        for copy in copies(chunk):
            copy.start()
    table = lane_sums(width, True)
    lane = lax.broadcasted_iota(jnp.int32, (depth, LANES), 1)
    line_copy.wait()
    line = [line_ref[s] * scale for s in range(n_species)]
    for part in range(rows // LANES):

        def step(piece, total):
            chunk = part * (LANES // CHUNK) + piece
            for copy in copies(chunk):
                copy.wait()
            absorber = []
            for q in range(CHUNK):
                x = chunk * CHUNK + q
                absorber.append(weighted(line, [conc_ref[s, x] for s in range(n_species)]))
            sums = jnp.dot(split(jnp.concatenate(absorber, axis=0)), table, preferred_element_type=F32)
            for q in range(CHUNK):
                here = sums[q * depth : (q + 1) * depth]
                beyond_ref[chunk * CHUNK + q] = here[:, :width]
                total = jnp.where(lane == piece * CHUNK + q, here[:, width : width + LANES], total)
            return total

        total_ref[:, part * LANES : (part + 1) * LANES] = lax.fori_loop(
            0, LANES // CHUNK, step, jnp.zeros((depth, LANES), F32)
        )


def local_body(scale, cross_ref, index_ref, conc_ref, beyond_ref, trans_ref, emit_ref, depth_ref):
    n_species, rows, depth, width = conc_ref.shape
    n_energy = trans_ref.shape[0]
    sigma = [[v * scale for v in row] for row in selected(cross_ref, index_ref)]

    def step(block, path):
        path = list(path)
        for q in range(STEP):
            x = block * STEP + q
            conc = [conc_ref[s, x] for s in range(n_species)]
            beyond = beyond_ref[x]
            for e in range(n_energy):
                emission = weighted([sigma[s][e] for s in range(n_species)], conc)
                trans = jnp.exp2(path[e] + beyond)
                trans_ref[e, x] = trans
                emit_ref[e, x] = emission * trans
                path[e] = path[e] + emission
        return tuple(path)

    zero = jnp.zeros((depth, width), F32)
    path = lax.fori_loop(0, rows // STEP, step, (zero,) * n_energy)
    for e in range(n_energy):
        depth_ref[e] = path[e]


def spread(source_ref, change, width, body, init):
    depth, rows = source_ref.shape
    carry = init
    for part in range(rows // LANES):
        held = change(source_ref[:, part * LANES : (part + 1) * LANES])

        def step(block, state):
            held, carry = state
            for q in range(STEP):
                column = jnp.broadcast_to(held[:, q : q + 1], (depth, width))
                carry = body(part * LANES + block * STEP + q, column, carry)
            return pltpu.roll(held, LANES - STEP, 1), carry

        _, carry = lax.fori_loop(0, LANES // STEP, step, (held, carry))
    return carry


def line_body(far_ref, emit_ref, far_out, line_ref):
    n_energy, rows, depth, width = emit_ref.shape

    def one(x, factor, sums):
        far_out[x] = factor
        return tuple(sums[e] + factor * emit_ref[e, x] for e in range(n_energy))

    zero = jnp.zeros((depth, width), F32)
    sums = spread(far_ref, jnp.exp2, width, one, (zero,) * n_energy)
    for e in range(n_energy):
        line_ref[e] = sums[e]


def ahead_body(far_ref, trans_ref, emit_ref, fluor_ref, rest_ref):
    n_energy, rows, depth, width = emit_ref.shape

    def step(block, ahead):
        ahead = list(ahead)
        for q in range(STEP):
            x = rows - 1 - (block * STEP + q)
            far = far_ref[x]
            for e in range(n_energy):
                fluor = far * emit_ref[e, x]
                fluor_ref[e, x] = fluor
                rest_ref[e, x] = far * trans_ref[e, x] + ahead[e]
                ahead[e] = ahead[e] + LN2 * fluor
        return tuple(ahead)

    zero = jnp.zeros((depth, width), F32)
    lax.fori_loop(0, rows // STEP, step, (zero,) * n_energy)


def fan_body(fan_ref, measured_ref, gram_ref, pull_ref):
    depth = pull_ref.shape[1]
    own = fan_ref[:depth, :]
    gram_ref[...] = lax.dot_general(
        own.astype(BF16), fan_ref[...].astype(BF16), (((1,), (1,)), ((), ())), preferred_element_type=F32
    )
    for e in range(pull_ref.shape[0]):
        pull_ref[e] = jnp.dot(
            own, measured_ref[e], precision=lax.Precision.HIGHEST, preferred_element_type=F32
        )


def back_body(
    scale, cross_ref, index_ref, gram_ref, pull_ref, lines_ref, up_ref, further_ref, fluor_ref,
    near_ref, total_ref, gain_ref, shift_ref,
):
    n_energy, rows, depth, width = fluor_ref.shape
    n_species = shift_ref.shape[0]
    sums = [None] * n_energy
    for r in range(lines_ref.shape[0]):
        for z in range(depth):
            place = r * depth + z
            weight = jnp.broadcast_to(gram_ref[:, place : place + 1], (depth, width))
            for e in range(n_energy):
                value = weight * lines_ref[r, e, z : z + 1, :]
                sums[e] = value if place == 0 else sums[e] + value
    back = [sums[e] * scale - pull_ref[e] for e in range(n_energy)]
    gain = [back[e] * jnp.exp2(up_ref[e]) for e in range(n_energy)]
    sigma = selected(cross_ref, index_ref)
    pushed = [LN2 * back[e] * further_ref[e] for e in range(n_energy)]
    for e in range(n_energy):
        gain_ref[e] = gain[e]
    for s in range(n_species):
        shift_ref[s] = weighted(sigma[s], pushed)
    table = lane_sums(width, False)
    lane = lax.broadcasted_iota(jnp.int32, (depth, LANES), 1)
    for part in range(rows // LANES):

        def step(piece, total):
            first = part * LANES + piece * CHUNK
            heavy = [weighted(gain, [fluor_ref[e, first + q] for e in range(n_energy)]) for q in range(CHUNK)]
            found = jnp.dot(split(jnp.concatenate(heavy, axis=0)), table, preferred_element_type=F32)
            for q in range(CHUNK):
                here = found[q * depth : (q + 1) * depth]
                near_ref[first + q] = here[:, :width]
                total = jnp.where(lane == piece * CHUNK + q, here[:, width : width + LANES], total)
            return total

        total_ref[:, part * LANES : (part + 1) * LANES] = lax.fori_loop(
            0, LANES // CHUNK, step, jnp.zeros((depth, LANES), F32)
        )


def grad_body(
    scale, cross_ref, index_ref, line_ref, nearer_ref, gain_ref, shift_ref, near_ref, rest_ref,
    out_hbm, out_ref, sems,
):
    n_energy, rows, depth, width = rest_ref.shape
    n_species = out_ref.shape[0]
    sigma = selected(cross_ref, index_ref)
    mixed = [[sigma[s][e] * gain_ref[e] for e in range(n_energy)] for s in range(n_species)]
    shift = [shift_ref[s] for s in range(n_species)]
    line = [line_ref[s] * scale for s in range(n_species)]

    def copies(chunk):
        span = pl.ds(chunk * CHUNK, CHUNK)
        return [
            pltpu.make_async_copy(out_ref.at[:, span, z, :], out_hbm.at[:, z, span, :], sems.at[chunk])
            for z in range(depth)
        ]

    for part in range(rows // LANES):

        def step(piece, held):
            chunk = part * (LANES // CHUNK) + piece
            for q in range(CHUNK):
                x = chunk * CHUNK + q
                column = jnp.broadcast_to(held[:, q : q + 1], (depth, width))
                before = near_ref[x] + column
                rest = [rest_ref[e, x] for e in range(n_energy)]
                for s in range(n_species):
                    out_ref[s, x] = weighted(mixed[s], rest) + shift[s] + line[s] * before
            for copy in copies(chunk):
                copy.start()
            return pltpu.roll(held, LANES - CHUNK, 1)

        lax.fori_loop(0, LANES // CHUNK, step, nearer_ref[:, part * LANES : (part + 1) * LANES])

    def finish(chunk, carry):
        for copy in copies(chunk):
            copy.wait()
        return carry

    lax.fori_loop(0, rows // CHUNK, finish, 0)


def signal_body(scale, fan_ref, lines_ref, measured_ref, out_ref):
    n_energy, share, width = out_ref.shape
    depth = lines_ref.shape[2]
    sums = [None] * n_energy
    for r in range(lines_ref.shape[0]):
        for z in range(depth):
            place = r * depth + z
            weight = jnp.broadcast_to(fan_ref[:, place : place + 1], (share, width))
            for e in range(n_energy):
                value = weight * lines_ref[r, e, z : z + 1, :]
                sums[e] = value if place == 0 else sums[e] + value
    for e in range(n_energy):
        out_ref[e] = sums[e] * scale - measured_ref[e]


def swap(value, axis, distance):
    return lax.ppermute(value, axis, [(i, i ^ distance) for i in range(lax.axis_size(axis))])


def beyond(value, axis, backward):
    count, mine = lax.axis_size(axis), lax.axis_index(axis)
    if count == 2:
        keep = (mine == 1) if backward else (mine == 0)
        return jnp.where(keep, swap(value, axis, 1), 0.0)
    pieces = lax.all_gather(value, axis)
    places = jnp.arange(count)
    keep = (places < mine) if backward else (places > mine)
    return jnp.sum(jnp.where(keep.reshape((-1,) + (1,) * value.ndim), pieces, 0.0), axis=0)


def fan_rows(fan_offset, fan_weight, slices):
    taps = fan_weight.shape[1]
    total = 0.0
    for j in range(taps):
        match = slices[:, None] == fan_offset[None, :] + j
        total = total + jnp.where(match, fan_weight[:, j].astype(F32)[None, :], 0.0)
    return total


def shards(conc, cross, line, index, fan_offset, fan_weight, measured):
    n_species, depth, rows, width = conc.shape
    n_energy = index.shape[0]
    n_beam, n_det, n_slab = (lax.axis_size(a) for a in ("beam", "det", "slab"))
    assert n_beam & (n_beam - 1) == 0 and n_slab & (n_slab - 1) == 0
    assert rows % LANES == 0 and width % LANES == 0 and depth % 8 == 0
    full_x, full_y = rows * n_beam, width * n_det
    scale_x = -(1.5 / full_x) * LOG2E
    scale_y = -(1.5 / full_y) * LOG2E
    voxels = depth * rows * width
    cube = VMEM((n_energy, rows, depth, width), F32)
    plane = VMEM((rows, depth, width), F32)

    conc_x, far_local, row_total = call(
        functools.partial(load_body, scale_y),
        "load",
        (VMEM((n_species, rows, depth, width), F32), plane, plain(depth, rows)),
        (VMEM, VMEM, VMEM),
        (HBM, HBM),
        [SMEM((n_species,), F32), pltpu.SemaphoreType.DMA, pltpu.SemaphoreType.DMA((rows // CHUNK,))],
        cost=(8 * voxels, 0, 16 * voxels),
    )(pltpu.with_memory_space_constraint(line, HBM), pltpu.with_memory_space_constraint(conc, HBM))

    far = beyond(row_total, "det", False)

    trans, emit, own_depth = call(
        functools.partial(local_body, scale_x),
        "local",
        (cube, cube, plain(n_energy, depth, width)),
        (VMEM, VMEM, VMEM),
        (SMEM, SMEM, VMEM, VMEM),
        cost=(40 * voxels, 4 * voxels, 1024),
    )(cross, index, conc_x, far_local)

    far_wide, own_line = call(
        line_body, "line", (plane, plain(n_energy, depth, width)), (VMEM, VMEM), (VMEM, VMEM),
        cost=(8 * voxels, 0, 1024),
    )(far, emit)

    beam = lax.axis_index("beam")
    span, sums = own_depth, own_line
    up, further = jnp.zeros_like(own_depth), jnp.zeros_like(own_line)
    distance = 1
    while distance < n_beam:
        other = swap(jnp.stack([span, sums]), "beam", distance)
        lower = (beam & distance) == 0
        first = jnp.where(lower, span, other[0])
        fade = jnp.exp2(first)
        late = fade * jnp.where(lower, other[1], sums)
        further = jnp.where(lower, further + late, fade * further)
        up = jnp.where(lower, up, up + first)
        sums = jnp.where(lower, sums, other[1]) + late
        span = span + other[0]
        distance *= 2

    fluor, rest = call(
        ahead_body, "ahead", (cube, cube), (VMEM, VMEM), (VMEM, VMEM, VMEM),
        cost=(20 * voxels, 0, 1024),
    )(far_wide, trans, emit)

    lines = sums[None]
    distance = 1
    while distance < n_slab:
        lines = jnp.concatenate([lines, swap(lines, "slab", distance)], axis=0)
        distance *= 2

    slab = lax.axis_index("slab")
    order = (slab ^ jnp.arange(n_slab, dtype=jnp.int32))[:, None] * depth
    slices = (order + jnp.arange(depth, dtype=jnp.int32)[None, :]).reshape(-1)
    fan_all = fan_rows(fan_offset, fan_weight, slices)
    gram, pull = call(
        fan_body, "fan", (plain(depth, depth * n_slab), plain(n_energy, depth, width)),
        (VMEM, VMEM), (VMEM, VMEM), cost=(4 * 2 * depth * measured.size // width * width, 0, 4 * measured.size),
    )(fan_all, measured)

    near, column_total, gain, shift = call(
        functools.partial(back_body, 1.0 / (scale_x * full_x)),
        "back",
        (plane, plain(depth, rows), plain(n_energy, depth, width), plain(n_species, depth, width)),
        (VMEM,) * 4,
        (SMEM, SMEM) + (VMEM,) * 6,
        cost=(10 * voxels, 0, 1024),
    )(cross, index, gram, pull, lines, up, further, fluor)

    nearer = beyond(column_total, "det", True)

    share = fan_offset.shape[0] // (n_beam * n_slab)
    start = lax.axis_index(("beam", "slab")) * share
    fan_own = fan_rows(
        lax.dynamic_slice_in_dim(fan_offset, start, share), lax.dynamic_slice_in_dim(fan_weight, start, share), slices
    ).T
    residual = call(
        functools.partial(signal_body, 1.0 / (scale_x * full_x)),
        "signal", (plain(n_energy, share, width),), (VMEM,), (VMEM, VMEM, VMEM),
        cost=(1 << 16, 0, 1024),
    )(fan_own, lines, lax.dynamic_slice_in_dim(measured, start, share, 1))[0]

    grad = call(
        functools.partial(grad_body, 1.0 / scale_x * scale_y * LN2),
        "grad",
        (plain(n_species, depth, rows, width),),
        (HBM,),
        (SMEM, SMEM, SMEM) + (VMEM,) * 5,
        [VMEM((n_species, rows, depth, width), F32), pltpu.SemaphoreType.DMA((rows // CHUNK,))],
        limit=16,
        cost=(40 * voxels, 0, 16 * voxels),
    )(cross, index, line, nearer, gain, shift, near, rest)[0]
    return grad, residual


def solution(mesh):
    in_specs = (P(None, "slab", "beam", "det"), P(), P(), P(), P(), P(), P(None, None, "det"))
    out_specs = (P(None, "slab", "beam", "det"), P(None, ("beam", "slab"), "det"))
    return jax.shard_map(shards, mesh=mesh, in_specs=in_specs, out_specs=out_specs, check_vma=False)
```

```python
import functools
import math

import jax
import jax.numpy as jnp
from jax import lax
from jax.experimental import pallas as pl
from jax.experimental.pallas import tpu as pltpu
from jax.sharding import PartitionSpec as P

VMEM, SMEM, HBM = pltpu.VMEM, pltpu.SMEM, pltpu.HBM
F32, BF16 = jnp.float32, jnp.bfloat16
LANES = 128
CHUNK = 32
STEP = 16
LN2 = math.log(2.0)
LOG2E = 1.0 / LN2


def call(body, name, out_shape, out_spaces, in_spaces, scratch=(), limit=8, cost=None):
    flops, exps, size = cost
    return pl.pallas_call(
        body,
        out_shape=out_shape,
        in_specs=[pl.BlockSpec(memory_space=s) for s in in_spaces],
        out_specs=[pl.BlockSpec(memory_space=s) for s in out_spaces],
        scratch_shapes=list(scratch),
        compiler_params=pltpu.CompilerParams(vmem_limit_bytes=limit << 20),
        cost_estimate=pl.CostEstimate(flops=flops, transcendentals=exps, bytes_accessed=size),
        name=name,
    )


def plain(*shape):
    return jax.ShapeDtypeStruct(shape, F32)


def split(value):
    high = value.astype(BF16)
    low = (value - high.astype(F32)).astype(BF16)
    return jnp.concatenate([high, low], axis=1)


def lane_sums(width, beyond):
    row = lax.broadcasted_iota(jnp.int32, (width, 2 * width), 0)
    col = lax.broadcasted_iota(jnp.int32, (width, 2 * width), 1)
    part = (row > col) if beyond else (row < col)
    ones = jnp.where(part | (col >= width), 1.0, 0.0).astype(BF16)
    return jnp.concatenate([ones, ones], axis=0)


def selected(cross_ref, index_ref):
    n_energy = index_ref.shape[0]
    columns = [index_ref[e] for e in range(n_energy)]
    return [[cross_ref[s, columns[e]] for e in range(n_energy)] for s in range(cross_ref.shape[0])]


def weighted(weights, values):
    total = weights[0] * values[0]
    for weight, value in zip(weights[1:], values[1:]):
        total = total + weight * value
    return total


def load_body(scale, line_hbm, conc_hbm, conc_ref, beyond_ref, total_ref, line_ref, line_sem, sems):
    n_species, depth, rows, width = conc_hbm.shape

    def copies(chunk):
        span = pl.ds(chunk * CHUNK, CHUNK)
        return [
            pltpu.make_async_copy(conc_hbm.at[:, z, span, :], conc_ref.at[:, span, z, :], sems.at[chunk])
            for z in range(depth)
        ]

    line_copy = pltpu.make_async_copy(line_hbm, line_ref, line_sem)
    line_copy.start()

    for chunk in range(rows // CHUNK):
        for copy in copies(chunk):
            copy.start()
    table = lane_sums(width, True)
    lane = lax.broadcasted_iota(jnp.int32, (depth, LANES), 1)
    line_copy.wait()
    line = [line_ref[s] * scale for s in range(n_species)]
    for part in range(rows // LANES):

        def step(piece, total):
            chunk = part * (LANES // CHUNK) + piece
            for copy in copies(chunk):
                copy.wait()
            absorber = []
            for q in range(CHUNK):
                x = chunk * CHUNK + q
                absorber.append(weighted(line, [conc_ref[s, x] for s in range(n_species)]))
            sums = jnp.dot(split(jnp.concatenate(absorber, axis=0)), table, preferred_element_type=F32)
            for q in range(CHUNK):
                here = sums[q * depth : (q + 1) * depth]
                beyond_ref[chunk * CHUNK + q] = here[:, :width]
                total = jnp.where(lane == piece * CHUNK + q, here[:, width : width + LANES], total)
            return total

        total_ref[:, part * LANES : (part + 1) * LANES] = lax.fori_loop(
            0, LANES // CHUNK, step, jnp.zeros((depth, LANES), F32)
        )


def local_body(scale, cross_ref, index_ref, conc_ref, beyond_ref, trans_ref, emit_ref, depth_ref):
    n_species, rows, depth, width = conc_ref.shape
    n_energy = trans_ref.shape[0]
    sigma = [[v * scale for v in row] for row in selected(cross_ref, index_ref)]

    def step(block, path):
        path = list(path)
        for q in range(STEP):
            x = block * STEP + q
            conc = [conc_ref[s, x] for s in range(n_species)]
            beyond = beyond_ref[x]
            for e in range(n_energy):
                emission = weighted([sigma[s][e] for s in range(n_species)], conc)
                trans = jnp.exp2(path[e] + beyond)
                trans_ref[e, x] = trans
                emit_ref[e, x] = emission * trans
                path[e] = path[e] + emission
        return tuple(path)

    zero = jnp.zeros((depth, width), F32)
    path = lax.fori_loop(0, rows // STEP, step, (zero,) * n_energy)
    for e in range(n_energy):
        depth_ref[e] = path[e]


def reached(axis, count, backward):
    if count != 2:
        return True
    return lax.axis_index(axis) == (1 if backward else 0)


def spread(source_ref, change, width, body, init):
    depth, rows = source_ref.shape
    carry = init
    for part in range(rows // LANES):
        held = change(source_ref[:, part * LANES : (part + 1) * LANES])

        def step(block, state):
            held, carry = state
            for q in range(STEP):
                column = jnp.broadcast_to(held[:, q : q + 1], (depth, width))
                carry = body(part * LANES + block * STEP + q, column, carry)
            return pltpu.roll(held, LANES - STEP, 1), carry

        _, carry = lax.fori_loop(0, LANES // STEP, step, (held, carry))
    return carry


def line_body(count, far_ref, emit_ref, depth_ref, far_out, pair_ref):
    n_energy, rows, depth, width = emit_ref.shape
    keep = jnp.where(reached("det", count, False), 1.0, 0.0)

    def one(x, factor, sums):
        far_out[x] = factor
        return tuple(sums[e] + factor * emit_ref[e, x] for e in range(n_energy))

    zero = jnp.zeros((depth, width), F32)
    sums = spread(far_ref, lambda v: jnp.exp2(v * keep), width, one, (zero,) * n_energy)
    for e in range(n_energy):
        pair_ref[0, e] = depth_ref[e]
        pair_ref[1, e] = sums[e]


def merge_body(distance, first_round, own_ref, other_ref, up_ref, further_ref, out_ref, up_out, further_out):
    lower = (lax.axis_index("beam") & distance) == 0
    span, sums = own_ref[0], own_ref[1]
    first = jnp.where(lower, span, other_ref[0])
    fade = jnp.exp2(first)
    late = fade * jnp.where(lower, other_ref[1], sums)
    zero = jnp.zeros_like(late)
    if first_round:
        further_out[...] = jnp.where(lower, late, zero)
        up_out[...] = jnp.where(lower, zero, first)
    else:
        further_out[...] = jnp.where(lower, further_ref[...] + late, fade * further_ref[...])
        up_out[...] = up_ref[...] + jnp.where(lower, zero, first)
    total = jnp.where(lower, sums, other_ref[1]) + late
    if out_ref.shape[0] == 2:
        out_ref[0] = span + other_ref[0]
        out_ref[1] = total
    else:
        out_ref[0] = total


def ahead_body(far_ref, trans_ref, emit_ref, fluor_ref, rest_ref):
    n_energy, rows, depth, width = emit_ref.shape

    def step(block, ahead):
        ahead = list(ahead)
        for q in range(STEP):
            x = rows - 1 - (block * STEP + q)
            far = far_ref[x]
            for e in range(n_energy):
                fluor = far * emit_ref[e, x]
                fluor_ref[e, x] = fluor
                rest_ref[e, x] = far * trans_ref[e, x] + ahead[e]
                ahead[e] = ahead[e] + LN2 * fluor
        return tuple(ahead)

    zero = jnp.zeros((depth, width), F32)
    lax.fori_loop(0, rows // STEP, step, (zero,) * n_energy)


def fan_body(offset_ref, weight_ref, measured_ref, gram_ref, pull_ref, turned_ref):
    depth, n_slices = gram_ref.shape
    taps, pixels = weight_ref.shape
    slab = lax.axis_index("slab")
    offset = jnp.broadcast_to(offset_ref[...], (depth, pixels))
    level = lax.broadcasted_iota(jnp.int32, (depth, pixels), 0)
    blocks = []
    for r in range(n_slices // depth):
        place = level + (slab ^ r) * depth - offset
        block = jnp.zeros((depth, pixels), F32)
        for j in range(taps):
            tap = jnp.broadcast_to(weight_ref[j : j + 1, :], (depth, pixels)).astype(F32)
            block = block + jnp.where(place == j, tap, 0.0)
        blocks.append(block)
    every = jnp.concatenate(blocks, axis=0)
    turned_ref[...] = every.T
    gram_ref[...] = lax.dot_general(
        blocks[0].astype(BF16), every.astype(BF16), (((1,), (1,)), ((), ())), preferred_element_type=F32
    )
    for e in range(pull_ref.shape[0]):
        pull_ref[e] = jnp.dot(
            blocks[0], measured_ref[e], precision=lax.Precision.HIGHEST, preferred_element_type=F32
        )


def slices_of(refs):
    return [(ref, i) for ref in refs for i in range(ref.shape[0])]


def back_body(scale, cross_ref, index_ref, gram_ref, pull_ref, up_ref, further_ref, fluor_ref, *refs):
    lines, (near_ref, total_ref, gain_ref, shift_ref) = slices_of(refs[:-4]), refs[-4:]
    n_energy, rows, depth, width = fluor_ref.shape
    n_species = shift_ref.shape[0]
    sums = [None] * n_energy
    for r, (lines_ref, i) in enumerate(lines):
        for z in range(depth):
            place = r * depth + z
            weight = jnp.broadcast_to(gram_ref[:, place : place + 1], (depth, width))
            for e in range(n_energy):
                value = weight * lines_ref[i, e, z : z + 1, :]
                sums[e] = value if place == 0 else sums[e] + value
    back = [sums[e] * scale - pull_ref[e] for e in range(n_energy)]
    gain = [back[e] * jnp.exp2(up_ref[e]) for e in range(n_energy)]
    sigma = selected(cross_ref, index_ref)
    pushed = [LN2 * back[e] * further_ref[e] for e in range(n_energy)]
    for e in range(n_energy):
        gain_ref[e] = gain[e]
    for s in range(n_species):
        shift_ref[s] = weighted(sigma[s], pushed)
    table = lane_sums(width, False)
    lane = lax.broadcasted_iota(jnp.int32, (depth, LANES), 1)
    for part in range(rows // LANES):

        def step(piece, total):
            first = part * LANES + piece * CHUNK
            heavy = [weighted(gain, [fluor_ref[e, first + q] for e in range(n_energy)]) for q in range(CHUNK)]
            found = jnp.dot(split(jnp.concatenate(heavy, axis=0)), table, preferred_element_type=F32)
            for q in range(CHUNK):
                here = found[q * depth : (q + 1) * depth]
                near_ref[first + q] = here[:, :width]
                total = jnp.where(lane == piece * CHUNK + q, here[:, width : width + LANES], total)
            return total

        total_ref[:, part * LANES : (part + 1) * LANES] = lax.fori_loop(
            0, LANES // CHUNK, step, jnp.zeros((depth, LANES), F32)
        )


def grad_body(
    scale, count, cross_ref, index_ref, line_ref, nearer_ref, gain_ref, shift_ref, near_ref, rest_ref,
    out_hbm, out_ref, sems,
):
    n_energy, rows, depth, width = rest_ref.shape
    n_species = out_ref.shape[0]
    sigma = selected(cross_ref, index_ref)
    mixed = [[sigma[s][e] * gain_ref[e] for e in range(n_energy)] for s in range(n_species)]
    shift = [shift_ref[s] for s in range(n_species)]
    line = [line_ref[s] * scale for s in range(n_species)]
    keep = jnp.where(reached("det", count, True), 1.0, 0.0)

    def copies(chunk):
        span = pl.ds(chunk * CHUNK, CHUNK)
        return [
            pltpu.make_async_copy(out_ref.at[:, span, z, :], out_hbm.at[:, z, span, :], sems.at[chunk])
            for z in range(depth)
        ]

    for part in range(rows // LANES):

        def step(piece, held):
            chunk = part * (LANES // CHUNK) + piece
            for q in range(CHUNK):
                x = chunk * CHUNK + q
                column = jnp.broadcast_to(held[:, q : q + 1], (depth, width))
                before = near_ref[x] + column
                rest = [rest_ref[e, x] for e in range(n_energy)]
                for s in range(n_species):
                    out_ref[s, x] = weighted(mixed[s], rest) + shift[s] + line[s] * before
            for copy in copies(chunk):
                copy.start()
            return pltpu.roll(held, LANES - CHUNK, 1)

        lax.fori_loop(0, LANES // CHUNK, step, nearer_ref[:, part * LANES : (part + 1) * LANES] * keep)

    def finish(chunk, carry):
        for copy in copies(chunk):
            copy.wait()
        return carry

    lax.fori_loop(0, rows // CHUNK, finish, 0)


def signal_body(scale, fan_ref, measured_ref, *refs):
    lines, out_ref = slices_of(refs[:-1]), refs[-1]
    n_energy, share, width = out_ref.shape
    depth = fan_ref.shape[1] // len(lines)
    start = pl.multiple_of(lax.axis_index(("beam", "slab")) * share, share)
    fan = fan_ref[pl.ds(start, share), :]
    sums = [None] * n_energy
    for r, (lines_ref, i) in enumerate(lines):
        for z in range(depth):
            place = r * depth + z
            weight = jnp.broadcast_to(fan[:, place : place + 1], (share, width))
            for e in range(n_energy):
                value = weight * lines_ref[i, e, z : z + 1, :]
                sums[e] = value if place == 0 else sums[e] + value
    for e in range(n_energy):
        out_ref[e] = sums[e] * scale - measured_ref[e, pl.ds(start, share), :]


def swap(value, axis, distance):
    return lax.ppermute(value, axis, [(i, i ^ distance) for i in range(lax.axis_size(axis))])


def beyond(value, axis, backward):
    count = lax.axis_size(axis)
    if count == 2:
        return swap(value, axis, 1)
    mine = lax.axis_index(axis)
    pieces = lax.all_gather(value, axis)
    places = jnp.arange(count)
    keep = (places < mine) if backward else (places > mine)
    return jnp.sum(jnp.where(keep.reshape((-1,) + (1,) * value.ndim), pieces, 0.0), axis=0)


def shards(conc, cross, line, index, fan_offset, fan_weight, measured):
    n_species, depth, rows, width = conc.shape
    n_energy = index.shape[0]
    n_beam, n_det, n_slab = (lax.axis_size(a) for a in ("beam", "det", "slab"))
    assert n_beam & (n_beam - 1) == 0 and n_slab & (n_slab - 1) == 0
    assert rows % LANES == 0 and width % LANES == 0 and depth % 8 == 0
    full_x, full_y = rows * n_beam, width * n_det
    scale_x = -(1.5 / full_x) * LOG2E
    scale_y = -(1.5 / full_y) * LOG2E
    voxels = depth * rows * width
    cube = VMEM((n_energy, rows, depth, width), F32)
    plane = VMEM((rows, depth, width), F32)

    conc_x, far_local, row_total = call(
        functools.partial(load_body, scale_y),
        "load",
        (VMEM((n_species, rows, depth, width), F32), plane, plain(depth, rows)),
        (VMEM, VMEM, VMEM),
        (HBM, HBM),
        [SMEM((n_species,), F32), pltpu.SemaphoreType.DMA, pltpu.SemaphoreType.DMA((rows // CHUNK,))],
        cost=(8 * voxels, 0, 16 * voxels),
    )(pltpu.with_memory_space_constraint(line, HBM), pltpu.with_memory_space_constraint(conc, HBM))

    far = beyond(row_total, "det", False)

    trans, emit, own_depth = call(
        functools.partial(local_body, scale_x),
        "local",
        (cube, cube, plain(n_energy, depth, width)),
        (VMEM, VMEM, VMEM),
        (SMEM, SMEM, VMEM, VMEM),
        cost=(40 * voxels, 4 * voxels, 1024),
    )(cross, index, conc_x, far_local)

    wide = (n_energy, depth, width)
    far_wide, pair = call(
        functools.partial(line_body, n_det), "line", (plane, plain(2, *wide)), (VMEM,) * 2, (VMEM,) * 3,
        cost=(8 * voxels, 0, 1024),
    )(far, emit, own_depth)

    up = further = own_depth
    distance = 1
    while distance < n_beam:
        other = swap(pair, "beam", distance)
        kept = 1 if 2 * distance == n_beam else 2
        pair, up, further = call(
            functools.partial(merge_body, distance, distance == 1),
            "merge", (plain(kept, *wide), plain(*wide), plain(*wide)), (VMEM,) * 3, (VMEM,) * 4,
            cost=(1 << 14, 1 << 12, 1024),
        )(pair, other, up, further)
        distance *= 2

    fluor, rest = call(
        ahead_body, "ahead", (cube, cube), (VMEM, VMEM), (VMEM, VMEM, VMEM),
        cost=(20 * voxels, 0, 1024),
    )(far_wide, trans, emit)

    lines = [pair]
    distance = 1
    while distance < n_slab:
        whole = lines[0] if distance == 1 else jnp.concatenate(lines, axis=0)
        lines.append(swap(whole, "slab", distance))
        distance *= 2

    pixels = fan_offset.shape[0]
    gram, pull, fan_turned = call(
        fan_body, "fan", (plain(depth, depth * n_slab), plain(*wide), plain(pixels, depth * n_slab)),
        (VMEM,) * 3, (VMEM,) * 3, cost=(8 * depth * measured.size, 0, 4 * measured.size),
    )(fan_offset[None, :], fan_weight.T, measured)

    near, column_total, gain, shift = call(
        functools.partial(back_body, 1.0 / (scale_x * full_x)),
        "back",
        (plane, plain(depth, rows), plain(*wide), plain(n_species, depth, width)),
        (VMEM,) * 4,
        (SMEM, SMEM) + (VMEM,) * (5 + len(lines)),
        cost=(10 * voxels, 0, 1024),
    )(cross, index, gram, pull, up, further, fluor, *lines)

    nearer = beyond(column_total, "det", True)

    residual = call(
        functools.partial(signal_body, 1.0 / (scale_x * full_x)),
        "signal", (plain(n_energy, pixels // (n_beam * n_slab), width),), (VMEM,), (VMEM,) * (2 + len(lines)),
        cost=(1 << 16, 0, 1024),
    )(fan_turned, measured, *lines)[0]

    grad = call(
        functools.partial(grad_body, scale_y * LN2 / scale_x, n_det),
        "grad",
        (plain(n_species, depth, rows, width),),
        (HBM,),
        (SMEM, SMEM, SMEM) + (VMEM,) * 5,
        [VMEM((n_species, rows, depth, width), F32), pltpu.SemaphoreType.DMA((rows // CHUNK,))],
        limit=16,
        cost=(40 * voxels, 0, 16 * voxels),
    )(cross, index, line, nearer, gain, shift, near, rest)[0]
    return grad, residual


def solution(mesh):
    in_specs = (P(None, "slab", "beam", "det"), P(), P(), P(), P(), P(), P(None, None, "det"))
    out_specs = (P(None, "slab", "beam", "det"), P(None, ("beam", "slab"), "det"))
    return jax.shard_map(shards, mesh=mesh, in_specs=in_specs, out_specs=out_specs, check_vma=False)
```

```python
import functools
import math

import jax
import jax.numpy as jnp
from jax import lax
from jax.experimental import pallas as pl
from jax.experimental.pallas import tpu as pltpu
from jax.sharding import PartitionSpec as P

VMEM, SMEM, HBM = pltpu.VMEM, pltpu.SMEM, pltpu.HBM
F32, BF16 = jnp.float32, jnp.bfloat16
LANES = 128
CHUNK = 32
STEP = 16
LN2 = math.log(2.0)
LOG2E = 1.0 / LN2


def call(body, name, out_shape, out_spaces, in_spaces, scratch=(), limit=8, cost=None):
    flops, exps, size = cost
    return pl.pallas_call(
        body,
        out_shape=out_shape,
        in_specs=[pl.BlockSpec(memory_space=s) for s in in_spaces],
        out_specs=[pl.BlockSpec(memory_space=s) for s in out_spaces],
        scratch_shapes=list(scratch),
        compiler_params=pltpu.CompilerParams(vmem_limit_bytes=limit << 20),
        cost_estimate=pl.CostEstimate(flops=flops, transcendentals=exps, bytes_accessed=size),
        name=name,
    )


def plain(*shape):
    return jax.ShapeDtypeStruct(shape, F32)


def split(value):
    high = value.astype(BF16)
    low = (value - high.astype(F32)).astype(BF16)
    return jnp.concatenate([high, low], axis=1)


def lane_sums(width, beyond):
    row = lax.broadcasted_iota(jnp.int32, (width, 2 * width), 0)
    col = lax.broadcasted_iota(jnp.int32, (width, 2 * width), 1)
    part = (row > col) if beyond else (row < col)
    ones = jnp.where(part | (col >= width), 1.0, 0.0).astype(BF16)
    return jnp.concatenate([ones, ones], axis=0)


def selected(cross_ref, index_ref):
    n_energy = index_ref.shape[0]
    columns = [index_ref[e] for e in range(n_energy)]
    return [[cross_ref[s, columns[e]] for e in range(n_energy)] for s in range(cross_ref.shape[0])]


def weighted(weights, values):
    total = weights[0] * values[0]
    for weight, value in zip(weights[1:], values[1:]):
        total = total + weight * value
    return total


def load_body(scale, line_hbm, conc_hbm, conc_ref, beyond_ref, total_ref, line_ref, line_sem, sems):
    n_species, depth, rows, width = conc_hbm.shape

    def copies(chunk):
        span = pl.ds(chunk * CHUNK, CHUNK)
        return [
            pltpu.make_async_copy(conc_hbm.at[:, z, span, :], conc_ref.at[:, span, z, :], sems.at[chunk])
            for z in range(depth)
        ]

    line_copy = pltpu.make_async_copy(line_hbm, line_ref, line_sem)
    line_copy.start()

    for chunk in range(rows // CHUNK):
        for copy in copies(chunk):
            copy.start()
    table = lane_sums(width, True)
    lane = lax.broadcasted_iota(jnp.int32, (depth, LANES), 1)
    line_copy.wait()
    line = [line_ref[s] * scale for s in range(n_species)]
    for part in range(rows // LANES):

        def step(piece, total):
            chunk = part * (LANES // CHUNK) + piece
            for copy in copies(chunk):
                copy.wait()
            absorber = []
            for q in range(CHUNK):
                x = chunk * CHUNK + q
                absorber.append(weighted(line, [conc_ref[s, x] for s in range(n_species)]))
            sums = jnp.dot(split(jnp.concatenate(absorber, axis=0)), table, preferred_element_type=F32)
            for q in range(CHUNK):
                here = sums[q * depth : (q + 1) * depth]
                beyond_ref[chunk * CHUNK + q] = here[:, :width]
                total = jnp.where(lane == piece * CHUNK + q, here[:, width : width + LANES], total)
            return total

        total_ref[:, part * LANES : (part + 1) * LANES] = lax.fori_loop(
            0, LANES // CHUNK, step, jnp.zeros((depth, LANES), F32)
        )


def local_body(scale, cross_ref, index_ref, conc_ref, beyond_ref, trans_ref, emit_ref, depth_ref):
    n_species, rows, depth, width = conc_ref.shape
    n_energy = trans_ref.shape[0]
    sigma = [[v * scale for v in row] for row in selected(cross_ref, index_ref)]

    def step(block, path):
        path = list(path)
        for q in range(STEP):
            x = block * STEP + q
            conc = [conc_ref[s, x] for s in range(n_species)]
            beyond = beyond_ref[x]
            for e in range(n_energy):
                emission = weighted([sigma[s][e] for s in range(n_species)], conc)
                trans = jnp.exp2(path[e] + beyond)
                trans_ref[e, x] = trans
                emit_ref[e, x] = emission * trans
                path[e] = path[e] + emission
        return tuple(path)

    zero = jnp.zeros((depth, width), F32)
    path = lax.fori_loop(0, rows // STEP, step, (zero,) * n_energy)
    for e in range(n_energy):
        depth_ref[e] = path[e]


def reached(axis, count, backward):
    if count != 2:
        return True
    return lax.axis_index(axis) == (1 if backward else 0)


def columns(source_ref, change, width):
    depth, rows = source_ref.shape
    for part in range(rows // LANES):
        held = change(source_ref[:, part * LANES : (part + 1) * LANES])
        for q in range(LANES):
            yield part * LANES + q, jnp.broadcast_to(held[:, q : q + 1], (depth, width))


def line_body(count, far_ref, emit_ref, depth_ref, far_out, pair_ref):
    n_energy, rows, depth, width = emit_ref.shape
    keep = jnp.where(reached("det", count, False), 1.0, 0.0)
    sums = [[None, None] for _ in range(n_energy)]
    for x, factor in columns(far_ref, lambda v: jnp.exp2(v * keep), width):
        far_out[x] = factor
        for e in range(n_energy):
            value = factor * emit_ref[e, x]
            sums[e][x % 2] = value if x < 2 else sums[e][x % 2] + value
    for e in range(n_energy):
        pair_ref[0, e] = depth_ref[e]
        pair_ref[1, e] = sums[e][0] + sums[e][1]


def merge_body(distance, first_round, own_ref, other_ref, up_ref, further_ref, out_ref, up_out, further_out):
    lower = (lax.axis_index("beam") & distance) == 0
    span, sums = own_ref[0], own_ref[1]
    first = jnp.where(lower, span, other_ref[0])
    fade = jnp.exp2(first)
    late = fade * jnp.where(lower, other_ref[1], sums)
    zero = jnp.zeros_like(late)
    if first_round:
        further_out[...] = jnp.where(lower, late, zero)
        up_out[...] = jnp.where(lower, zero, first)
    else:
        further_out[...] = jnp.where(lower, further_ref[...] + late, fade * further_ref[...])
        up_out[...] = up_ref[...] + jnp.where(lower, zero, first)
    total = jnp.where(lower, sums, other_ref[1]) + late
    if out_ref.shape[0] == 2:
        out_ref[0] = span + other_ref[0]
        out_ref[1] = total
    else:
        out_ref[0] = total


def ahead_body(far_ref, trans_ref, emit_ref, fluor_ref, rest_ref):
    n_energy, rows, depth, width = emit_ref.shape

    def step(block, ahead):
        ahead = list(ahead)
        for q in range(STEP):
            x = rows - 1 - (block * STEP + q)
            far = far_ref[x]
            for e in range(n_energy):
                fluor = far * emit_ref[e, x]
                fluor_ref[e, x] = fluor
                rest_ref[e, x] = far * trans_ref[e, x] + ahead[e]
                ahead[e] = ahead[e] + LN2 * fluor
        return tuple(ahead)

    zero = jnp.zeros((depth, width), F32)
    lax.fori_loop(0, rows // STEP, step, (zero,) * n_energy)


def fan_body(offset_ref, weight_ref, measured_ref, gram_ref, pull_ref, turned_ref):
    depth, n_slices = gram_ref.shape
    taps, pixels = weight_ref.shape
    slab = lax.axis_index("slab")
    offset = jnp.broadcast_to(offset_ref[...], (depth, pixels))
    level = lax.broadcasted_iota(jnp.int32, (depth, pixels), 0)
    blocks = []
    for r in range(n_slices // depth):
        place = level + (slab ^ r) * depth - offset
        block = jnp.zeros((depth, pixels), F32)
        for j in range(taps):
            tap = jnp.broadcast_to(weight_ref[j : j + 1, :], (depth, pixels)).astype(F32)
            block = block + jnp.where(place == j, tap, 0.0)
        blocks.append(block)
    every = jnp.concatenate(blocks, axis=0)
    turned_ref[...] = every.T
    gram_ref[...] = lax.dot_general(
        blocks[0].astype(BF16), every.astype(BF16), (((1,), (1,)), ((), ())), preferred_element_type=F32
    )
    for e in range(pull_ref.shape[0]):
        pull_ref[e] = jnp.dot(
            blocks[0], measured_ref[e], precision=lax.Precision.HIGHEST, preferred_element_type=F32
        )


def slices_of(refs):
    return [(ref, i) for ref in refs for i in range(ref.shape[0])]


def weigh(weights, lines, depth, n_energy, width):
    height = weights.shape[0]
    sums = [[None, None] for _ in range(n_energy)]
    for r, (lines_ref, i) in enumerate(lines):
        for z in range(depth):
            place = r * depth + z
            weight = jnp.broadcast_to(weights[:, place : place + 1], (height, width))
            for e in range(n_energy):
                value = weight * lines_ref[i, e, z : z + 1, :]
                sums[e][z % 2] = value if place < 2 else sums[e][z % 2] + value
    return [a + b for a, b in sums]


def back_body(scale, cross_ref, index_ref, gram_ref, pull_ref, up_ref, further_ref, fluor_ref, *refs):
    lines, (near_ref, total_ref, gain_ref, shift_ref) = slices_of(refs[:-4]), refs[-4:]
    n_energy, rows, depth, width = fluor_ref.shape
    n_species = shift_ref.shape[0]
    sums = weigh(gram_ref[...], lines, depth, n_energy, width)
    back = [sums[e] * scale - pull_ref[e] for e in range(n_energy)]
    gain = [back[e] * jnp.exp2(up_ref[e]) for e in range(n_energy)]
    sigma = selected(cross_ref, index_ref)
    pushed = [LN2 * back[e] * further_ref[e] for e in range(n_energy)]
    for e in range(n_energy):
        gain_ref[e] = gain[e]
    for s in range(n_species):
        shift_ref[s] = weighted(sigma[s], pushed)
    table = lane_sums(width, False)
    lane = lax.broadcasted_iota(jnp.int32, (depth, LANES), 1)
    for part in range(rows // LANES):
        total = jnp.zeros((depth, LANES), F32)
        for piece in range(LANES // CHUNK):
            first = part * LANES + piece * CHUNK
            heavy = [weighted(gain, [fluor_ref[e, first + q] for e in range(n_energy)]) for q in range(CHUNK)]
            found = jnp.dot(split(jnp.concatenate(heavy, axis=0)), table, preferred_element_type=F32)
            for q in range(CHUNK):
                here = found[q * depth : (q + 1) * depth]
                near_ref[first + q] = here[:, :width]
                total = jnp.where(lane == piece * CHUNK + q, here[:, width : width + LANES], total)
        total_ref[:, part * LANES : (part + 1) * LANES] = total


def mix_body(scale, cross_ref, index_ref, line_ref, gain_ref, shift_ref, near_ref, rest_ref, out_ref):
    n_energy, rows, depth, width = rest_ref.shape
    n_species = out_ref.shape[0]
    sigma = selected(cross_ref, index_ref)
    line = [line_ref[s] * scale for s in range(n_species)]

    def step(block, carry):
        for s in range(n_species):
            mixed = [sigma[s][e] * gain_ref[e] for e in range(n_energy)]
            shift = shift_ref[s]
            for q in range(STEP):
                x = block * STEP + q
                rest = weighted(mixed, [rest_ref[e, x] for e in range(n_energy)])
                out_ref[s, x] = rest + (shift + line[s] * near_ref[x])
        return carry

    lax.fori_loop(0, rows // STEP, step, 0)


def finish_body(
    scale, scale_line, count, line_ref, nearer_ref, mix_ref, fan_ref, measured_ref, *refs
):
    lines, (grad_hbm, residual_hbm, grad_ref, residual_ref, sems, residual_sem) = slices_of(refs[:-6]), refs[-6:]
    n_species, rows, depth, width = mix_ref.shape
    n_energy, share, _ = residual_ref.shape
    line = [line_ref[s] * scale_line for s in range(n_species)]
    keep = jnp.where(reached("det", count, True), 1.0, 0.0)

    def copies(chunk):
        span = pl.ds(chunk * CHUNK, CHUNK)
        return [
            pltpu.make_async_copy(grad_ref.at[:, span, z, :], grad_hbm.at[:, z, span, :], sems.at[chunk])
            for z in range(depth)
        ]

    for x, column in columns(nearer_ref, lambda v: v * keep, width):
        for s in range(n_species):
            grad_ref[s, x] = mix_ref[s, x] + line[s] * column
        if x % CHUNK == CHUNK - 1:
            for copy in copies(x // CHUNK):
                copy.start()

    start = pl.multiple_of(lax.axis_index(("beam", "slab")) * share, share)
    sums = weigh(fan_ref[pl.ds(start, share), :], lines, depth, n_energy, width)
    for e in range(n_energy):
        residual_ref[e] = sums[e] * scale - measured_ref[e, pl.ds(start, share), :]
    copy = pltpu.make_async_copy(residual_ref, residual_hbm, residual_sem)
    copy.start()

    def finish(chunk, carry):
        for done in copies(chunk):
            done.wait()
        return carry

    lax.fori_loop(0, rows // CHUNK, finish, 0)
    copy.wait()


def swap(value, axis, distance):
    return lax.ppermute(value, axis, [(i, i ^ distance) for i in range(lax.axis_size(axis))])


def beyond(value, axis, backward):
    count = lax.axis_size(axis)
    if count == 2:
        return swap(value, axis, 1)
    mine = lax.axis_index(axis)
    pieces = lax.all_gather(value, axis)
    places = jnp.arange(count)
    keep = (places < mine) if backward else (places > mine)
    return jnp.sum(jnp.where(keep.reshape((-1,) + (1,) * value.ndim), pieces, 0.0), axis=0)


def shards(conc, cross, line, index, fan_offset, fan_weight, measured):
    n_species, depth, rows, width = conc.shape
    n_energy = index.shape[0]
    n_beam, n_det, n_slab = (lax.axis_size(a) for a in ("beam", "det", "slab"))
    assert n_beam & (n_beam - 1) == 0 and n_slab & (n_slab - 1) == 0
    assert rows % LANES == 0 and width % LANES == 0 and depth % 8 == 0
    full_x, full_y = rows * n_beam, width * n_det
    scale_x = -(1.5 / full_x) * LOG2E
    scale_y = -(1.5 / full_y) * LOG2E
    voxels = depth * rows * width
    cube = VMEM((n_energy, rows, depth, width), F32)
    plane = VMEM((rows, depth, width), F32)

    conc_x, far_local, row_total = call(
        functools.partial(load_body, scale_y),
        "load",
        (VMEM((n_species, rows, depth, width), F32), plane, plain(depth, rows)),
        (VMEM, VMEM, VMEM),
        (HBM, HBM),
        [SMEM((n_species,), F32), pltpu.SemaphoreType.DMA, pltpu.SemaphoreType.DMA((rows // CHUNK,))],
        cost=(8 * voxels, 0, 16 * voxels),
    )(pltpu.with_memory_space_constraint(line, HBM), pltpu.with_memory_space_constraint(conc, HBM))

    far = beyond(row_total, "det", False)

    trans, emit, own_depth = call(
        functools.partial(local_body, scale_x),
        "local",
        (cube, cube, plain(n_energy, depth, width)),
        (VMEM, VMEM, VMEM),
        (SMEM, SMEM, VMEM, VMEM),
        cost=(40 * voxels, 4 * voxels, 1024),
    )(cross, index, conc_x, far_local)

    wide = (n_energy, depth, width)
    far_wide, pair = call(
        functools.partial(line_body, n_det), "line", (plane, plain(2, *wide)), (VMEM,) * 2, (VMEM,) * 3,
        cost=(8 * voxels, 0, 1024),
    )(far, emit, own_depth)

    fluor, rest = call(
        ahead_body, "ahead", (cube, cube), (VMEM, VMEM), (VMEM, VMEM, VMEM),
        cost=(20 * voxels, 0, 1024),
    )(far_wide, trans, emit)

    up = further = own_depth
    distance = 1
    while distance < n_beam:
        other = swap(pair, "beam", distance)
        kept = 1 if 2 * distance == n_beam else 2
        if kept == 1:
            other, fluor, rest = lax.optimization_barrier((other, fluor, rest))
        pair, up, further = call(
            functools.partial(merge_body, distance, distance == 1),
            "merge", (plain(kept, *wide), plain(*wide), plain(*wide)), (VMEM,) * 3, (VMEM,) * 4,
            cost=(1 << 14, 1 << 12, 1024),
        )(pair, other, up, further)
        distance *= 2

    lines = [pair]
    distance = 1
    while distance < n_slab:
        whole = lines[0] if distance == 1 else jnp.concatenate(lines, axis=0)
        lines.append(swap(whole, "slab", distance))
        distance *= 2

    pixels = fan_offset.shape[0]
    gram, pull, fan_turned = call(
        fan_body, "fan", (plain(depth, depth * n_slab), plain(*wide), plain(pixels, depth * n_slab)),
        (VMEM,) * 3, (VMEM,) * 3, cost=(8 * depth * measured.size, 0, 4 * measured.size),
    )(fan_offset[None, :], fan_weight.T, measured)

    near, column_total, gain, shift = call(
        functools.partial(back_body, 1.0 / (scale_x * full_x)),
        "back",
        (plane, plain(depth, rows), plain(*wide), plain(n_species, depth, width)),
        (VMEM,) * 4,
        (SMEM, SMEM) + (VMEM,) * (5 + len(lines)),
        cost=(10 * voxels, 0, 1024),
    )(cross, index, gram, pull, up, further, fluor, *lines)

    nearer = beyond(column_total, "det", True)

    scale_line = scale_y * LN2 / scale_x
    mixed = call(
        functools.partial(mix_body, scale_line), "mix", (VMEM(conc_x.shape, F32),), (VMEM,), (SMEM,) * 3 + (VMEM,) * 4,
        cost=(40 * voxels, 0, 1024),
    )(cross, index, line, gain, shift, near, rest)[0]

    share = pixels // (n_beam * n_slab)
    return tuple(
        call(
            functools.partial(finish_body, 1.0 / (scale_x * full_x), scale_line, n_det),
            "finish",
            (plain(*conc.shape), plain(n_energy, share, width)),
            (HBM, HBM),
            (SMEM,) + (VMEM,) * (4 + len(lines)),
            [
                VMEM(conc_x.shape, F32),
                VMEM((n_energy, share, width), F32),
                pltpu.SemaphoreType.DMA((rows // CHUNK,)),
                pltpu.SemaphoreType.DMA,
            ],
            limit=16,
            cost=(10 * voxels, 0, 16 * voxels),
        )(line, nearer, mixed, fan_turned, measured, *lines)
    )


def solution(mesh):
    in_specs = (P(None, "slab", "beam", "det"), P(), P(), P(), P(), P(), P(None, None, "det"))
    out_specs = (P(None, "slab", "beam", "det"), P(None, ("beam", "slab"), "det"))
    return jax.shard_map(shards, mesh=mesh, in_specs=in_specs, out_specs=out_specs, check_vma=False)
```

```python
import functools
import math

import jax
import jax.numpy as jnp
from jax import lax
from jax.experimental import pallas as pl
from jax.experimental.pallas import tpu as pltpu
from jax.sharding import PartitionSpec as P

VMEM, SMEM, HBM = pltpu.VMEM, pltpu.SMEM, pltpu.HBM
F32, BF16 = jnp.float32, jnp.bfloat16
LANES = 128
CHUNK = 32
STEP = 16
LN2 = math.log(2.0)
LOG2E = 1.0 / LN2


def call(body, name, out_shape, out_spaces, in_spaces, scratch=(), limit=8, cost=None):
    flops, exps, size = cost
    return pl.pallas_call(
        body,
        out_shape=out_shape,
        in_specs=[pl.BlockSpec(memory_space=s) for s in in_spaces],
        out_specs=[pl.BlockSpec(memory_space=s) for s in out_spaces],
        scratch_shapes=list(scratch),
        compiler_params=pltpu.CompilerParams(vmem_limit_bytes=limit << 20),
        cost_estimate=pl.CostEstimate(flops=flops, transcendentals=exps, bytes_accessed=size),
        name=name,
    )


def plain(*shape):
    return jax.ShapeDtypeStruct(shape, F32)


def split(value):
    high = value.astype(BF16)
    low = (value - high.astype(F32)).astype(BF16)
    return jnp.concatenate([high, low], axis=1)


def lane_sums(width, beyond):
    row = lax.broadcasted_iota(jnp.int32, (width, 2 * width), 0)
    col = lax.broadcasted_iota(jnp.int32, (width, 2 * width), 1)
    part = (row > col) if beyond else (row < col)
    ones = jnp.where(part | (col >= width), 1.0, 0.0).astype(BF16)
    return jnp.concatenate([ones, ones], axis=0)


def selected(cross_ref, index_ref):
    n_energy = index_ref.shape[0]
    columns = [index_ref[e] for e in range(n_energy)]
    return [[cross_ref[s, columns[e]] for e in range(n_energy)] for s in range(cross_ref.shape[0])]


def weighted(weights, values):
    total = weights[0] * values[0]
    for weight, value in zip(weights[1:], values[1:]):
        total = total + weight * value
    return total


def load_body(
    scale, scale_x, line_hbm, cross_hbm, index_hbm, conc_hbm, emit_ref, beyond_ref, total_ref,
    conc_ref, line_ref, cross_ref, index_ref, small_sems, sems,
):
    n_species, depth, rows, width = conc_hbm.shape
    n_energy = emit_ref.shape[0]

    def copies(chunk):
        span = pl.ds(chunk * CHUNK, CHUNK)
        return [
            pltpu.make_async_copy(conc_hbm.at[:, z, span, :], conc_ref.at[:, span, z, :], sems.at[chunk])
            for z in range(depth)
        ]

    small = [
        pltpu.make_async_copy(source, target, small_sems.at[i])
        for i, (source, target) in enumerate(
            [(line_hbm, line_ref), (cross_hbm, cross_ref), (index_hbm, index_ref)]
        )
    ]
    for copy in small:
        copy.start()
    for chunk in range(rows // CHUNK):
        for copy in copies(chunk):
            copy.start()
    table = lane_sums(width, True)
    lane = lax.broadcasted_iota(jnp.int32, (depth, LANES), 1)
    for copy in small:
        copy.wait()
    line = [line_ref[s] * scale for s in range(n_species)]
    sigma = [[v * scale_x for v in row] for row in selected(cross_ref, index_ref)]
    for part in range(rows // LANES):
        total = jnp.zeros((depth, LANES), F32)
        for piece in range(LANES // CHUNK):
            chunk = part * (LANES // CHUNK) + piece
            for copy in copies(chunk):
                copy.wait()
            absorber = []
            for q in range(CHUNK):
                x = chunk * CHUNK + q
                conc = [conc_ref[s, x] for s in range(n_species)]
                absorber.append(weighted(line, conc))
                for e in range(n_energy):
                    emit_ref[e, x] = weighted([sigma[s][e] for s in range(n_species)], conc)
            sums = jnp.dot(split(jnp.concatenate(absorber, axis=0)), table, preferred_element_type=F32)
            for q in range(CHUNK):
                here = sums[q * depth : (q + 1) * depth]
                beyond_ref[chunk * CHUNK + q] = here[:, :width]
                total = jnp.where(lane == piece * CHUNK + q, here[:, width : width + LANES], total)
        total_ref[:, part * LANES : (part + 1) * LANES] = total


def local_body(source_ref, beyond_ref, trans_ref, emit_ref, depth_ref):
    n_energy, rows, depth, width = trans_ref.shape

    def step(block, path):
        path = list(path)
        for q in range(STEP):
            x = block * STEP + q
            beyond = beyond_ref[x]
            for e in range(n_energy):
                emission = source_ref[e, x]
                trans = jnp.exp2(path[e] + beyond)
                trans_ref[e, x] = trans
                emit_ref[e, x] = emission * trans
                path[e] = path[e] + emission
        return tuple(path)

    zero = jnp.zeros((depth, width), F32)
    path = lax.fori_loop(0, rows // STEP, step, (zero,) * n_energy)
    for e in range(n_energy):
        depth_ref[e] = path[e]


def reached(axis, count, backward):
    if count != 2:
        return True
    return lax.axis_index(axis) == (1 if backward else 0)


def columns(source_ref, change, width):
    depth, rows = source_ref.shape
    for part in range(rows // LANES):
        held = change(source_ref[:, part * LANES : (part + 1) * LANES])
        for q in range(LANES):
            yield part * LANES + q, jnp.broadcast_to(held[:, q : q + 1], (depth, width))


def line_body(count, far_ref, emit_ref, depth_ref, far_out, pair_ref):
    n_energy, rows, depth, width = emit_ref.shape
    keep = jnp.where(reached("det", count, False), 1.0, 0.0)
    sums = [[None, None] for _ in range(n_energy)]
    for x, factor in columns(far_ref, lambda v: jnp.exp2(v * keep), width):
        far_out[x] = factor
        for e in range(n_energy):
            value = factor * emit_ref[e, x]
            sums[e][x % 2] = value if x < 2 else sums[e][x % 2] + value
    for e in range(n_energy):
        pair_ref[0, e] = depth_ref[e]
        pair_ref[1, e] = sums[e][0] + sums[e][1]


def merge_body(distance, first_round, own_ref, other_ref, up_ref, further_ref, out_ref, up_out, further_out):
    lower = (lax.axis_index("beam") & distance) == 0
    span, sums = own_ref[0], own_ref[1]
    first = jnp.where(lower, span, other_ref[0])
    fade = jnp.exp2(first)
    late = fade * jnp.where(lower, other_ref[1], sums)
    zero = jnp.zeros_like(late)
    if first_round:
        further_out[...] = jnp.where(lower, late, zero)
        up_out[...] = jnp.where(lower, zero, first)
    else:
        further_out[...] = jnp.where(lower, further_ref[...] + late, fade * further_ref[...])
        up_out[...] = up_ref[...] + jnp.where(lower, zero, first)
    total = jnp.where(lower, sums, other_ref[1]) + late
    if out_ref.shape[0] == 2:
        out_ref[0] = span + other_ref[0]
        out_ref[1] = total
    else:
        out_ref[0] = total


def ahead_body(far_ref, trans_ref, emit_ref, fluor_ref, rest_ref):
    n_energy, rows, depth, width = emit_ref.shape

    def step(block, ahead):
        ahead = list(ahead)
        for q in range(STEP):
            x = rows - 1 - (block * STEP + q)
            far = far_ref[x]
            for e in range(n_energy):
                fluor = far * emit_ref[e, x]
                fluor_ref[e, x] = fluor
                rest_ref[e, x] = far * trans_ref[e, x] + ahead[e]
                ahead[e] = ahead[e] + LN2 * fluor
        return tuple(ahead)

    zero = jnp.zeros((depth, width), F32)
    lax.fori_loop(0, rows // STEP, step, (zero,) * n_energy)


def fan_body(offset_ref, weight_ref, measured_ref, gram_ref, pull_ref, turned_ref):
    depth, n_slices = gram_ref.shape
    taps, pixels = weight_ref.shape
    slab = lax.axis_index("slab")
    offset = jnp.broadcast_to(offset_ref[...], (depth, pixels))
    level = lax.broadcasted_iota(jnp.int32, (depth, pixels), 0)
    blocks = []
    for r in range(n_slices // depth):
        place = level + (slab ^ r) * depth - offset
        block = jnp.zeros((depth, pixels), F32)
        for j in range(taps):
            tap = jnp.broadcast_to(weight_ref[j : j + 1, :], (depth, pixels)).astype(F32)
            block = block + jnp.where(place == j, tap, 0.0)
        blocks.append(block)
    every = jnp.concatenate(blocks, axis=0)
    turned_ref[...] = every.T
    gram_ref[...] = lax.dot_general(
        blocks[0].astype(BF16), every.astype(BF16), (((1,), (1,)), ((), ())), preferred_element_type=F32
    )
    for e in range(pull_ref.shape[0]):
        pull_ref[e] = jnp.dot(
            blocks[0], measured_ref[e], precision=lax.Precision.HIGHEST, preferred_element_type=F32
        )


def weigh(weights, lines, depth, n_energy, width):
    height = weights.shape[0]
    sums = [[None, None] for _ in range(n_energy)]
    for order, (r, lines_ref) in enumerate(lines):
        for z in range(depth):
            place = r * depth + z
            weight = jnp.broadcast_to(weights[:, place : place + 1], (height, width))
            for e in range(n_energy):
                value = weight * lines_ref[0, e, z : z + 1, :]
                sums[e][z % 2] = value if order == 0 and z < 2 else sums[e][z % 2] + value
    return [a + b for a, b in sums]


def back_body(scale, close, cross_ref, index_ref, gram_ref, pull_ref, up_ref, further_ref, fluor_ref, *refs):
    lines, (near_ref, total_ref, gain_ref, shift_ref) = refs[:-4], refs[-4:]
    n_energy, rows, depth, width = fluor_ref.shape
    n_species = shift_ref.shape[0]
    sums = weigh(gram_ref[...], list(zip(close, lines)), depth, n_energy, width)
    back = [sums[e] * scale - pull_ref[e] for e in range(n_energy)]
    gain = [back[e] * jnp.exp2(up_ref[e]) for e in range(n_energy)]
    sigma = selected(cross_ref, index_ref)
    pushed = [LN2 * back[e] * further_ref[e] for e in range(n_energy)]
    for e in range(n_energy):
        gain_ref[e] = gain[e]
    for s in range(n_species):
        shift_ref[s] = weighted(sigma[s], pushed)
    table = lane_sums(width, False)
    lane = lax.broadcasted_iota(jnp.int32, (depth, LANES), 1)
    for part in range(rows // LANES):
        total = jnp.zeros((depth, LANES), F32)
        for piece in range(LANES // CHUNK):
            first = part * LANES + piece * CHUNK
            heavy = [weighted(gain, [fluor_ref[e, first + q] for e in range(n_energy)]) for q in range(CHUNK)]
            found = jnp.dot(split(jnp.concatenate(heavy, axis=0)), table, preferred_element_type=F32)
            for q in range(CHUNK):
                here = found[q * depth : (q + 1) * depth]
                near_ref[first + q] = here[:, :width]
                total = jnp.where(lane == piece * CHUNK + q, here[:, width : width + LANES], total)
        total_ref[:, part * LANES : (part + 1) * LANES] = total


def mix_body(cross_ref, index_ref, gain_ref, shift_ref, rest_ref, out_ref):
    n_energy, rows, depth, width = rest_ref.shape
    n_species = out_ref.shape[0]
    sigma = selected(cross_ref, index_ref)
    mixed = [[sigma[s][e] * gain_ref[e] for e in range(n_energy)] for s in range(n_species)]
    shift = [shift_ref[s] for s in range(n_species)]

    def step(block, carry):
        for q in range(STEP):
            x = block * STEP + q
            rest = [rest_ref[e, x] for e in range(n_energy)]
            for s in range(n_species):
                out_ref[s, x] = weighted(mixed[s], rest) + shift[s]
        return carry

    lax.fori_loop(0, rows // STEP, step, 0)


def finish_body(
    scale, scale_line, count, line_ref, nearer_ref, near_ref, mix_ref, fan_ref, measured_ref, *refs
):
    lines, (grad_hbm, residual_hbm, grad_ref, residual_ref, sems, residual_sem) = refs[:-6], refs[-6:]
    n_species, rows, depth, width = mix_ref.shape
    n_energy, share, _ = residual_ref.shape
    line = [line_ref[s] * scale_line for s in range(n_species)]
    keep = jnp.where(reached("det", count, True), 1.0, 0.0)

    def copies(chunk):
        span = pl.ds(chunk * CHUNK, CHUNK)
        return [
            pltpu.make_async_copy(grad_ref.at[:, span, z, :], grad_hbm.at[:, z, span, :], sems.at[chunk])
            for z in range(depth)
        ]

    for x, column in columns(nearer_ref, lambda v: v * keep, width):
        before = near_ref[x] + column
        for s in range(n_species):
            grad_ref[s, x] = mix_ref[s, x] + line[s] * before
        if x % CHUNK == CHUNK - 1:
            for copy in copies(x // CHUNK):
                copy.start()

    start = pl.multiple_of(lax.axis_index(("beam", "slab")) * share, share)
    sums = weigh(fan_ref[pl.ds(start, share), :], list(enumerate(lines)), depth, n_energy, width)
    for e in range(n_energy):
        residual_ref[e] = sums[e] * scale - measured_ref[e, pl.ds(start, share), :]
    copy = pltpu.make_async_copy(residual_ref, residual_hbm, residual_sem)
    copy.start()

    def finish(chunk, carry):
        for done in copies(chunk):
            done.wait()
        return carry

    lax.fori_loop(0, rows // CHUNK, finish, 0)
    copy.wait()


def swap(value, axis, distance):
    return lax.ppermute(value, axis, [(i, i ^ distance) for i in range(lax.axis_size(axis))])


def beyond(value, axis, backward):
    count = lax.axis_size(axis)
    if count == 2:
        return swap(value, axis, 1)
    mine = lax.axis_index(axis)
    pieces = lax.all_gather(value, axis)
    places = jnp.arange(count)
    keep = (places < mine) if backward else (places > mine)
    return jnp.sum(jnp.where(keep.reshape((-1,) + (1,) * value.ndim), pieces, 0.0), axis=0)


def shards(conc, cross, line, index, fan_offset, fan_weight, measured):
    n_species, depth, rows, width = conc.shape
    n_energy = index.shape[0]
    n_beam, n_det, n_slab = (lax.axis_size(a) for a in ("beam", "det", "slab"))
    assert n_beam & (n_beam - 1) == 0 and n_slab & (n_slab - 1) == 0
    assert fan_weight.shape[1] <= depth + 1
    assert rows % LANES == 0 and width % LANES == 0 and depth % 8 == 0
    full_x, full_y = rows * n_beam, width * n_det
    scale_x = -(1.5 / full_x) * LOG2E
    scale_y = -(1.5 / full_y) * LOG2E
    voxels = depth * rows * width
    cube = VMEM((n_energy, rows, depth, width), F32)
    plane = VMEM((rows, depth, width), F32)

    emission, far_local, row_total = call(
        functools.partial(load_body, scale_y, scale_x),
        "load",
        (cube, plane, plain(depth, rows)),
        (VMEM, VMEM, VMEM),
        (HBM,) * 4,
        [
            VMEM((n_species, rows, depth, width), F32),
            SMEM(line.shape, F32),
            SMEM(cross.shape, F32),
            SMEM(index.shape, index.dtype),
            pltpu.SemaphoreType.DMA((3,)),
            pltpu.SemaphoreType.DMA((rows // CHUNK,)),
        ],
        cost=(40 * voxels, 0, 16 * voxels),
    )(*(pltpu.with_memory_space_constraint(v, HBM) for v in (line, cross, index, conc)))

    far = beyond(row_total, "det", False)

    trans, emit, own_depth = call(
        local_body,
        "local",
        (cube, cube, plain(n_energy, depth, width)),
        (VMEM, VMEM, VMEM),
        (VMEM, VMEM),
        cost=(20 * voxels, 4 * voxels, 1024),
    )(emission, far_local)

    wide = (n_energy, depth, width)
    far_wide, pair = call(
        functools.partial(line_body, n_det), "line", (plane, plain(2, *wide)), (VMEM,) * 2, (VMEM,) * 3,
        cost=(8 * voxels, 0, 1024),
    )(far, emit, own_depth)

    fluor, rest = call(
        ahead_body, "ahead", (cube, cube), (VMEM, VMEM), (VMEM, VMEM, VMEM),
        cost=(20 * voxels, 0, 1024),
    )(far_wide, trans, emit)

    up = further = own_depth
    distance = 1
    while distance < n_beam:
        other = swap(pair, "beam", distance)
        kept = 1 if 2 * distance == n_beam else 2
        if kept == 1:
            other, fluor, rest = lax.optimization_barrier((other, fluor, rest))
        pair, up, further = call(
            functools.partial(merge_body, distance, distance == 1),
            "merge", (plain(kept, *wide), plain(*wide), plain(*wide)), (VMEM,) * 3, (VMEM,) * 4,
            cost=(1 << 14, 1 << 12, 1024),
        )(pair, other, up, further)
        distance *= 2

    lines = [pair] + [swap(pair, "slab", r) for r in range(1, n_slab)]
    close = [r for r in range(n_slab) if r & (r + 1) == 0]

    pixels = fan_offset.shape[0]
    gram, pull, fan_turned = call(
        fan_body, "fan", (plain(depth, depth * n_slab), plain(*wide), plain(pixels, depth * n_slab)),
        (VMEM,) * 3, (VMEM,) * 3, cost=(8 * depth * measured.size, 0, 4 * measured.size),
    )(fan_offset[None, :], fan_weight.T, measured)

    near, column_total, gain, shift = call(
        functools.partial(back_body, 1.0 / (scale_x * full_x), close),
        "back",
        (plane, plain(depth, rows), plain(*wide), plain(n_species, depth, width)),
        (VMEM,) * 4,
        (SMEM, SMEM) + (VMEM,) * (5 + len(close)),
        cost=(10 * voxels, 0, 1024),
    )(cross, index, gram, pull, up, further, fluor, *(lines[r] for r in close))

    nearer = beyond(column_total, "det", True)

    scale_line = scale_y * LN2 / scale_x
    turned = (n_species, rows, depth, width)
    mixed = call(
        mix_body, "mix", (VMEM(turned, F32),), (VMEM,), (SMEM,) * 2 + (VMEM,) * 3,
        cost=(40 * voxels, 0, 1024),
    )(cross, index, gain, shift, rest)[0]

    share = pixels // (n_beam * n_slab)
    return tuple(
        call(
            functools.partial(finish_body, 1.0 / (scale_x * full_x), scale_line, n_det),
            "finish",
            (plain(*conc.shape), plain(n_energy, share, width)),
            (HBM, HBM),
            (SMEM,) + (VMEM,) * (5 + len(lines)),
            [
                VMEM(turned, F32),
                VMEM((n_energy, share, width), F32),
                pltpu.SemaphoreType.DMA((rows // CHUNK,)),
                pltpu.SemaphoreType.DMA,
            ],
            limit=16,
            cost=(10 * voxels, 0, 16 * voxels),
        )(line, nearer, near, mixed, fan_turned, measured, *lines)
    )


def solution(mesh):
    in_specs = (P(None, "slab", "beam", "det"), P(), P(), P(), P(), P(), P(None, None, "det"))
    out_specs = (P(None, "slab", "beam", "det"), P(None, ("beam", "slab"), "det"))
    return jax.shard_map(shards, mesh=mesh, in_specs=in_specs, out_specs=out_specs, check_vma=False)
```

```python
import functools
import math

import jax
import jax.numpy as jnp
from jax import lax
from jax.experimental import pallas as pl
from jax.experimental.pallas import tpu as pltpu
from jax.sharding import PartitionSpec as P

VMEM, SMEM, HBM = pltpu.VMEM, pltpu.SMEM, pltpu.HBM
F32, BF16 = jnp.float32, jnp.bfloat16
LANES = 128
CHUNK = 32
STEP = 16
LN2 = math.log(2.0)
LOG2E = 1.0 / LN2


def call(body, name, out_shape, out_spaces, in_spaces, scratch=(), limit=8, cost=None):
    flops, exps, size = cost
    return pl.pallas_call(
        body,
        out_shape=out_shape,
        in_specs=[pl.BlockSpec(memory_space=s) for s in in_spaces],
        out_specs=[pl.BlockSpec(memory_space=s) for s in out_spaces],
        scratch_shapes=list(scratch),
        compiler_params=pltpu.CompilerParams(vmem_limit_bytes=limit << 20),
        cost_estimate=pl.CostEstimate(flops=flops, transcendentals=exps, bytes_accessed=size),
        name=name,
    )


def plain(*shape):
    return jax.ShapeDtypeStruct(shape, F32)


def split(value):
    high = value.astype(BF16)
    low = (value - high.astype(F32)).astype(BF16)
    return jnp.concatenate([high, low], axis=1)


def lane_sums(width, beyond):
    row = lax.broadcasted_iota(jnp.int32, (width, 2 * width), 0)
    col = lax.broadcasted_iota(jnp.int32, (width, 2 * width), 1)
    part = (row > col) if beyond else (row < col)
    ones = jnp.where(part | (col >= width), 1.0, 0.0).astype(BF16)
    return jnp.concatenate([ones, ones], axis=0)


def selected(cross_ref, index_ref):
    n_energy = index_ref.shape[0]
    columns = [index_ref[e] for e in range(n_energy)]
    return [[cross_ref[s, columns[e]] for e in range(n_energy)] for s in range(cross_ref.shape[0])]


def weighted(weights, values):
    total = weights[0] * values[0]
    for weight, value in zip(weights[1:], values[1:]):
        total = total + weight * value
    return total


def load_body(
    scale, scale_x, line_hbm, cross_hbm, index_hbm, conc_hbm, conc_ref, emit_ref, beyond_ref, total_ref,
    line_ref, cross_ref, index_ref, small_sems, sems,
):
    n_species, depth, rows, width = conc_hbm.shape
    n_early = emit_ref.shape[0]

    def copies(chunk):
        span = pl.ds(chunk * CHUNK, CHUNK)
        return [
            pltpu.make_async_copy(conc_hbm.at[:, z, span, :], conc_ref.at[:, span, z, :], sems.at[chunk])
            for z in range(depth)
        ]

    small = [
        pltpu.make_async_copy(source, target, small_sems.at[i])
        for i, (source, target) in enumerate(
            [(line_hbm, line_ref), (cross_hbm, cross_ref), (index_hbm, index_ref)]
        )
    ]
    for copy in small:
        copy.start()
    for chunk in range(rows // CHUNK):
        for copy in copies(chunk):
            copy.start()
    table = lane_sums(width, True)
    lane = lax.broadcasted_iota(jnp.int32, (depth, LANES), 1)
    for copy in small:
        copy.wait()
    line = [line_ref[s] * scale for s in range(n_species)]
    sigma = [[v * scale_x for v in row] for row in selected(cross_ref, index_ref)]
    for part in range(rows // LANES):
        total = jnp.zeros((depth, LANES), F32)
        for piece in range(LANES // CHUNK):
            chunk = part * (LANES // CHUNK) + piece
            for copy in copies(chunk):
                copy.wait()
            absorber = []
            for q in range(CHUNK):
                x = chunk * CHUNK + q
                conc = [conc_ref[s, x] for s in range(n_species)]
                absorber.append(weighted(line, conc))
                for e in range(n_early):
                    emit_ref[e, x] = weighted([sigma[s][e] for s in range(n_species)], conc)
            sums = jnp.dot(split(jnp.concatenate(absorber, axis=0)), table, preferred_element_type=F32)
            for q in range(CHUNK):
                here = sums[q * depth : (q + 1) * depth]
                beyond_ref[chunk * CHUNK + q] = here[:, :width]
                total = jnp.where(lane == piece * CHUNK + q, here[:, width : width + LANES], total)
        total_ref[:, part * LANES : (part + 1) * LANES] = total


def local_body(scale, cross_ref, index_ref, conc_ref, early_ref, beyond_ref, trans_ref, emit_ref, depth_ref):
    n_energy, rows, depth, width = trans_ref.shape
    n_species, n_early = conc_ref.shape[0], early_ref.shape[0]
    sigma = [[v * scale for v in row] for row in selected(cross_ref, index_ref)]

    def step(block, path):
        path = list(path)
        for q in range(STEP):
            x = block * STEP + q
            beyond = beyond_ref[x]
            conc = [conc_ref[s, x] for s in range(n_species)]
            for e in range(n_energy):
                if e < n_early:
                    emission = early_ref[e, x]
                else:
                    emission = weighted([sigma[s][e] for s in range(n_species)], conc)
                trans = jnp.exp2(path[e] + beyond)
                trans_ref[e, x] = trans
                emit_ref[e, x] = emission * trans
                path[e] = path[e] + emission
        return tuple(path)

    zero = jnp.zeros((depth, width), F32)
    path = lax.fori_loop(0, rows // STEP, step, (zero,) * n_energy)
    for e in range(n_energy):
        depth_ref[e] = path[e]


def reached(axis, count, backward):
    if count != 2:
        return True
    return lax.axis_index(axis) == (1 if backward else 0)


def columns(source_ref, change, width):
    depth, rows = source_ref.shape
    for part in range(rows // LANES):
        held = change(source_ref[:, part * LANES : (part + 1) * LANES])
        for q in range(LANES):
            yield part * LANES + q, jnp.broadcast_to(held[:, q : q + 1], (depth, width))


def line_body(count, far_ref, emit_ref, depth_ref, far_out, pair_ref):
    n_energy, rows, depth, width = emit_ref.shape
    keep = jnp.where(reached("det", count, False), 1.0, 0.0)
    sums = [[None, None] for _ in range(n_energy)]
    for x, factor in columns(far_ref, lambda v: jnp.exp2(v * keep), width):
        far_out[x] = factor
        for e in range(n_energy):
            value = factor * emit_ref[e, x]
            sums[e][x % 2] = value if x < 2 else sums[e][x % 2] + value
    for e in range(n_energy):
        pair_ref[0, e] = depth_ref[e]
        pair_ref[1, e] = sums[e][0] + sums[e][1]


def merge_body(distance, first_round, own_ref, other_ref, up_ref, further_ref, out_ref, up_out, further_out):
    lower = (lax.axis_index("beam") & distance) == 0
    span, sums = own_ref[0], own_ref[1]
    first = jnp.where(lower, span, other_ref[0])
    fade = jnp.exp2(first)
    late = fade * jnp.where(lower, other_ref[1], sums)
    zero = jnp.zeros_like(late)
    if first_round:
        further_out[...] = jnp.where(lower, late, zero)
        up_out[...] = jnp.where(lower, zero, first)
    else:
        further_out[...] = jnp.where(lower, further_ref[...] + late, fade * further_ref[...])
        up_out[...] = up_ref[...] + jnp.where(lower, zero, first)
    total = jnp.where(lower, sums, other_ref[1]) + late
    if out_ref.shape[0] == 2:
        out_ref[0] = span + other_ref[0]
        out_ref[1] = total
    else:
        out_ref[0] = total


def ahead_body(far_ref, trans_ref, emit_ref, fluor_ref, rest_ref):
    n_energy, rows, depth, width = emit_ref.shape

    def step(block, ahead):
        ahead = list(ahead)
        for q in range(STEP):
            x = rows - 1 - (block * STEP + q)
            far = far_ref[x]
            for e in range(n_energy):
                fluor = far * emit_ref[e, x]
                fluor_ref[e, x] = fluor
                rest_ref[e, x] = far * trans_ref[e, x] + ahead[e]
                ahead[e] = ahead[e] + LN2 * fluor
        return tuple(ahead)

    zero = jnp.zeros((depth, width), F32)
    lax.fori_loop(0, rows // STEP, step, (zero,) * n_energy)


def fan_body(scale, offset_ref, weight_ref, measured_ref, own_ref, gram_ref, pull_ref, turned_ref):
    depth, n_slices = gram_ref.shape
    taps, pixels = weight_ref.shape
    slab = lax.axis_index("slab")
    offset = jnp.broadcast_to(offset_ref[...], (depth, pixels))
    level = lax.broadcasted_iota(jnp.int32, (depth, pixels), 0)
    blocks = []
    for r in range(n_slices // depth):
        place = level + (slab ^ r) * depth - offset
        block = jnp.zeros((depth, pixels), F32)
        for j in range(taps):
            tap = jnp.broadcast_to(weight_ref[j : j + 1, :], (depth, pixels)).astype(F32)
            block = block + jnp.where(place == j, tap, 0.0)
        blocks.append(block)
    every = jnp.concatenate(blocks, axis=0)
    turned_ref[...] = every.T
    gram = lax.dot_general(
        blocks[0].astype(BF16), every.astype(BF16), (((1,), (1,)), ((), ())), preferred_element_type=F32
    )
    gram_ref[...] = gram
    n_energy, _, width = pull_ref.shape
    sums = weigh(gram, [(0, own_ref)], depth, n_energy, width)
    for e in range(n_energy):
        pull_ref[e] = sums[e] * scale - jnp.dot(
            blocks[0], measured_ref[e], precision=lax.Precision.HIGHEST, preferred_element_type=F32
        )


def weigh(weights, lines, depth, n_energy, width):
    height = weights.shape[0]
    sums = [[None, None] for _ in range(n_energy)]
    for order, (r, lines_ref) in enumerate(lines):
        for z in range(depth):
            place = r * depth + z
            weight = jnp.broadcast_to(weights[:, place : place + 1], (height, width))
            for e in range(n_energy):
                value = weight * lines_ref[0, e, z : z + 1, :]
                sums[e][z % 2] = value if order == 0 and z < 2 else sums[e][z % 2] + value
    return [a + b for a, b in sums]


def back_body(scale, close, cross_ref, index_ref, gram_ref, pull_ref, up_ref, further_ref, fluor_ref, *refs):
    lines, (near_ref, total_ref, gain_ref, shift_ref) = refs[:-4], refs[-4:]
    n_energy, rows, depth, width = fluor_ref.shape
    n_species = shift_ref.shape[0]
    sums = weigh(gram_ref[...], list(zip(close, lines)), depth, n_energy, width)
    back = [sums[e] * scale + pull_ref[e] for e in range(n_energy)]
    gain = [back[e] * jnp.exp2(up_ref[e]) for e in range(n_energy)]
    sigma = selected(cross_ref, index_ref)
    pushed = [LN2 * back[e] * further_ref[e] for e in range(n_energy)]
    for e in range(n_energy):
        gain_ref[e] = gain[e]
    for s in range(n_species):
        shift_ref[s] = weighted(sigma[s], pushed)
    table = lane_sums(width, False)
    lane = lax.broadcasted_iota(jnp.int32, (depth, LANES), 1)
    for part in range(rows // LANES):
        total = jnp.zeros((depth, LANES), F32)
        for piece in range(LANES // CHUNK):
            first = part * LANES + piece * CHUNK
            heavy = [weighted(gain, [fluor_ref[e, first + q] for e in range(n_energy)]) for q in range(CHUNK)]
            found = jnp.dot(split(jnp.concatenate(heavy, axis=0)), table, preferred_element_type=F32)
            for q in range(CHUNK):
                here = found[q * depth : (q + 1) * depth]
                near_ref[first + q] = here[:, :width]
                total = jnp.where(lane == piece * CHUNK + q, here[:, width : width + LANES], total)
        total_ref[:, part * LANES : (part + 1) * LANES] = total


def mix_body(cross_ref, index_ref, gain_ref, shift_ref, rest_ref, out_ref):
    n_energy, rows, depth, width = rest_ref.shape
    n_species = out_ref.shape[0]
    sigma = selected(cross_ref, index_ref)
    mixed = [[sigma[s][e] * gain_ref[e] for e in range(n_energy)] for s in range(n_species)]
    shift = [shift_ref[s] for s in range(n_species)]

    def step(block, carry):
        for q in range(STEP):
            x = block * STEP + q
            rest = [rest_ref[e, x] for e in range(n_energy)]
            for s in range(n_species):
                out_ref[s, x] = weighted(mixed[s], rest) + shift[s]
        return carry

    lax.fori_loop(0, rows // STEP, step, 0)


def finish_body(
    scale, scale_line, count, line_ref, nearer_ref, near_ref, mix_ref, fan_ref, measured_ref, *refs
):
    lines, (grad_hbm, residual_hbm, grad_ref, residual_ref, sems, residual_sem) = refs[:-6], refs[-6:]
    n_species, rows, depth, width = mix_ref.shape
    n_energy, share, _ = residual_ref.shape
    line = [line_ref[s] * scale_line for s in range(n_species)]
    keep = jnp.where(reached("det", count, True), 1.0, 0.0)

    ends = [8, 16] + list(range(CHUNK, rows + 1, CHUNK))

    def copies(chunk):
        first = ends[chunk - 1] if chunk else 0
        span = pl.ds(first, ends[chunk] - first)
        return [
            pltpu.make_async_copy(grad_ref.at[:, span, z, :], grad_hbm.at[:, z, span, :], sems.at[chunk])
            for z in range(depth)
        ]

    for x, column in columns(nearer_ref, lambda v: v * keep, width):
        before = near_ref[x] + column
        for s in range(n_species):
            grad_ref[s, x] = mix_ref[s, x] + line[s] * before
        if x + 1 in ends:
            for copy in copies(ends.index(x + 1)):
                copy.start()

    start = pl.multiple_of(lax.axis_index(("beam", "slab")) * share, share)
    sums = weigh(fan_ref[pl.ds(start, share), :], list(enumerate(lines)), depth, n_energy, width)
    for e in range(n_energy):
        residual_ref[e] = sums[e] * scale - measured_ref[e, pl.ds(start, share), :]
    copy = pltpu.make_async_copy(residual_ref, residual_hbm, residual_sem)
    copy.start()

    for chunk in range(len(ends)):
        for done in copies(chunk):
            done.wait()
    copy.wait()


def swap(value, axis, distance):
    return lax.ppermute(value, axis, [(i, i ^ distance) for i in range(lax.axis_size(axis))])


def beyond(value, axis, backward):
    count = lax.axis_size(axis)
    if count == 2:
        return swap(value, axis, 1)
    mine = lax.axis_index(axis)
    pieces = lax.all_gather(value, axis)
    places = jnp.arange(count)
    keep = (places < mine) if backward else (places > mine)
    return jnp.sum(jnp.where(keep.reshape((-1,) + (1,) * value.ndim), pieces, 0.0), axis=0)


def shards(conc, cross, line, index, fan_offset, fan_weight, measured):
    n_species, depth, rows, width = conc.shape
    n_energy = index.shape[0]
    n_beam, n_det, n_slab = (lax.axis_size(a) for a in ("beam", "det", "slab"))
    assert n_beam & (n_beam - 1) == 0 and n_slab & (n_slab - 1) == 0
    assert fan_weight.shape[1] <= depth + 1
    assert rows % LANES == 0 and width % LANES == 0 and depth % 8 == 0
    full_x, full_y = rows * n_beam, width * n_det
    scale_x = -(1.5 / full_x) * LOG2E
    scale_y = -(1.5 / full_y) * LOG2E
    scale_sum = 1.0 / (scale_x * full_x)
    voxels = depth * rows * width
    turned = (n_species, rows, depth, width)
    cube = VMEM((n_energy, rows, depth, width), F32)
    plane = VMEM((rows, depth, width), F32)

    n_early = n_energy // 2
    conc_x, emission, far_local, row_total = call(
        functools.partial(load_body, scale_y, scale_x),
        "load",
        (VMEM(turned, F32), VMEM((n_early, rows, depth, width), F32), plane, plain(depth, rows)),
        (VMEM,) * 4,
        (HBM,) * 4,
        [
            SMEM(line.shape, F32),
            SMEM(cross.shape, F32),
            SMEM(index.shape, index.dtype),
            pltpu.SemaphoreType.DMA((3,)),
            pltpu.SemaphoreType.DMA((rows // CHUNK,)),
        ],
        cost=(40 * voxels, 0, 16 * voxels),
    )(*(pltpu.with_memory_space_constraint(v, HBM) for v in (line, cross, index, conc)))

    far = beyond(row_total, "det", False)

    trans, emit, own_depth = call(
        functools.partial(local_body, scale_x),
        "local",
        (cube, cube, plain(n_energy, depth, width)),
        (VMEM, VMEM, VMEM),
        (SMEM, SMEM) + (VMEM,) * 3,
        cost=(20 * voxels, 4 * voxels, 1024),
    )(cross, index, conc_x, emission, far_local)

    wide = (n_energy, depth, width)
    far_wide, pair = call(
        functools.partial(line_body, n_det), "line", (plane, plain(2, *wide)), (VMEM,) * 2, (VMEM,) * 3,
        cost=(8 * voxels, 0, 1024),
    )(far, emit, own_depth)

    fluor, rest = call(
        ahead_body, "ahead", (cube, cube), (VMEM, VMEM), (VMEM, VMEM, VMEM),
        cost=(20 * voxels, 0, 1024),
    )(far_wide, trans, emit)

    up = further = own_depth
    distance = 1
    while distance < n_beam:
        other = swap(pair, "beam", distance)
        kept = 1 if 2 * distance == n_beam else 2
        if kept == 1:
            other, fluor, rest = lax.optimization_barrier((other, fluor, rest))
        pair, up, further = call(
            functools.partial(merge_body, distance, distance == 1),
            "merge", (plain(kept, *wide), plain(*wide), plain(*wide)), (VMEM,) * 3, (VMEM,) * 4,
            cost=(1 << 14, 1 << 12, 1024),
        )(pair, other, up, further)
        distance *= 2

    lines = [pair] + [swap(pair, "slab", r) for r in range(1, n_slab)]
    close = [r for r in range(1, n_slab) if r & (r + 1) == 0]

    pixels = fan_offset.shape[0]
    gram, pull, fan_turned = call(
        functools.partial(fan_body, scale_sum), "fan", (plain(depth, depth * n_slab), plain(*wide), plain(pixels, depth * n_slab)),
        (VMEM,) * 3, (VMEM,) * 4, cost=(8 * depth * measured.size, 0, 4 * measured.size),
    )(fan_offset[None, :], fan_weight.T, measured, pair)

    near, column_total, gain, shift = call(
        functools.partial(back_body, scale_sum, close),
        "back",
        (plane, plain(depth, rows), plain(*wide), plain(n_species, depth, width)),
        (VMEM,) * 4,
        (SMEM, SMEM) + (VMEM,) * (5 + len(close)),
        cost=(10 * voxels, 0, 1024),
    )(cross, index, gram, pull, up, further, fluor, *(lines[r] for r in close))

    nearer = beyond(column_total, "det", True)

    scale_line = scale_y * LN2 / scale_x
    mixed = call(
        mix_body, "mix", (VMEM(turned, F32),), (VMEM,), (SMEM,) * 2 + (VMEM,) * 3,
        cost=(40 * voxels, 0, 1024),
    )(cross, index, gain, shift, rest)[0]

    share = pixels // (n_beam * n_slab)
    return tuple(
        call(
            functools.partial(finish_body, scale_sum, scale_line, n_det),
            "finish",
            (plain(*conc.shape), plain(n_energy, share, width)),
            (HBM, HBM),
            (SMEM,) + (VMEM,) * (5 + len(lines)),
            [
                VMEM(turned, F32),
                VMEM((n_energy, share, width), F32),
                pltpu.SemaphoreType.DMA((rows // CHUNK + 2,)),
                pltpu.SemaphoreType.DMA,
            ],
            limit=16,
            cost=(10 * voxels, 0, 16 * voxels),
        )(line, nearer, near, mixed, fan_turned, measured, *lines)
    )


def solution(mesh):
    in_specs = (P(None, "slab", "beam", "det"), P(), P(), P(), P(), P(), P(None, None, "det"))
    out_specs = (P(None, "slab", "beam", "det"), P(None, ("beam", "slab"), "det"))
    return jax.shard_map(shards, mesh=mesh, in_specs=in_specs, out_specs=out_specs, check_vma=False)
```

```python
import functools
import math

import jax
import jax.numpy as jnp
from jax import lax
from jax.experimental import pallas as pl
from jax.experimental.pallas import tpu as pltpu
from jax.sharding import PartitionSpec as P


VMEM, SMEM, HBM = pltpu.VMEM, pltpu.SMEM, pltpu.HBM
F32, BF16 = jnp.float32, jnp.bfloat16
LANES = 128
CHUNK = 32
STEP = 16
LN2 = math.log(2.0)
LOG2E = 1.0 / LN2


def call(body, out_shape, out_spaces, in_spaces, scratch=(), limit=8, cost=None):
    flops, exps, size = cost
    return pl.pallas_call(
        body,
        out_shape=out_shape,
        in_specs=[pl.BlockSpec(memory_space=s) for s in in_spaces],
        out_specs=[pl.BlockSpec(memory_space=s) for s in out_spaces],
        scratch_shapes=list(scratch),
        compiler_params=pltpu.CompilerParams(vmem_limit_bytes=limit << 20),
        cost_estimate=pl.CostEstimate(flops=flops, transcendentals=exps, bytes_accessed=size),
    )


def plain(*shape):
    return jax.ShapeDtypeStruct(shape, F32)


def split(value):
    high = value.astype(BF16)
    low = (value - high.astype(F32)).astype(BF16)
    return jnp.concatenate([high, low], axis=1)


def lane_sums(width, beyond):
    row = lax.broadcasted_iota(jnp.int32, (width, 2 * width), 0)
    col = lax.broadcasted_iota(jnp.int32, (width, 2 * width), 1)
    part = (row > col) if beyond else (row < col)
    ones = jnp.where(part | (col >= width), 1.0, 0.0).astype(BF16)
    return jnp.concatenate([ones, ones], axis=0)


def selected(cross_ref, index_ref):
    n_energy = index_ref.shape[0]
    columns = [index_ref[e] for e in range(n_energy)]
    return [[cross_ref[s, columns[e]] for e in range(n_energy)] for s in range(cross_ref.shape[0])]


def weighted(weights, values):
    total = weights[0] * values[0]
    for weight, value in zip(weights[1:], values[1:]):
        total = total + weight * value
    return total


def load_body(
    scale, scale_x, line_hbm, cross_hbm, index_hbm, conc_hbm, conc_ref, emit_ref, beyond_ref, total_ref,
    line_ref, cross_ref, index_ref, small_sems, sems,
):
    n_species, depth, rows, width = conc_hbm.shape
    n_early = emit_ref.shape[0]

    def copies(chunk):
        span = pl.ds(chunk * CHUNK, CHUNK)
        return [
            pltpu.make_async_copy(conc_hbm.at[:, z, span, :], conc_ref.at[:, span, z, :], sems.at[chunk])
            for z in range(depth)
        ]

    small = [
        pltpu.make_async_copy(source, target, small_sems.at[i])
        for i, (source, target) in enumerate(
            [(line_hbm, line_ref), (cross_hbm, cross_ref), (index_hbm, index_ref)]
        )
    ]
    for copy in small:
        copy.start()
    for chunk in range(rows // CHUNK):
        for copy in copies(chunk):
            copy.start()
    table = lane_sums(width, True)
    lane = lax.broadcasted_iota(jnp.int32, (depth, LANES), 1)
    for copy in small:
        copy.wait()
    line = [line_ref[s] * scale for s in range(n_species)]
    sigma = [[v * scale_x for v in row] for row in selected(cross_ref, index_ref)]
    for part in range(rows // LANES):
        total = jnp.zeros((depth, LANES), F32)
        for piece in range(LANES // CHUNK):
            chunk = part * (LANES // CHUNK) + piece
            for copy in copies(chunk):
                copy.wait()
            absorber = []
            for q in range(CHUNK):
                x = chunk * CHUNK + q
                conc = [conc_ref[s, x] for s in range(n_species)]
                absorber.append(weighted(line, conc))
                for e in range(n_early):
                    emit_ref[e, x] = weighted([sigma[s][e] for s in range(n_species)], conc)
            sums = jnp.dot(split(jnp.concatenate(absorber, axis=0)), table, preferred_element_type=F32)
            for q in range(CHUNK):
                here = sums[q * depth : (q + 1) * depth]
                beyond_ref[chunk * CHUNK + q] = here[:, :width]
                total = jnp.where(lane == piece * CHUNK + q, here[:, width : width + LANES], total)
        total_ref[:, part * LANES : (part + 1) * LANES] = total


def local_body(scale, cross_ref, index_ref, conc_ref, early_ref, beyond_ref, trans_ref, emit_ref, depth_ref):
    n_energy, rows, depth, width = trans_ref.shape
    n_species, n_early = conc_ref.shape[0], early_ref.shape[0]
    sigma = [[v * scale for v in row] for row in selected(cross_ref, index_ref)]

    def step(block, path):
        path = list(path)
        for q in range(STEP):
            x = block * STEP + q
            beyond = beyond_ref[x]
            conc = [conc_ref[s, x] for s in range(n_species)]
            for e in range(n_energy):
                if e < n_early:
                    emission = early_ref[e, x]
                else:
                    emission = weighted([sigma[s][e] for s in range(n_species)], conc)
                trans = jnp.exp2(path[e] + beyond)
                trans_ref[e, x] = trans
                emit_ref[e, x] = emission * trans
                path[e] = path[e] + emission
        return tuple(path)

    zero = jnp.zeros((depth, width), F32)
    path = lax.fori_loop(0, rows // STEP, step, (zero,) * n_energy)
    for e in range(n_energy):
        depth_ref[e] = path[e]


def reached(axis, count, backward):
    if count != 2:
        return True
    return lax.axis_index(axis) == (1 if backward else 0)


def columns(source_ref, change, width):
    depth, rows = source_ref.shape
    for part in range(rows // LANES):
        held = change(source_ref[:, part * LANES : (part + 1) * LANES])
        for q in range(LANES):
            yield part * LANES + q, jnp.broadcast_to(held[:, q : q + 1], (depth, width))


def line_body(count, far_ref, emit_ref, depth_ref, far_out, pair_ref):
    n_energy, _, _, width = emit_ref.shape
    keep = jnp.where(reached("det", count, False), 1.0, 0.0)
    sums = [[None, None] for _ in range(n_energy)]
    for x, factor in columns(far_ref, lambda v: jnp.exp2(v * keep), width):
        far_out[x] = factor
        for e in range(n_energy):
            value = factor * emit_ref[e, x]
            sums[e][x % 2] = value if x < 2 else sums[e][x % 2] + value
    for e in range(n_energy):
        pair_ref[0, e] = depth_ref[e]
        pair_ref[1, e] = sums[e][0] + sums[e][1]


def merge_body(*refs):
    pairs, (total_ref, up_ref, further_ref) = refs[:-3], refs[-3:]
    beam = lax.axis_index("beam")
    state = [(ref[0], ref[1]) for ref in pairs]
    up, further = jnp.zeros_like(state[0][0]), jnp.zeros_like(state[0][0])
    distance = 1
    while len(state) > 1:
        lower = (beam & distance) == 0
        merged = []
        for i in range(0, len(state), 2):
            (span, sums), (other_span, other_sums) = state[i], state[i + 1]
            fade = jnp.exp2(jnp.where(lower, span, other_span))
            late = fade * jnp.where(lower, other_sums, sums)
            if i == 0:
                further = jnp.where(lower, further + late, fade * further)
                up = jnp.where(lower, up, up + other_span)
            merged.append((span + other_span, jnp.where(lower, sums, other_sums) + late))
        state = merged
        distance *= 2
    total_ref[0] = state[0][1]
    up_ref[...] = up
    further_ref[...] = further


def ahead_body(far_ref, trans_ref, emit_ref, fluor_ref, rest_ref):
    n_energy, rows, depth, width = emit_ref.shape

    def step(block, ahead):
        ahead = list(ahead)
        for q in range(STEP):
            x = rows - 1 - (block * STEP + q)
            far = far_ref[x]
            for e in range(n_energy):
                fluor = far * emit_ref[e, x]
                fluor_ref[e, x] = fluor
                rest_ref[e, x] = far * trans_ref[e, x] + ahead[e]
                ahead[e] = ahead[e] + LN2 * fluor
        return tuple(ahead)

    zero = jnp.zeros((depth, width), F32)
    lax.fori_loop(0, rows // STEP, step, (zero,) * n_energy)


def fan_body(scale, near_slabs, offset_ref, weight_ref, measured_ref, own_ref, gram_ref, pull_ref, turned_ref):
    depth, n_slab = gram_ref.shape[0], turned_ref.shape[1] // gram_ref.shape[0]
    taps, pixels = weight_ref.shape
    own = lax.axis_index("slab")
    offset = jnp.broadcast_to(offset_ref[...], (depth, pixels))
    level = lax.broadcasted_iota(jnp.int32, (depth, pixels), 0) - offset
    taps = [jnp.broadcast_to(weight_ref[j : j + 1, :], (depth, pixels)).astype(F32) for j in range(taps)]

    def block(slab):
        place = level + slab * depth
        found = jnp.zeros((depth, pixels), F32)
        for j, tap in enumerate(taps):
            found = found + jnp.where(place == j, tap, 0.0)
        return found

    blocks = [block(own ^ r) for r in range(n_slab)]
    turned_ref[...] = jnp.concatenate(blocks, axis=0).T
    odd = own + jnp.where((own & 1) == 1, 1, -1)
    near = jnp.concatenate([block(odd) if r is None else blocks[r] for r in near_slabs], axis=0)
    gram = lax.dot_general(
        blocks[0].astype(BF16), near.astype(BF16), (((1,), (1,)), ((), ())), preferred_element_type=F32
    )
    gram_ref[...] = gram
    n_energy, _, width = pull_ref.shape
    sums = weigh(gram, [(0, own_ref, 0)], depth, n_energy, width)
    for e in range(n_energy):
        pull_ref[e] = sums[e] * scale - jnp.dot(
            blocks[0], measured_ref[e], precision=lax.Precision.HIGHEST, preferred_element_type=F32
        )


def weigh(weights, lines, depth, n_energy, width):
    height = weights.shape[0]
    sums = [[None, None] for _ in range(n_energy)]
    for order, (r, lines_ref, i) in enumerate(lines):
        for z in range(depth):
            place = r * depth + z
            weight = jnp.broadcast_to(weights[:, place : place + 1], (height, width))
            for e in range(n_energy):
                value = weight * lines_ref[i, e, z : z + 1, :]
                sums[e][z % 2] = value if order == 0 and z < 2 else sums[e][z % 2] + value
    return [a + b for a, b in sums]


def back_body(scale, cross_ref, index_ref, gram_ref, pull_ref, up_ref, further_ref, fluor_ref, *refs):
    lines, (near_ref, total_ref, gain_ref, shift_ref) = refs[:-4], refs[-4:]
    n_energy, rows, depth, width = fluor_ref.shape
    n_species = shift_ref.shape[0]
    sums = weigh(gram_ref[...], [(r + 1, ref, 0) for r, ref in enumerate(lines)], depth, n_energy, width)
    back = [sums[e] * scale + pull_ref[e] for e in range(n_energy)]
    gain = [back[e] * jnp.exp2(up_ref[e]) for e in range(n_energy)]
    sigma = selected(cross_ref, index_ref)
    pushed = [LN2 * back[e] * further_ref[e] for e in range(n_energy)]
    for e in range(n_energy):
        gain_ref[e] = gain[e]
    for s in range(n_species):
        shift_ref[s] = weighted(sigma[s], pushed)
    table = lane_sums(width, False)
    lane = lax.broadcasted_iota(jnp.int32, (depth, LANES), 1)
    for part in range(rows // LANES):
        total = jnp.zeros((depth, LANES), F32)
        for piece in range(LANES // CHUNK):
            first = part * LANES + piece * CHUNK
            heavy = [weighted(gain, [fluor_ref[e, first + q] for e in range(n_energy)]) for q in range(CHUNK)]
            found = jnp.dot(split(jnp.concatenate(heavy, axis=0)), table, preferred_element_type=F32)
            for q in range(CHUNK):
                here = found[q * depth : (q + 1) * depth]
                near_ref[first + q] = here[:, :width]
                total = jnp.where(lane == piece * CHUNK + q, here[:, width : width + LANES], total)
        total_ref[:, part * LANES : (part + 1) * LANES] = total


def mix_body(cross_ref, index_ref, gain_ref, shift_ref, rest_ref, out_ref):
    n_energy, rows, _, _ = rest_ref.shape
    n_species = out_ref.shape[0]
    sigma = selected(cross_ref, index_ref)
    mixed = [[sigma[s][e] * gain_ref[e] for e in range(n_energy)] for s in range(n_species)]
    shift = [shift_ref[s] for s in range(n_species)]

    def step(block, carry):
        for q in range(STEP):
            x = block * STEP + q
            rest = [rest_ref[e, x] for e in range(n_energy)]
            for s in range(n_species):
                out_ref[s, x] = weighted(mixed[s], rest) + shift[s]
        return carry

    lax.fori_loop(0, rows // STEP, step, 0)


def finish_body(
    scale, scale_line, count, line_ref, nearer_ref, near_ref, mix_ref, fan_ref, measured_ref, *refs
):
    lines, (grad_hbm, residual_hbm, grad_ref, residual_ref, sems, residual_sem) = refs[:-6], refs[-6:]
    n_species, rows, depth, width = mix_ref.shape
    n_energy, share, _ = residual_ref.shape
    line = [line_ref[s] * scale_line for s in range(n_species)]
    keep = jnp.where(reached("det", count, True), 1.0, 0.0)

    ends = [8, 16] + list(range(CHUNK, rows + 1, CHUNK))

    def copies(chunk):
        first = ends[chunk - 1] if chunk else 0
        span = pl.ds(first, ends[chunk] - first)
        return [
            pltpu.make_async_copy(grad_ref.at[:, span, z, :], grad_hbm.at[:, z, span, :], sems.at[chunk])
            for z in range(depth)
        ]

    for x, column in columns(nearer_ref, lambda v: v * keep, width):
        before = near_ref[x] + column
        for s in range(n_species):
            grad_ref[s, x] = mix_ref[s, x] + line[s] * before
        if x + 1 in ends:
            for copy in copies(ends.index(x + 1)):
                copy.start()

    start = pl.multiple_of(lax.axis_index(("beam", "slab")) * share, share)
    pieces = [(ref, i) for ref in lines for i in range(ref.shape[0])]
    pieces = [(r, ref, i) for r, (ref, i) in enumerate(pieces)]
    sums = weigh(fan_ref[pl.ds(start, share), :], pieces, depth, n_energy, width)
    for e in range(n_energy):
        residual_ref[e] = sums[e] * scale - measured_ref[e, pl.ds(start, share), :]
    copy = pltpu.make_async_copy(residual_ref, residual_hbm, residual_sem)
    copy.start()

    for chunk in range(len(ends)):
        for done in copies(chunk):
            done.wait()
    copy.wait()


def odd_pairs(n_beam, n_slab):
    pairs = []
    for beam in range(n_beam):
        for slab in range(n_slab):
            other = slab + 1 if slab % 2 else slab - 1
            if 0 <= other < n_slab:
                target = beam * n_slab + other
            else:
                target = (beam ^ (n_beam // 2)) * n_slab + slab
            pairs.append((beam * n_slab + slab, target))
    return pairs


def swap(value, axis, distance):
    return lax.ppermute(value, axis, [(i, i ^ distance) for i in range(lax.axis_size(axis))])


def beyond(value, axis, backward):
    count = lax.axis_size(axis)
    if count == 2:
        return swap(value, axis, 1)
    mine = lax.axis_index(axis)
    pieces = lax.all_gather(value, axis)
    places = jnp.arange(count)
    keep = (places < mine) if backward else (places > mine)
    return jnp.sum(jnp.where(keep.reshape((-1,) + (1,) * value.ndim), pieces, 0.0), axis=0)


def shards(conc, cross, line, index, fan_offset, fan_weight, measured):
    n_species, depth, rows, width = conc.shape
    n_energy = index.shape[0]
    n_beam, n_det, n_slab = (lax.axis_size(a) for a in ("beam", "det", "slab"))
    assert n_beam & (n_beam - 1) == 0 and n_slab & (n_slab - 1) == 0
    assert fan_weight.shape[1] <= depth + 1
    assert rows % LANES == 0 and width % LANES == 0 and depth % 8 == 0
    full_x, full_y = rows * n_beam, width * n_det
    scale_x = -(1.5 / full_x) * LOG2E
    scale_y = -(1.5 / full_y) * LOG2E
    scale_sum = 1.0 / (scale_x * full_x)
    voxels = depth * rows * width
    turned = (n_species, rows, depth, width)
    cube = VMEM((n_energy, rows, depth, width), F32)
    plane = VMEM((rows, depth, width), F32)

    n_early = n_energy // 2
    conc_x, emission, far_local, row_total = call(
        functools.partial(load_body, scale_y, scale_x),
        (VMEM(turned, F32), VMEM((n_early, rows, depth, width), F32), plane, plain(depth, rows)),
        (VMEM,) * 4,
        (HBM,) * 4,
        [
            SMEM(line.shape, F32),
            SMEM(cross.shape, F32),
            SMEM(index.shape, index.dtype),
            pltpu.SemaphoreType.DMA((3,)),
            pltpu.SemaphoreType.DMA((rows // CHUNK,)),
        ],
        cost=(40 * voxels, 0, 16 * voxels),
    )(*(pltpu.with_memory_space_constraint(v, HBM) for v in (line, cross, index, conc)))

    far = beyond(row_total, "det", False)

    trans, emit, own_depth = call(
        functools.partial(local_body, scale_x),
        (cube, cube, plain(n_energy, depth, width)),
        (VMEM, VMEM, VMEM),
        (SMEM, SMEM) + (VMEM,) * 3,
        cost=(20 * voxels, 4 * voxels, 1024),
    )(cross, index, conc_x, emission, far_local)

    wide = (n_energy, depth, width)
    far_wide, pair = call(
        functools.partial(line_body, n_det), (plane, plain(2, *wide)), (VMEM,) * 2, (VMEM,) * 3,
        cost=(8 * voxels, 0, 1024),
    )(far, emit, own_depth)

    fluor, rest = call(
        ahead_body, (cube, cube), (VMEM, VMEM), (VMEM, VMEM, VMEM),
        cost=(20 * voxels, 0, 1024),
    )(far_wide, trans, emit)

    others = [swap(pair, "beam", r) for r in range(1, n_beam)]
    if others:
        others[-1], fluor, rest = lax.optimization_barrier((others[-1], fluor, rest))
    total, up, further = call(
        merge_body, (plain(1, *wide), plain(*wide), plain(*wide)), (VMEM,) * 3, (VMEM,) * n_beam,
        cost=(1 << 15, 1 << 13, 1024),
    )(pair, *others)

    if n_slab == 4 and n_beam > 1:
        even = swap(total, "slab", 1)
        odd = lax.ppermute(total, ("beam", "slab"), odd_pairs(n_beam, n_slab))
        near_lines = [total, even, odd]
        near_slabs = [0, 1, None]
        half = jnp.concatenate([total, even], axis=0)
        lines = [total, even, swap(half, "slab", 2)]
    else:
        lines = [total] + [swap(total, "slab", r) for r in range(1, n_slab)]
        near_slabs = [r for r in range(n_slab) if r & (r + 1) == 0]
        near_lines = [lines[r] for r in near_slabs]

    pixels = fan_offset.shape[0]
    gram, pull, fan_turned = call(
        functools.partial(fan_body, scale_sum, near_slabs), (plain(depth, depth * len(near_slabs)), plain(*wide), plain(pixels, depth * n_slab)),
        (VMEM,) * 3, (VMEM,) * 4, cost=(8 * depth * measured.size, 0, 4 * measured.size),
    )(fan_offset[None, :], fan_weight.T, measured, total)

    near, column_total, gain, shift = call(
        functools.partial(back_body, scale_sum),
        (plane, plain(depth, rows), plain(*wide), plain(n_species, depth, width)),
        (VMEM,) * 4,
        (SMEM, SMEM) + (VMEM,) * (4 + len(near_lines)),
        cost=(10 * voxels, 0, 1024),
    )(cross, index, gram, pull, up, further, fluor, *near_lines[1:])

    nearer = beyond(column_total, "det", True)

    scale_line = scale_y * LN2 / scale_x
    mixed = call(
        mix_body, (VMEM(turned, F32),), (VMEM,), (SMEM,) * 2 + (VMEM,) * 3,
        cost=(40 * voxels, 0, 1024),
    )(cross, index, gain, shift, rest)[0]

    share = pixels // (n_beam * n_slab)
    return tuple(
        call(
            functools.partial(finish_body, scale_sum, scale_line, n_det),
            (plain(*conc.shape), plain(n_energy, share, width)),
            (HBM, HBM),
            (SMEM,) + (VMEM,) * (5 + len(lines)),
            [
                VMEM(turned, F32),
                VMEM((n_energy, share, width), F32),
                pltpu.SemaphoreType.DMA((rows // CHUNK + 2,)),
                pltpu.SemaphoreType.DMA,
            ],
            limit=16,
            cost=(10 * voxels, 0, 16 * voxels),
        )(line, nearer, near, mixed, fan_turned, measured, *lines)
    )


def solution(mesh):
    in_specs = (P(None, "slab", "beam", "det"), P(), P(), P(), P(), P(), P(None, None, "det"))
    out_specs = (P(None, "slab", "beam", "det"), P(None, ("beam", "slab"), "det"))
    return jax.shard_map(shards, mesh=mesh, in_specs=in_specs, out_specs=out_specs, check_vma=False)
```

```python
import functools
import math

import jax
import jax.numpy as jnp
from jax import lax
from jax.experimental import pallas as pl
from jax.experimental.pallas import tpu as pltpu
from jax.sharding import PartitionSpec as P


VMEM, SMEM, HBM = pltpu.VMEM, pltpu.SMEM, pltpu.HBM
F32, BF16 = jnp.float32, jnp.bfloat16
LANES = 128
CHUNK = 32
STEP = 16
LN2 = math.log(2.0)
LOG2E = 1.0 / LN2


def call(body, out_shape, out_spaces, in_spaces, scratch=(), limit=8, cost=None):
    flops, exps, size = cost
    return pl.pallas_call(
        body,
        out_shape=out_shape,
        in_specs=[pl.BlockSpec(memory_space=s) for s in in_spaces],
        out_specs=[pl.BlockSpec(memory_space=s) for s in out_spaces],
        scratch_shapes=list(scratch),
        compiler_params=pltpu.CompilerParams(vmem_limit_bytes=limit << 20),
        cost_estimate=pl.CostEstimate(flops=flops, transcendentals=exps, bytes_accessed=size),
    )


def plain(*shape):
    return jax.ShapeDtypeStruct(shape, F32)


def split(value):
    high = value.astype(BF16)
    low = (value - high.astype(F32)).astype(BF16)
    return jnp.concatenate([high, low], axis=1)


def lane_sums(width, beyond):
    row = lax.broadcasted_iota(jnp.int32, (width, 2 * width), 0)
    col = lax.broadcasted_iota(jnp.int32, (width, 2 * width), 1)
    part = (row > col) if beyond else (row < col)
    ones = jnp.where(part | (col >= width), 1.0, 0.0).astype(BF16)
    return jnp.concatenate([ones, ones], axis=0)


def selected(cross_ref, index_ref):
    n_energy = index_ref.shape[0]
    columns = [index_ref[e] for e in range(n_energy)]
    return [[cross_ref[s, columns[e]] for e in range(n_energy)] for s in range(cross_ref.shape[0])]


def planes(plane_ref, n_species, n_energy):
    cross = [[plane_ref[s * n_energy + e] for e in range(n_energy)] for s in range(n_species)]
    return cross, [plane_ref[n_species * n_energy + s] for s in range(n_species)]


def weighted(weights, values):
    total = weights[0] * values[0]
    for weight, value in zip(weights[1:], values[1:]):
        total = total + weight * value
    return total


def load_body(
    scale, scale_x, line_hbm, cross_hbm, index_hbm, conc_hbm, conc_ref, emit_ref, beyond_ref, total_ref, plane_ref,
    line_ref, cross_ref, index_ref, small_sems, sems,
):
    n_species, depth, rows, width = conc_hbm.shape
    n_early = emit_ref.shape[0]

    def copies(chunk):
        span = pl.ds(chunk * CHUNK, CHUNK)
        return [
            pltpu.make_async_copy(conc_hbm.at[:, z, span, :], conc_ref.at[:, span, z, :], sems.at[chunk])
            for z in range(depth)
        ]

    small = [
        pltpu.make_async_copy(source, target, small_sems.at[i])
        for i, (source, target) in enumerate(
            [(line_hbm, line_ref), (cross_hbm, cross_ref), (index_hbm, index_ref)]
        )
    ]
    for copy in small:
        copy.start()
    for chunk in range(rows // CHUNK):
        for copy in copies(chunk):
            copy.start()
    table = lane_sums(width, True)
    lane = lax.broadcasted_iota(jnp.int32, (depth, LANES), 1)
    for copy in small:
        copy.wait()
    line = [line_ref[s] * scale for s in range(n_species)]
    sigma = selected(cross_ref, index_ref)
    scalars = [v for row in sigma for v in row] + [line_ref[s] for s in range(n_species)]
    for i, value in enumerate(scalars):
        plane_ref[i] = jnp.full((depth, width), value)
    sigma = [[v * scale_x for v in row] for row in sigma]
    for part in range(rows // LANES):
        total = jnp.zeros((depth, LANES), F32)
        for piece in range(LANES // CHUNK):
            chunk = part * (LANES // CHUNK) + piece
            for copy in copies(chunk):
                copy.wait()
            absorber = []
            for q in range(CHUNK):
                x = chunk * CHUNK + q
                conc = [conc_ref[s, x] for s in range(n_species)]
                absorber.append(weighted(line, conc))
                for e in range(n_early):
                    emit_ref[e, x] = weighted([sigma[s][e] for s in range(n_species)], conc)
            sums = jnp.dot(split(jnp.concatenate(absorber, axis=0)), table, preferred_element_type=F32)
            for q in range(CHUNK):
                here = sums[q * depth : (q + 1) * depth]
                beyond_ref[chunk * CHUNK + q] = here[:, :width]
                total = jnp.where(lane == piece * CHUNK + q, here[:, width : width + LANES], total)
        total_ref[:, part * LANES : (part + 1) * LANES] = total


def local_body(scale, plane_ref, conc_ref, early_ref, beyond_ref, trans_ref, emit_ref, depth_ref):
    n_energy, rows, depth, width = trans_ref.shape
    n_species, n_early = conc_ref.shape[0], early_ref.shape[0]
    sigma = [[v * scale for v in row] for row in planes(plane_ref, n_species, n_energy)[0]]

    def step(block, path):
        path = list(path)
        for q in range(STEP):
            x = block * STEP + q
            beyond = beyond_ref[x]
            conc = [conc_ref[s, x] for s in range(n_species)]
            for e in range(n_energy):
                if e < n_early:
                    emission = early_ref[e, x]
                else:
                    emission = weighted([sigma[s][e] for s in range(n_species)], conc)
                trans = jnp.exp2(path[e] + beyond)
                trans_ref[e, x] = trans
                emit_ref[e, x] = emission * trans
                path[e] = path[e] + emission
        return tuple(path)

    zero = jnp.zeros((depth, width), F32)
    path = lax.fori_loop(0, rows // STEP, step, (zero,) * n_energy)
    for e in range(n_energy):
        depth_ref[e] = path[e]


def reached(axis, count, backward):
    if count != 2:
        return True
    return lax.axis_index(axis) == (1 if backward else 0)


def columns(source_ref, change, width):
    depth, rows = source_ref.shape
    for part in range(rows // LANES):
        held = change(source_ref[:, part * LANES : (part + 1) * LANES])
        for q in range(LANES):
            yield part * LANES + q, jnp.broadcast_to(held[:, q : q + 1], (depth, width))


def line_body(count, far_ref, emit_ref, depth_ref, far_out, pair_ref):
    n_energy, _, _, width = emit_ref.shape
    keep = jnp.where(reached("det", count, False), 1.0, 0.0)
    sums = [[None, None] for _ in range(n_energy)]
    for x, factor in columns(far_ref, lambda v: jnp.exp2(v * keep), width):
        far_out[x] = factor
        for e in range(n_energy):
            value = factor * emit_ref[e, x]
            sums[e][x % 2] = value if x < 2 else sums[e][x % 2] + value
    for e in range(n_energy):
        pair_ref[0, e] = depth_ref[e]
        pair_ref[1, e] = sums[e][0] + sums[e][1]


def merge_body(*refs):
    pairs, (total_ref, up_ref, further_ref) = refs[:-3], refs[-3:]
    beam = lax.axis_index("beam")
    state = [(ref[0], ref[1]) for ref in pairs]
    up, further = jnp.zeros_like(state[0][0]), jnp.zeros_like(state[0][0])
    distance = 1
    while len(state) > 1:
        lower = (beam & distance) == 0
        merged = []
        for i in range(0, len(state), 2):
            (span, sums), (other_span, other_sums) = state[i], state[i + 1]
            fade = jnp.exp2(jnp.where(lower, span, other_span))
            late = fade * jnp.where(lower, other_sums, sums)
            if i == 0:
                further = jnp.where(lower, further + late, fade * further)
                up = jnp.where(lower, up, up + other_span)
            merged.append((span + other_span, jnp.where(lower, sums, other_sums) + late))
        state = merged
        distance *= 2
    total_ref[0] = state[0][1]
    up_ref[...] = up
    further_ref[...] = further


def ahead_body(far_ref, trans_ref, emit_ref, fluor_ref, rest_ref):
    n_energy, rows, depth, width = emit_ref.shape

    def step(block, ahead):
        ahead = list(ahead)
        for q in range(STEP):
            x = rows - 1 - (block * STEP + q)
            far = far_ref[x]
            for e in range(n_energy):
                fluor = far * emit_ref[e, x]
                fluor_ref[e, x] = fluor
                rest_ref[e, x] = far * trans_ref[e, x] + ahead[e]
                ahead[e] = ahead[e] + LN2 * fluor
        return tuple(ahead)

    zero = jnp.zeros((depth, width), F32)
    lax.fori_loop(0, rows // STEP, step, (zero,) * n_energy)


def fan_body(scale, near_slabs, offset_ref, weight_ref, measured_ref, own_ref, gram_ref, pull_ref, turned_ref):
    depth, n_slab = gram_ref.shape[0], turned_ref.shape[1] // gram_ref.shape[0]
    taps, pixels = weight_ref.shape
    own = lax.axis_index("slab")
    offset = jnp.broadcast_to(offset_ref[...], (depth, pixels))
    level = lax.broadcasted_iota(jnp.int32, (depth, pixels), 0) - offset
    taps = [jnp.broadcast_to(weight_ref[j : j + 1, :], (depth, pixels)).astype(F32) for j in range(taps)]

    def block(slab):
        place = level + slab * depth
        found = jnp.zeros((depth, pixels), F32)
        for j, tap in enumerate(taps):
            found = found + jnp.where(place == j, tap, 0.0)
        return found

    blocks = [block(own ^ r) for r in range(n_slab)]
    turned_ref[...] = jnp.concatenate(blocks, axis=0).T
    odd = own + jnp.where((own & 1) == 1, 1, -1)
    near = jnp.concatenate([block(odd) if r is None else blocks[r] for r in near_slabs], axis=0)
    gram = lax.dot_general(
        blocks[0].astype(BF16), near.astype(BF16), (((1,), (1,)), ((), ())), preferred_element_type=F32
    )
    gram_ref[...] = gram
    n_energy, _, width = pull_ref.shape
    sums = weigh(gram, [(0, own_ref, 0)], depth, n_energy, width)
    for e in range(n_energy):
        pull_ref[e] = sums[e] * scale - jnp.dot(
            blocks[0], measured_ref[e], precision=lax.Precision.HIGHEST, preferred_element_type=F32
        )


def weigh(weights, lines, depth, n_energy, width):
    height = weights.shape[0]
    sums = [[None, None] for _ in range(n_energy)]
    for order, (r, lines_ref, i) in enumerate(lines):
        for z in range(depth):
            place = r * depth + z
            weight = jnp.broadcast_to(weights[:, place : place + 1], (height, width))
            for e in range(n_energy):
                value = weight * lines_ref[i, e, z : z + 1, :]
                sums[e][z % 2] = value if order == 0 and z < 2 else sums[e][z % 2] + value
    return [a + b for a, b in sums]


def back_body(scale, plane_ref, gram_ref, pull_ref, up_ref, further_ref, fluor_ref, *refs):
    lines, (near_ref, total_ref, gain_ref, shift_ref) = refs[:-4], refs[-4:]
    n_energy, rows, depth, width = fluor_ref.shape
    n_species = shift_ref.shape[0]
    sums = weigh(gram_ref[...], [(r + 1, ref, 0) for r, ref in enumerate(lines)], depth, n_energy, width)
    back = [sums[e] * scale + pull_ref[e] for e in range(n_energy)]
    gain = [back[e] * jnp.exp2(up_ref[e]) for e in range(n_energy)]
    sigma, _ = planes(plane_ref, n_species, n_energy)
    pushed = [LN2 * back[e] * further_ref[e] for e in range(n_energy)]
    for e in range(n_energy):
        gain_ref[e] = gain[e]
    for s in range(n_species):
        shift_ref[s] = weighted(sigma[s], pushed)
    table = lane_sums(width, False)
    lane = lax.broadcasted_iota(jnp.int32, (depth, LANES), 1)
    for part in range(rows // LANES):
        total = jnp.zeros((depth, LANES), F32)
        for piece in range(LANES // CHUNK):
            first = part * LANES + piece * CHUNK
            heavy = [weighted(gain, [fluor_ref[e, first + q] for e in range(n_energy)]) for q in range(CHUNK)]
            found = jnp.dot(split(jnp.concatenate(heavy, axis=0)), table, preferred_element_type=F32)
            for q in range(CHUNK):
                here = found[q * depth : (q + 1) * depth]
                near_ref[first + q] = here[:, :width]
                total = jnp.where(lane == piece * CHUNK + q, here[:, width : width + LANES], total)
        total_ref[:, part * LANES : (part + 1) * LANES] = total


def mix_body(plane_ref, gain_ref, shift_ref, rest_ref, out_ref):
    n_energy, rows, _, _ = rest_ref.shape
    n_species = out_ref.shape[0]
    sigma, _ = planes(plane_ref, n_species, n_energy)
    mixed = [[sigma[s][e] * gain_ref[e] for e in range(n_energy)] for s in range(n_species)]
    shift = [shift_ref[s] for s in range(n_species)]

    def step(block, carry):
        for q in range(STEP):
            x = block * STEP + q
            rest = [rest_ref[e, x] for e in range(n_energy)]
            for s in range(n_species):
                out_ref[s, x] = weighted(mixed[s], rest) + shift[s]
        return carry

    lax.fori_loop(0, rows // STEP, step, 0)


def finish_body(
    scale, scale_line, count, plane_ref, nearer_ref, near_ref, mix_ref, fan_ref, measured_ref, *refs
):
    lines, (grad_hbm, residual_hbm, grad_ref, residual_ref, sems, residual_sem) = refs[:-6], refs[-6:]
    n_species, rows, depth, width = mix_ref.shape
    n_energy, share, _ = residual_ref.shape
    line = [v * scale_line for v in planes(plane_ref, n_species, n_energy)[1]]
    keep = jnp.where(reached("det", count, True), 1.0, 0.0)

    ends = [8, 16] + list(range(CHUNK, rows + 1, CHUNK))

    def copies(chunk):
        first = ends[chunk - 1] if chunk else 0
        span = pl.ds(first, ends[chunk] - first)
        return [
            pltpu.make_async_copy(grad_ref.at[:, span, z, :], grad_hbm.at[:, z, span, :], sems.at[chunk])
            for z in range(depth)
        ]

    for x, column in columns(nearer_ref, lambda v: v * keep, width):
        before = near_ref[x] + column
        for s in range(n_species):
            grad_ref[s, x] = mix_ref[s, x] + line[s] * before
        if x + 1 in ends:
            for copy in copies(ends.index(x + 1)):
                copy.start()

    start = pl.multiple_of(lax.axis_index(("beam", "slab")) * share, share)
    pieces = [(ref, i) for ref in lines for i in range(ref.shape[0])]
    pieces = [(r, ref, i) for r, (ref, i) in enumerate(pieces)]
    sums = weigh(fan_ref[pl.ds(start, share), :], pieces, depth, n_energy, width)
    for e in range(n_energy):
        residual_ref[e] = sums[e] * scale - measured_ref[e, pl.ds(start, share), :]
    copy = pltpu.make_async_copy(residual_ref, residual_hbm, residual_sem)
    copy.start()

    for chunk in range(len(ends)):
        for done in copies(chunk):
            done.wait()
    copy.wait()


def odd_pairs(n_beam, n_slab):
    pairs = []
    for beam in range(n_beam):
        for slab in range(n_slab):
            other = slab + 1 if slab % 2 else slab - 1
            if 0 <= other < n_slab:
                target = beam * n_slab + other
            else:
                target = (beam ^ (n_beam // 2)) * n_slab + slab
            pairs.append((beam * n_slab + slab, target))
    return pairs


def swap(value, axis, distance):
    return lax.ppermute(value, axis, [(i, i ^ distance) for i in range(lax.axis_size(axis))])


def beyond(value, axis, backward):
    count = lax.axis_size(axis)
    if count == 2:
        return swap(value, axis, 1)
    mine = lax.axis_index(axis)
    pieces = lax.all_gather(value, axis)
    places = jnp.arange(count)
    keep = (places < mine) if backward else (places > mine)
    return jnp.sum(jnp.where(keep.reshape((-1,) + (1,) * value.ndim), pieces, 0.0), axis=0)


def shards(conc, cross, line, index, fan_offset, fan_weight, measured):
    n_species, depth, rows, width = conc.shape
    n_energy = index.shape[0]
    n_beam, n_det, n_slab = (lax.axis_size(a) for a in ("beam", "det", "slab"))
    assert n_beam & (n_beam - 1) == 0 and n_slab & (n_slab - 1) == 0
    assert fan_weight.shape[1] <= depth + 1
    assert rows % LANES == 0 and width % LANES == 0 and depth % 8 == 0
    full_x, full_y = rows * n_beam, width * n_det
    scale_x = -(1.5 / full_x) * LOG2E
    scale_y = -(1.5 / full_y) * LOG2E
    scale_sum = 1.0 / (scale_x * full_x)
    voxels = depth * rows * width
    turned = (n_species, rows, depth, width)
    cube = VMEM((n_energy, rows, depth, width), F32)
    plane = VMEM((rows, depth, width), F32)

    n_early = n_energy // 2
    conc_x, emission, far_local, row_total, fixed = call(
        functools.partial(load_body, scale_y, scale_x),
        (VMEM(turned, F32), VMEM((n_early, rows, depth, width), F32), plane, plain(depth, rows),
         VMEM((n_species * n_energy + n_species, depth, width), F32)),
        (VMEM,) * 5,
        (HBM,) * 4,
        [
            SMEM(line.shape, F32),
            SMEM(cross.shape, F32),
            SMEM(index.shape, index.dtype),
            pltpu.SemaphoreType.DMA((3,)),
            pltpu.SemaphoreType.DMA((rows // CHUNK,)),
        ],
        cost=(40 * voxels, 0, 16 * voxels),
    )(*(pltpu.with_memory_space_constraint(v, HBM) for v in (line, cross, index, conc)))

    far = beyond(row_total, "det", False)

    trans, emit, own_depth = call(
        functools.partial(local_body, scale_x),
        (cube, cube, plain(n_energy, depth, width)),
        (VMEM, VMEM, VMEM),
        (VMEM,) * 4,
        cost=(20 * voxels, 4 * voxels, 1024),
    )(fixed, conc_x, emission, far_local)

    wide = (n_energy, depth, width)
    far_wide, pair = call(
        functools.partial(line_body, n_det), (plane, plain(2, *wide)), (VMEM,) * 2, (VMEM,) * 3,
        cost=(8 * voxels, 0, 1024),
    )(far, emit, own_depth)

    fluor, rest = call(
        ahead_body, (cube, cube), (VMEM, VMEM), (VMEM, VMEM, VMEM),
        cost=(20 * voxels, 0, 1024),
    )(far_wide, trans, emit)

    others = [swap(pair, "beam", r) for r in range(1, n_beam)]
    if others:
        others[-1], fluor, rest = lax.optimization_barrier((others[-1], fluor, rest))
    total, up, further = call(
        merge_body, (plain(1, *wide), plain(*wide), plain(*wide)), (VMEM,) * 3, (VMEM,) * n_beam,
        cost=(1 << 15, 1 << 13, 1024),
    )(pair, *others)

    if n_slab == 4 and n_beam > 1:
        even = swap(total, "slab", 1)
        odd = lax.ppermute(total, ("beam", "slab"), odd_pairs(n_beam, n_slab))
        near_lines = [total, even, odd]
        near_slabs = [0, 1, None]
        half = jnp.concatenate([total, even], axis=0)
        lines = [total, even, swap(half, "slab", 2)]
    else:
        lines = [total] + [swap(total, "slab", r) for r in range(1, n_slab)]
        near_slabs = [r for r in range(n_slab) if r & (r + 1) == 0]
        near_lines = [lines[r] for r in near_slabs]

    pixels = fan_offset.shape[0]
    gram, pull, fan_turned = call(
        functools.partial(fan_body, scale_sum, near_slabs), (plain(depth, depth * len(near_slabs)), plain(*wide), plain(pixels, depth * n_slab)),
        (VMEM,) * 3, (VMEM,) * 4, cost=(8 * depth * measured.size, 0, 4 * measured.size),
    )(fan_offset[None, :], fan_weight.T, measured, total)

    near, column_total, gain, shift = call(
        functools.partial(back_body, scale_sum),
        (plane, plain(depth, rows), plain(*wide), plain(n_species, depth, width)),
        (VMEM,) * 4,
        (VMEM,) * (5 + len(near_lines)),
        cost=(10 * voxels, 0, 1024),
    )(fixed, gram, pull, up, further, fluor, *near_lines[1:])

    nearer = beyond(column_total, "det", True)

    scale_line = scale_y * LN2 / scale_x
    mixed = call(
        mix_body, (VMEM(turned, F32),), (VMEM,), (VMEM,) * 4,
        cost=(40 * voxels, 0, 1024),
    )(fixed, gain, shift, rest)[0]

    share = pixels // (n_beam * n_slab)
    return tuple(
        call(
            functools.partial(finish_body, scale_sum, scale_line, n_det),
            (plain(*conc.shape), plain(n_energy, share, width)),
            (HBM, HBM),
            (VMEM,) * (6 + len(lines)),
            [
                VMEM(turned, F32),
                VMEM((n_energy, share, width), F32),
                pltpu.SemaphoreType.DMA((rows // CHUNK + 2,)),
                pltpu.SemaphoreType.DMA,
            ],
            limit=16,
            cost=(10 * voxels, 0, 16 * voxels),
        )(fixed, nearer, near, mixed, fan_turned, measured, *lines)
    )


def solution(mesh):
    in_specs = (P(None, "slab", "beam", "det"), P(), P(), P(), P(), P(), P(None, None, "det"))
    out_specs = (P(None, "slab", "beam", "det"), P(None, ("beam", "slab"), "det"))
    return jax.shard_map(shards, mesh=mesh, in_specs=in_specs, out_specs=out_specs, check_vma=False)
```

```python
import functools
import math

import jax
import jax.numpy as jnp
from jax import lax
from jax.experimental import pallas as pl
from jax.experimental.pallas import tpu as pltpu
from jax.sharding import PartitionSpec as P


VMEM, SMEM, HBM = pltpu.VMEM, pltpu.SMEM, pltpu.HBM
F32, BF16 = jnp.float32, jnp.bfloat16
LANES = 128
CHUNK = 32
STEP = 16
LN2 = math.log(2.0)
LOG2E = 1.0 / LN2


def call(body, out_shape, out_spaces, in_spaces, scratch=(), limit=8, cost=None):
    flops, exps, size = cost
    return pl.pallas_call(
        body,
        out_shape=out_shape,
        in_specs=[pl.BlockSpec(memory_space=s) for s in in_spaces],
        out_specs=[pl.BlockSpec(memory_space=s) for s in out_spaces],
        scratch_shapes=list(scratch),
        compiler_params=pltpu.CompilerParams(vmem_limit_bytes=limit << 20),
        cost_estimate=pl.CostEstimate(flops=flops, transcendentals=exps, bytes_accessed=size),
    )


def plain(*shape):
    return jax.ShapeDtypeStruct(shape, F32)


def split(value):
    high = value.astype(BF16)
    low = (value - high.astype(F32)).astype(BF16)
    return jnp.concatenate([high, low], axis=1)


def lane_sums(width, beyond):
    row = lax.broadcasted_iota(jnp.int32, (width, 2 * width), 0)
    col = lax.broadcasted_iota(jnp.int32, (width, 2 * width), 1)
    part = (row > col) if beyond else (row < col)
    ones = jnp.where(part | (col >= width), 1.0, 0.0).astype(BF16)
    return jnp.concatenate([ones, ones], axis=0)


def selected(cross_ref, index_ref):
    n_energy = index_ref.shape[0]
    columns = [index_ref[e] for e in range(n_energy)]
    return [[cross_ref[s, columns[e]] for e in range(n_energy)] for s in range(cross_ref.shape[0])]


def planes(plane_ref, n_species, n_energy):
    cross = [[plane_ref[s * n_energy + e] for e in range(n_energy)] for s in range(n_species)]
    return cross, [plane_ref[n_species * n_energy + s] for s in range(n_species)]


def weighted(weights, values):
    total = weights[0] * values[0]
    for weight, value in zip(weights[1:], values[1:]):
        total = total + weight * value
    return total


def load_body(
    scale, scale_x, line_hbm, cross_hbm, index_hbm, conc_hbm, conc_ref, emit_ref, beyond_ref, total_ref, plane_ref,
    line_ref, cross_ref, index_ref, small_sems, sems,
):
    n_species, depth, rows, width = conc_hbm.shape
    n_early = emit_ref.shape[0]
    ends = list(range(CHUNK, rows, CHUNK)) + [rows - CHUNK // 2, rows]
    starts = [0] + ends[:-1]

    def copies(chunk):
        span = pl.ds(starts[chunk], ends[chunk] - starts[chunk])
        return [
            pltpu.make_async_copy(conc_hbm.at[:, z, span, :], conc_ref.at[:, span, z, :], sems.at[chunk])
            for z in range(depth)
        ]

    small = [
        pltpu.make_async_copy(source, target, small_sems.at[i])
        for i, (source, target) in enumerate(
            [(line_hbm, line_ref), (cross_hbm, cross_ref), (index_hbm, index_ref)]
        )
    ]
    for copy in small:
        copy.start()
    for chunk in range(len(ends)):
        for copy in copies(chunk):
            copy.start()
    table = lane_sums(width, True)
    lane = lax.broadcasted_iota(jnp.int32, (depth, LANES), 1)
    for copy in small:
        copy.wait()
    line = [line_ref[s] * scale for s in range(n_species)]
    sigma = selected(cross_ref, index_ref)
    scalars = [v for row in sigma for v in row] + [line_ref[s] for s in range(n_species)]
    for i, value in enumerate(scalars):
        plane_ref[i] = jnp.full((depth, width), value)
    sigma = [[v * scale_x for v in row] for row in sigma]
    total = jnp.zeros((depth, LANES), F32)
    for chunk, (start, end) in enumerate(zip(starts, ends)):
        for copy in copies(chunk):
            copy.wait()
        absorber = []
        for x in range(start, end):
            conc = [conc_ref[s, x] for s in range(n_species)]
            absorber.append(weighted(line, conc))
            for e in range(n_early):
                emit_ref[e, x] = weighted([sigma[s][e] for s in range(n_species)], conc)
        sums = jnp.dot(split(jnp.concatenate(absorber, axis=0)), table, preferred_element_type=F32)
        for q, x in enumerate(range(start, end)):
            here = sums[q * depth : (q + 1) * depth]
            beyond_ref[x] = here[:, :width]
            total = jnp.where(lane == x % LANES, here[:, width : width + LANES], total)
        if end % LANES == 0:
            total_ref[:, end - LANES : end] = total


def local_body(scale, plane_ref, conc_ref, early_ref, beyond_ref, trans_ref, emit_ref, depth_ref):
    n_energy, rows, depth, width = trans_ref.shape
    n_species, n_early = conc_ref.shape[0], early_ref.shape[0]
    sigma = [[v * scale for v in row] for row in planes(plane_ref, n_species, n_energy)[0]]

    def step(block, path):
        path = list(path)
        for q in range(STEP):
            x = block * STEP + q
            beyond = beyond_ref[x]
            conc = [conc_ref[s, x] for s in range(n_species)]
            for e in range(n_energy):
                if e < n_early:
                    emission = early_ref[e, x]
                else:
                    emission = weighted([sigma[s][e] for s in range(n_species)], conc)
                trans = jnp.exp2(path[e] + beyond)
                trans_ref[e, x] = trans
                emit_ref[e, x] = emission * trans
                path[e] = path[e] + emission
        return tuple(path)

    zero = jnp.zeros((depth, width), F32)
    path = lax.fori_loop(0, rows // STEP, step, (zero,) * n_energy)
    for e in range(n_energy):
        depth_ref[e] = path[e]


def reached(axis, count, backward):
    if count != 2:
        return True
    return lax.axis_index(axis) == (1 if backward else 0)


def columns(source_ref, change, width):
    depth, rows = source_ref.shape
    for part in range(rows // LANES):
        held = change(source_ref[:, part * LANES : (part + 1) * LANES])
        for q in range(LANES):
            yield part * LANES + q, jnp.broadcast_to(held[:, q : q + 1], (depth, width))


def line_body(count, far_ref, emit_ref, depth_ref, far_out, pair_ref):
    n_energy, _, _, width = emit_ref.shape
    keep = jnp.where(reached("det", count, False), 1.0, 0.0)
    sums = [[None, None] for _ in range(n_energy)]
    for x, factor in columns(far_ref, lambda v: jnp.exp2(v * keep), width):
        far_out[x] = factor
        for e in range(n_energy):
            value = factor * emit_ref[e, x]
            sums[e][x % 2] = value if x < 2 else sums[e][x % 2] + value
    for e in range(n_energy):
        pair_ref[0, e] = depth_ref[e]
        pair_ref[1, e] = sums[e][0] + sums[e][1]


def merge_body(*refs):
    pairs, (total_ref, up_ref, further_ref) = refs[:-3], refs[-3:]
    beam = lax.axis_index("beam")
    state = [(ref[0], ref[1]) for ref in pairs]
    up, further = jnp.zeros_like(state[0][0]), jnp.zeros_like(state[0][0])
    distance = 1
    while len(state) > 1:
        lower = (beam & distance) == 0
        merged = []
        for i in range(0, len(state), 2):
            (span, sums), (other_span, other_sums) = state[i], state[i + 1]
            fade = jnp.exp2(jnp.where(lower, span, other_span))
            late = fade * jnp.where(lower, other_sums, sums)
            if i == 0:
                further = jnp.where(lower, further + late, fade * further)
                up = jnp.where(lower, up, up + other_span)
            merged.append((span + other_span, jnp.where(lower, sums, other_sums) + late))
        state = merged
        distance *= 2
    total_ref[0] = state[0][1]
    up_ref[...] = up
    further_ref[...] = further


def ahead_body(far_ref, trans_ref, emit_ref, fluor_ref, rest_ref):
    n_energy, rows, depth, width = emit_ref.shape

    def step(block, ahead):
        ahead = list(ahead)
        for q in range(STEP):
            x = rows - 1 - (block * STEP + q)
            far = far_ref[x]
            for e in range(n_energy):
                fluor = far * emit_ref[e, x]
                fluor_ref[e, x] = fluor
                rest_ref[e, x] = far * trans_ref[e, x] + ahead[e]
                ahead[e] = ahead[e] + LN2 * fluor
        return tuple(ahead)

    zero = jnp.zeros((depth, width), F32)
    lax.fori_loop(0, rows // STEP, step, (zero,) * n_energy)


def fan_body(scale, near_slabs, offset_ref, weight_ref, measured_ref, own_ref, gram_ref, pull_ref, turned_ref):
    depth, n_slab = gram_ref.shape[0], turned_ref.shape[1] // gram_ref.shape[0]
    taps, pixels = weight_ref.shape
    own = lax.axis_index("slab")
    offset = jnp.broadcast_to(offset_ref[...], (depth, pixels))
    level = lax.broadcasted_iota(jnp.int32, (depth, pixels), 0) - offset
    taps = [jnp.broadcast_to(weight_ref[j : j + 1, :], (depth, pixels)).astype(F32) for j in range(taps)]

    def block(slab):
        place = level + slab * depth
        found = jnp.zeros((depth, pixels), F32)
        for j, tap in enumerate(taps):
            found = found + jnp.where(place == j, tap, 0.0)
        return found

    blocks = [block(own ^ r) for r in range(n_slab)]
    turned_ref[...] = jnp.concatenate(blocks, axis=0).T
    odd = own + jnp.where((own & 1) == 1, 1, -1)
    near = jnp.concatenate([block(odd) if r is None else blocks[r] for r in near_slabs], axis=0)
    gram = lax.dot_general(
        blocks[0].astype(BF16), near.astype(BF16), (((1,), (1,)), ((), ())), preferred_element_type=F32
    )
    gram_ref[...] = gram
    n_energy, _, width = pull_ref.shape
    sums = weigh(gram, [(0, own_ref, 0)], depth, n_energy, width)
    for e in range(n_energy):
        pull_ref[e] = sums[e] * scale - jnp.dot(
            blocks[0], measured_ref[e], precision=lax.Precision.HIGHEST, preferred_element_type=F32
        )


def weigh(weights, lines, depth, n_energy, width):
    height = weights.shape[0]
    sums = [[None, None] for _ in range(n_energy)]
    for order, (r, lines_ref, i) in enumerate(lines):
        for z in range(depth):
            place = r * depth + z
            weight = jnp.broadcast_to(weights[:, place : place + 1], (height, width))
            for e in range(n_energy):
                value = weight * lines_ref[i, e, z : z + 1, :]
                sums[e][z % 2] = value if order == 0 and z < 2 else sums[e][z % 2] + value
    return [a + b for a, b in sums]


def back_body(scale, count, plane_ref, gram_ref, pull_ref, up_ref, further_ref, fluor_ref, *refs):
    lines, (near_ref, total_ref, gain_ref, shift_ref) = refs[:-4], refs[-4:]
    n_energy, _, depth, width = fluor_ref.shape
    n_species = shift_ref.shape[0]
    sums = weigh(gram_ref[...], [(r + 1, ref, 0) for r, ref in enumerate(lines)], depth, n_energy, width)
    back = [sums[e] * scale + pull_ref[e] for e in range(n_energy)]
    gain = [back[e] * jnp.exp2(up_ref[e]) for e in range(n_energy)]
    sigma, _ = planes(plane_ref, n_species, n_energy)
    pushed = [LN2 * back[e] * further_ref[e] for e in range(n_energy)]
    for e in range(n_energy):
        gain_ref[e] = gain[e]
    for s in range(n_species):
        shift_ref[s] = weighted(sigma[s], pushed)
    last = lax.axis_index("det") == count - 1

    @pl.when(jnp.logical_not(last))
    def _():
        column_sums(gain, fluor_ref, near_ref, total_ref)

    @pl.when(last)
    def _():
        total_ref[...] = jnp.zeros_like(total_ref)


def column_sums(gain, fluor_ref, near_ref, total_ref):
    n_energy, rows, depth, width = fluor_ref.shape
    table = lane_sums(width, False)
    lane = lax.broadcasted_iota(jnp.int32, (depth, LANES), 1)
    total = jnp.zeros((depth, LANES), F32)
    for start in range(0, rows, CHUNK):
        span = range(start, start + CHUNK)
        heavy = [weighted(gain, [fluor_ref[e, x] for e in range(n_energy)]) for x in span]
        found = jnp.dot(split(jnp.concatenate(heavy, axis=0)), table, preferred_element_type=F32)
        for q, x in enumerate(span):
            here = found[q * depth : (q + 1) * depth]
            near_ref[x] = here[:, :width]
            if total_ref is not None:
                total = jnp.where(lane == x % LANES, here[:, width : width + LANES], total)
        if total_ref is not None and (start + CHUNK) % LANES == 0:
            total_ref[:, start + CHUNK - LANES : start + CHUNK] = total


def mix_body(count, plane_ref, gain_ref, shift_ref, rest_ref, fluor_ref, out_ref, near_ref):
    n_energy, rows, _, _ = rest_ref.shape
    n_species = out_ref.shape[0]
    sigma, _ = planes(plane_ref, n_species, n_energy)
    mixed = [[sigma[s][e] * gain_ref[e] for e in range(n_energy)] for s in range(n_species)]
    shift = [shift_ref[s] for s in range(n_species)]

    def step(block, carry):
        for q in range(STEP):
            x = block * STEP + q
            rest = [rest_ref[e, x] for e in range(n_energy)]
            for s in range(n_species):
                out_ref[s, x] = weighted(mixed[s], rest) + shift[s]
        return carry

    lax.fori_loop(0, rows // STEP, step, 0)

    @pl.when(lax.axis_index("det") == count - 1)
    def _():
        column_sums([gain_ref[e] for e in range(n_energy)], fluor_ref, near_ref, None)


def finish_body(
    scale, scale_line, count, plane_ref, nearer_ref, near_ref, last_ref, mix_ref, fan_ref, measured_ref, *refs
):
    lines, (grad_hbm, residual_hbm, grad_ref, residual_ref, sems, residual_sem) = refs[:-6], refs[-6:]
    n_species, rows, depth, width = mix_ref.shape
    n_energy, share, _ = residual_ref.shape
    line = [v * scale_line for v in planes(plane_ref, n_species, n_energy)[1]]
    keep = jnp.where(reached("det", count, True), 1.0, 0.0)
    last = lax.axis_index("det") == count - 1

    ends = [8, 16] + list(range(CHUNK, rows + 1, CHUNK))

    def copies(chunk):
        first = ends[chunk - 1] if chunk else 0
        span = pl.ds(first, ends[chunk] - first)
        return [
            pltpu.make_async_copy(grad_ref.at[:, span, z, :], grad_hbm.at[:, z, span, :], sems.at[chunk])
            for z in range(depth)
        ]

    for x, column in columns(nearer_ref, lambda v: v * keep, width):
        before = jnp.where(last, last_ref[x], near_ref[x]) + column
        for s in range(n_species):
            grad_ref[s, x] = mix_ref[s, x] + line[s] * before
        if x + 1 in ends:
            for copy in copies(ends.index(x + 1)):
                copy.start()

    start = pl.multiple_of(lax.axis_index(("beam", "slab")) * share, share)
    pieces = [(ref, i) for ref in lines for i in range(ref.shape[0])]
    pieces = [(r, ref, i) for r, (ref, i) in enumerate(pieces)]
    sums = weigh(fan_ref[pl.ds(start, share), :], pieces, depth, n_energy, width)
    for e in range(n_energy):
        residual_ref[e] = sums[e] * scale - measured_ref[e, pl.ds(start, share), :]
    copy = pltpu.make_async_copy(residual_ref, residual_hbm, residual_sem)
    copy.start()

    for chunk in range(len(ends)):
        for done in copies(chunk):
            done.wait()
    copy.wait()


def odd_pairs(n_beam, n_slab):
    pairs = []
    for beam in range(n_beam):
        for slab in range(n_slab):
            other = slab + 1 if slab % 2 else slab - 1
            if 0 <= other < n_slab:
                target = beam * n_slab + other
            else:
                target = (beam ^ 1) * n_slab + slab
            pairs.append((beam * n_slab + slab, target))
    return pairs


def swap(value, axis, distance):
    return lax.ppermute(value, axis, [(i, i ^ distance) for i in range(lax.axis_size(axis))])


def beyond(value, axis, backward):
    count = lax.axis_size(axis)
    if count == 2:
        return swap(value, axis, 1)
    mine = lax.axis_index(axis)
    pieces = lax.all_gather(value, axis)
    places = jnp.arange(count)
    keep = (places < mine) if backward else (places > mine)
    return jnp.sum(jnp.where(keep.reshape((-1,) + (1,) * value.ndim), pieces, 0.0), axis=0)


def shards(conc, cross, line, index, fan_offset, fan_weight, measured):
    n_species, depth, rows, width = conc.shape
    n_energy = index.shape[0]
    n_beam, n_det, n_slab = (lax.axis_size(a) for a in ("beam", "det", "slab"))
    assert n_beam & (n_beam - 1) == 0 and n_slab & (n_slab - 1) == 0
    assert fan_weight.shape[1] <= depth + 1
    assert rows % LANES == 0 and width % LANES == 0 and depth % 8 == 0
    full_x, full_y = rows * n_beam, width * n_det
    scale_x = -(1.5 / full_x) * LOG2E
    scale_y = -(1.5 / full_y) * LOG2E
    scale_sum = 1.0 / (scale_x * full_x)
    voxels = depth * rows * width
    turned = (n_species, rows, depth, width)
    cube = VMEM((n_energy, rows, depth, width), F32)
    plane = VMEM((rows, depth, width), F32)

    n_early = (n_energy + 3) // 4
    conc_x, emission, far_local, row_total, fixed = call(
        functools.partial(load_body, scale_y, scale_x),
        (VMEM(turned, F32), VMEM((n_early, rows, depth, width), F32), plane, plain(depth, rows),
         VMEM((n_species * n_energy + n_species, depth, width), F32)),
        (VMEM,) * 5,
        (HBM,) * 4,
        [
            SMEM(line.shape, F32),
            SMEM(cross.shape, F32),
            SMEM(index.shape, index.dtype),
            pltpu.SemaphoreType.DMA((3,)),
            pltpu.SemaphoreType.DMA((rows // CHUNK + 1,)),
        ],
        cost=(40 * voxels, 0, 16 * voxels),
    )(*(pltpu.with_memory_space_constraint(v, HBM) for v in (line, cross, index, conc)))

    far = beyond(row_total, "det", False)

    trans, emit, own_depth = call(
        functools.partial(local_body, scale_x),
        (cube, cube, plain(n_energy, depth, width)),
        (VMEM, VMEM, VMEM),
        (VMEM,) * 4,
        cost=(20 * voxels, 4 * voxels, 1024),
    )(fixed, conc_x, emission, far_local)

    wide = (n_energy, depth, width)
    far_wide, pair = call(
        functools.partial(line_body, n_det), (plane, plain(2, *wide)), (VMEM,) * 2, (VMEM,) * 3,
        cost=(8 * voxels, 0, 1024),
    )(far, emit, own_depth)

    fluor, rest = call(
        ahead_body, (cube, cube), (VMEM, VMEM), (VMEM, VMEM, VMEM),
        cost=(20 * voxels, 0, 1024),
    )(far_wide, trans, emit)

    others = [swap(pair, "beam", r) for r in range(1, n_beam)]
    if others:
        others[-1], fluor, rest = lax.optimization_barrier((others[-1], fluor, rest))
    total, up, further = call(
        merge_body, (plain(1, *wide), plain(*wide), plain(*wide)), (VMEM,) * 3, (VMEM,) * n_beam,
        cost=(1 << 15, 1 << 13, 1024),
    )(pair, *others)

    if n_slab == 4 and n_beam > 1:
        even = swap(total, "slab", 1)
        odd = lax.ppermute(total, ("beam", "slab"), odd_pairs(n_beam, n_slab))
        near_lines = [total, even, odd]
        near_slabs = [0, 1, None]
        half = jnp.concatenate([total, even], axis=0)
        lines = [total, even, swap(half, "slab", 2)]
    else:
        lines = [total] + [swap(total, "slab", r) for r in range(1, n_slab)]
        near_slabs = [r for r in range(n_slab) if r & (r + 1) == 0]
        near_lines = [lines[r] for r in near_slabs]

    pixels = fan_offset.shape[0]
    gram, pull, fan_turned = call(
        functools.partial(fan_body, scale_sum, near_slabs), (plain(depth, depth * len(near_slabs)), plain(*wide), plain(pixels, depth * n_slab)),
        (VMEM,) * 3, (VMEM,) * 4, cost=(8 * depth * measured.size, 0, 4 * measured.size),
    )(fan_offset[None, :], fan_weight.T, measured, total)

    near, column_total, gain, shift = call(
        functools.partial(back_body, scale_sum, n_det),
        (plane, plain(depth, rows), plain(*wide), plain(n_species, depth, width)),
        (VMEM,) * 4,
        (VMEM,) * (5 + len(near_lines)),
        cost=(10 * voxels, 0, 1024),
    )(fixed, gram, pull, up, further, fluor, *near_lines[1:])

    nearer = beyond(column_total, "det", True)

    scale_line = scale_y * LN2 / scale_x
    mixed, near_last = call(
        functools.partial(mix_body, n_det), (VMEM(turned, F32), plane), (VMEM,) * 2, (VMEM,) * 5,
        cost=(40 * voxels, 0, 1024),
    )(fixed, gain, shift, rest, fluor)

    share = pixels // (n_beam * n_slab)
    return tuple(
        call(
            functools.partial(finish_body, scale_sum, scale_line, n_det),
            (plain(*conc.shape), plain(n_energy, share, width)),
            (HBM, HBM),
            (VMEM,) * (7 + len(lines)),
            [
                VMEM(turned, F32),
                VMEM((n_energy, share, width), F32),
                pltpu.SemaphoreType.DMA((rows // CHUNK + 2,)),
                pltpu.SemaphoreType.DMA,
            ],
            limit=16,
            cost=(10 * voxels, 0, 16 * voxels),
        )(fixed, nearer, near, near_last, mixed, fan_turned, measured, *lines)
    )


def solution(mesh):
    in_specs = (P(None, "slab", "beam", "det"), P(), P(), P(), P(), P(), P(None, None, "det"))
    out_specs = (P(None, "slab", "beam", "det"), P(None, ("beam", "slab"), "det"))
    return jax.shard_map(shards, mesh=mesh, in_specs=in_specs, out_specs=out_specs, check_vma=False)
```

```python
import functools
import math

import jax
import jax.numpy as jnp
from jax import lax
from jax.experimental import pallas as pl
from jax.experimental.pallas import tpu as pltpu
from jax.sharding import PartitionSpec as P


VMEM, SMEM, HBM = pltpu.VMEM, pltpu.SMEM, pltpu.HBM
F32, BF16 = jnp.float32, jnp.bfloat16
LANES = 128
CHUNK = 32
STEP = 16
LN2 = math.log(2.0)
LOG2E = 1.0 / LN2


def call(body, out_shape, out_spaces, in_spaces, scratch=(), limit=8, cost=None, aliases=None):
    flops, exps, size = cost
    return pl.pallas_call(
        body,
        out_shape=out_shape,
        in_specs=[pl.BlockSpec(memory_space=s) for s in in_spaces],
        out_specs=[pl.BlockSpec(memory_space=s) for s in out_spaces],
        scratch_shapes=list(scratch),
        input_output_aliases=aliases or {},
        compiler_params=pltpu.CompilerParams(vmem_limit_bytes=limit << 20),
        cost_estimate=pl.CostEstimate(flops=flops, transcendentals=exps, bytes_accessed=size),
    )


def plain(*shape):
    return jax.ShapeDtypeStruct(shape, F32)


def split(value):
    high = value.astype(BF16)
    low = (value - high.astype(F32)).astype(BF16)
    return jnp.concatenate([high, low], axis=1)


def lane_sums(width, beyond):
    row = lax.broadcasted_iota(jnp.int32, (width, 2 * width), 0)
    col = lax.broadcasted_iota(jnp.int32, (width, 2 * width), 1)
    part = (row > col) if beyond else (row < col)
    ones = jnp.where(part | (col >= width), 1.0, 0.0).astype(BF16)
    return jnp.concatenate([ones, ones], axis=0)


def selected(cross_ref, index_ref):
    n_energy = index_ref.shape[0]
    columns = [index_ref[e] for e in range(n_energy)]
    return [[cross_ref[s, columns[e]] for e in range(n_energy)] for s in range(cross_ref.shape[0])]


def planes(plane_ref, n_species, n_energy):
    cross = [[plane_ref[s * n_energy + e] for e in range(n_energy)] for s in range(n_species)]
    return cross, [plane_ref[n_species * n_energy + s] for s in range(n_species)]


def weighted(weights, values):
    total = weights[0] * values[0]
    for weight, value in zip(weights[1:], values[1:]):
        total = total + weight * value
    return total


def load_body(
    scale, scale_x, line_hbm, cross_hbm, index_hbm, conc_hbm, conc_ref, emit_ref, beyond_ref, total_ref, plane_ref,
    line_ref, cross_ref, index_ref, small_sems, sems,
):
    n_species, depth, rows, width = conc_hbm.shape
    n_early = emit_ref.shape[0]
    ends = list(range(CHUNK, rows, CHUNK)) + [rows - CHUNK // 2, rows]
    starts = [0] + ends[:-1]

    def copies(chunk):
        span = pl.ds(starts[chunk], ends[chunk] - starts[chunk])
        return [
            pltpu.make_async_copy(conc_hbm.at[:, z, span, :], conc_ref.at[:, span, z, :], sems.at[chunk])
            for z in range(depth)
        ]

    small = [
        pltpu.make_async_copy(source, target, small_sems.at[i])
        for i, (source, target) in enumerate(
            [(line_hbm, line_ref), (cross_hbm, cross_ref), (index_hbm, index_ref)]
        )
    ]
    for copy in small:
        copy.start()
    for chunk in range(len(ends)):
        for copy in copies(chunk):
            copy.start()
    table = lane_sums(width, True)
    lane = lax.broadcasted_iota(jnp.int32, (depth, LANES), 1)
    for copy in small:
        copy.wait()
    line = [line_ref[s] * scale for s in range(n_species)]
    sigma = selected(cross_ref, index_ref)
    scalars = [v for row in sigma for v in row] + [line_ref[s] for s in range(n_species)]
    for i, value in enumerate(scalars):
        plane_ref[i] = jnp.full((depth, width), value)
    sigma = [[v * scale_x for v in row] for row in sigma]
    total = jnp.zeros((depth, LANES), F32)
    for chunk, (start, end) in enumerate(zip(starts, ends)):
        for copy in copies(chunk):
            copy.wait()
        absorber = []
        for x in range(start, end):
            conc = [conc_ref[s, x] for s in range(n_species)]
            absorber.append(weighted(line, conc))
            for e in range(n_early):
                emit_ref[e, x] = weighted([sigma[s][e] for s in range(n_species)], conc)
        sums = jnp.dot(split(jnp.concatenate(absorber, axis=0)), table, preferred_element_type=F32)
        for q, x in enumerate(range(start, end)):
            here = sums[q * depth : (q + 1) * depth]
            beyond_ref[x] = here[:, :width]
            total = jnp.where(lane == x % LANES, here[:, width : width + LANES], total)
        if end % LANES == 0:
            total_ref[:, end - LANES : end] = total


def local_body(scale, plane_ref, conc_ref, early_ref, beyond_ref, trans_ref, emit_ref, pair_ref):
    n_energy, rows, depth, width = trans_ref.shape
    n_species, n_early = conc_ref.shape[0], early_ref.shape[0]
    sigma = [[v * scale for v in row] for row in planes(plane_ref, n_species, n_energy)[0]]

    def step(block, carry):
        path, sums = list(carry[:n_energy]), list(carry[n_energy:])
        for q in range(STEP):
            x = block * STEP + q
            beyond = beyond_ref[x]
            conc = [conc_ref[s, x] for s in range(n_species)]
            for e in range(n_energy):
                if e < n_early:
                    emission = early_ref[e, x]
                else:
                    emission = weighted([sigma[s][e] for s in range(n_species)], conc)
                trans = jnp.exp2(path[e] + beyond)
                trans_ref[e, x] = trans
                emit = emission * trans
                emit_ref[e, x] = emit
                path[e] = path[e] + emission
                sums[e] = sums[e] + emit
        return tuple(path + sums)

    zero = jnp.zeros((depth, width), F32)
    carry = lax.fori_loop(0, rows // STEP, step, (zero,) * (2 * n_energy))
    for e in range(n_energy):
        pair_ref[0, e] = carry[e]
        pair_ref[1, e] = carry[n_energy + e]


def columns(source_ref, change, width):
    depth, rows = source_ref.shape
    for part in range(rows // LANES):
        held = change(source_ref[:, part * LANES : (part + 1) * LANES])
        for q in range(LANES):
            yield part * LANES + q, jnp.broadcast_to(held[:, q : q + 1], (depth, width))


def line_body(count, far_ref, emit_ref, local_ref, far_out, pair_ref):
    n_energy, _, _, width = emit_ref.shape
    last = lax.axis_index("det") == count - 1

    @pl.when(last)
    def _():
        pair_ref[...] = local_ref[...]

    @pl.when(jnp.logical_not(last))
    def _():
        sums = [[None, None] for _ in range(n_energy)]
        for x, factor in columns(far_ref, jnp.exp2, width):
            far_out[x] = factor
            for e in range(n_energy):
                value = factor * emit_ref[e, x]
                sums[e][x % 2] = value if x < 2 else sums[e][x % 2] + value
        for e in range(n_energy):
            pair_ref[0, e] = local_ref[0, e]
            pair_ref[1, e] = sums[e][0] + sums[e][1]


def merge_body(*refs):
    pairs, (total_ref, up_ref, further_ref) = refs[:-3], refs[-3:]
    beam = lax.axis_index("beam")
    state = [(ref[0], ref[1]) for ref in pairs]
    up, further = jnp.zeros_like(state[0][0]), jnp.zeros_like(state[0][0])
    distance = 1
    while len(state) > 1:
        lower = (beam & distance) == 0
        merged = []
        for i in range(0, len(state), 2):
            (span, sums), (other_span, other_sums) = state[i], state[i + 1]
            fade = jnp.exp2(jnp.where(lower, span, other_span))
            late = fade * jnp.where(lower, other_sums, sums)
            if i == 0:
                further = jnp.where(lower, further + late, fade * further)
                up = jnp.where(lower, up, up + other_span)
            merged.append((span + other_span, jnp.where(lower, sums, other_sums) + late))
        state = merged
        distance *= 2
    total_ref[0] = state[0][1]
    up_ref[...] = up
    further_ref[...] = further


def ahead_body(count, far_ref, trans_ref, emit_ref, fluor_ref, rest_ref):
    n_energy, rows, depth, width = emit_ref.shape

    last = lax.axis_index("det") == count - 1

    def step(block, ahead):
        ahead = list(ahead)
        for q in range(STEP):
            x = rows - 1 - (block * STEP + q)
            far = jnp.where(last, 1.0, far_ref[x])
            for e in range(n_energy):
                fluor = far * emit_ref[e, x]
                fluor_ref[e, x] = fluor
                rest_ref[e, x] = far * trans_ref[e, x] + ahead[e]
                ahead[e] = ahead[e] + LN2 * fluor
        return tuple(ahead)

    zero = jnp.zeros((depth, width), F32)
    lax.fori_loop(0, rows // STEP, step, (zero,) * n_energy)


def fan_body(scale, near_slabs, offset_ref, weight_ref, measured_ref, own_ref, gram_ref, pull_ref, turned_ref):
    depth, n_slab = gram_ref.shape[0], turned_ref.shape[1] // gram_ref.shape[0]
    taps, pixels = weight_ref.shape
    own = lax.axis_index("slab")
    offset = jnp.broadcast_to(offset_ref[...], (depth, pixels))
    level = lax.broadcasted_iota(jnp.int32, (depth, pixels), 0) - offset
    taps = [jnp.broadcast_to(weight_ref[j : j + 1, :], (depth, pixels)).astype(F32) for j in range(taps)]

    def block(slab):
        place = level + slab * depth
        found = jnp.zeros((depth, pixels), F32)
        for j, tap in enumerate(taps):
            found = found + jnp.where(place == j, tap, 0.0)
        return found

    blocks = [block(own ^ r) for r in range(n_slab)]
    turned_ref[...] = jnp.concatenate(blocks, axis=0).T
    odd = own + jnp.where((own & 1) == 1, 1, -1)
    near = jnp.concatenate([block(odd) if r is None else blocks[r] for r in near_slabs], axis=0)
    gram = lax.dot_general(
        blocks[0].astype(BF16), near.astype(BF16), (((1,), (1,)), ((), ())), preferred_element_type=F32
    )
    gram_ref[...] = gram
    n_energy, _, width = pull_ref.shape
    sums = weigh(gram, [(0, own_ref, 0)], depth, n_energy, width)
    for e in range(n_energy):
        pull_ref[e] = sums[e] * scale - jnp.dot(
            blocks[0], measured_ref[e], precision=lax.Precision.HIGHEST, preferred_element_type=F32
        )


def weigh(weights, lines, depth, n_energy, width):
    height = weights.shape[0]
    sums = [[None, None] for _ in range(n_energy)]
    for order, (r, lines_ref, i) in enumerate(lines):
        for z in range(depth):
            place = r * depth + z
            weight = jnp.broadcast_to(weights[:, place : place + 1], (height, width))
            for e in range(n_energy):
                value = weight * lines_ref[i, e, z : z + 1, :]
                sums[e][z % 2] = value if order == 0 and z < 2 else sums[e][z % 2] + value
    return [a + b for a, b in sums]


def back_body(scale, count, plane_ref, gram_ref, pull_ref, up_ref, further_ref, fluor_ref, *refs):
    lines, (near_ref, total_ref, gain_ref, shift_ref) = refs[:-4], refs[-4:]
    n_energy, _, depth, width = fluor_ref.shape
    n_species = shift_ref.shape[0]
    sums = weigh(gram_ref[...], [(r + 1, ref, 0) for r, ref in enumerate(lines)], depth, n_energy, width)
    back = [sums[e] * scale + pull_ref[e] for e in range(n_energy)]
    gain = [back[e] * jnp.exp2(up_ref[e]) for e in range(n_energy)]
    sigma, _ = planes(plane_ref, n_species, n_energy)
    pushed = [LN2 * back[e] * further_ref[e] for e in range(n_energy)]
    for e in range(n_energy):
        gain_ref[e] = gain[e]
    for s in range(n_species):
        shift_ref[s] = weighted(sigma[s], pushed)
    last = jnp.logical_and(lax.axis_index("det") == count - 1, count > 1)

    @pl.when(jnp.logical_not(last))
    def _():
        column_sums(gain, fluor_ref, near_ref, total_ref)

    @pl.when(last)
    def _():
        total_ref[...] = jnp.zeros_like(total_ref)


def column_sums(gain, fluor_ref, near_ref, total_ref):
    n_energy, rows, depth, width = fluor_ref.shape
    table = lane_sums(width, False)
    lane = lax.broadcasted_iota(jnp.int32, (depth, LANES), 1)
    total = jnp.zeros((depth, LANES), F32)
    for start in range(0, rows, CHUNK):
        span = range(start, start + CHUNK)
        heavy = [weighted(gain, [fluor_ref[e, x] for e in range(n_energy)]) for x in span]
        found = jnp.dot(split(jnp.concatenate(heavy, axis=0)), table, preferred_element_type=F32)
        for q, x in enumerate(span):
            here = found[q * depth : (q + 1) * depth]
            near_ref[x] = here[:, :width]
            if total_ref is not None:
                total = jnp.where(lane == x % LANES, here[:, width : width + LANES], total)
        if total_ref is not None and (start + CHUNK) % LANES == 0:
            total_ref[:, start + CHUNK - LANES : start + CHUNK] = total


def out_copies(source_ref, out_hbm, sems, ends, chunk):
    start = ends[chunk - 1] if chunk else 0
    span = pl.ds(start, ends[chunk] - start)
    return [
        pltpu.make_async_copy(source_ref.at[:, span, z, :], out_hbm.at[:, z, span, :], sems.at[chunk])
        for z in range(out_hbm.shape[1])
    ]


def out_ends(rows):
    return [8, 16] + list(range(CHUNK, rows + 1, CHUNK))


def mix_body(
    scale_line, count, plane_ref, gain_ref, shift_ref, rest_ref, fluor_ref, near_ref,
    out_ref, last_ref, grad_hbm, sems,
):
    n_energy, rows, _, _ = rest_ref.shape
    n_species = out_ref.shape[0]
    sigma, line = planes(plane_ref, n_species, n_energy)
    mixed = [[sigma[s][e] * gain_ref[e] for e in range(n_energy)] for s in range(n_species)]
    shift = [shift_ref[s] for s in range(n_species)]
    place = lax.axis_index("det")

    @pl.when(place == 0)
    def _():
        ends = out_ends(rows)
        scaled = [v * scale_line for v in line]
        for x in range(rows):
            rest = [rest_ref[e, x] for e in range(n_energy)]
            before = near_ref[x]
            for s in range(n_species):
                out_ref[s, x] = weighted(mixed[s], rest) + (shift[s] + scaled[s] * before)
            if x + 1 in ends:
                for copy in out_copies(out_ref, grad_hbm, sems, ends, ends.index(x + 1)):
                    copy.start()
        for chunk in range(len(ends)):
            for copy in out_copies(out_ref, grad_hbm, sems, ends, chunk):
                copy.wait()

    @pl.when(place != 0)
    def _():
        def step(block, carry):
            for q in range(STEP):
                x = block * STEP + q
                rest = [rest_ref[e, x] for e in range(n_energy)]
                for s in range(n_species):
                    out_ref[s, x] = weighted(mixed[s], rest) + shift[s]
            return carry

        lax.fori_loop(0, rows // STEP, step, 0)

    if count > 1:

        @pl.when(place == count - 1)
        def _():
            column_sums([gain_ref[e] for e in range(n_energy)], fluor_ref, last_ref, None)


def finish_body(
    scale, scale_line, count, plane_ref, nearer_ref, near_ref, last_ref, mix_ref, fan_ref, measured_ref, grad_in, *refs
):
    lines, (grad_hbm, residual_hbm, grad_ref, residual_ref, sems, residual_sem) = refs[:-6], refs[-6:]
    n_species, rows, depth, width = mix_ref.shape
    n_energy, share, _ = residual_ref.shape
    place = lax.axis_index("det")
    ends = out_ends(rows)

    @pl.when(place != 0)
    def _():
        line = [v * scale_line for v in planes(plane_ref, n_species, n_energy)[1]]
        last = place == count - 1
        for x, column in columns(nearer_ref, lambda v: v, width):
            before = jnp.where(last, last_ref[x], near_ref[x]) + column
            for s in range(n_species):
                grad_ref[s, x] = mix_ref[s, x] + line[s] * before
            if x + 1 in ends:
                for copy in out_copies(grad_ref, grad_hbm, sems, ends, ends.index(x + 1)):
                    copy.start()

    start = pl.multiple_of(lax.axis_index(("beam", "slab")) * share, share)
    pieces = [(ref, i) for ref in lines for i in range(ref.shape[0])]
    pieces = [(r, ref, i) for r, (ref, i) in enumerate(pieces)]
    sums = weigh(fan_ref[pl.ds(start, share), :], pieces, depth, n_energy, width)
    for e in range(n_energy):
        residual_ref[e] = sums[e] * scale - measured_ref[e, pl.ds(start, share), :]
    copy = pltpu.make_async_copy(residual_ref, residual_hbm, residual_sem)
    copy.start()

    @pl.when(place != 0)
    def _():
        for chunk in range(len(ends)):
            for done in out_copies(grad_ref, grad_hbm, sems, ends, chunk):
                done.wait()

    copy.wait()


def odd_pairs(n_beam, n_slab):
    pairs = []
    for beam in range(n_beam):
        for slab in range(n_slab):
            other = slab + 1 if slab % 2 else slab - 1
            if 0 <= other < n_slab:
                target = beam * n_slab + other
            else:
                target = (beam ^ 1) * n_slab + slab
            pairs.append((beam * n_slab + slab, target))
    return pairs


def swap(value, axis, distance):
    return lax.ppermute(value, axis, [(i, i ^ distance) for i in range(lax.axis_size(axis))])


def beyond(value, axis, backward):
    count = lax.axis_size(axis)
    if count == 2:
        return swap(value, axis, 1)
    mine = lax.axis_index(axis)
    pieces = lax.all_gather(value, axis)
    places = jnp.arange(count)
    keep = (places < mine) if backward else (places > mine)
    return jnp.sum(jnp.where(keep.reshape((-1,) + (1,) * value.ndim), pieces, 0.0), axis=0)


def shards(conc, cross, line, index, fan_offset, fan_weight, measured):
    n_species, depth, rows, width = conc.shape
    n_energy = index.shape[0]
    n_beam, n_det, n_slab = (lax.axis_size(a) for a in ("beam", "det", "slab"))
    assert n_beam & (n_beam - 1) == 0 and n_slab & (n_slab - 1) == 0
    assert fan_weight.shape[1] <= depth + 1
    assert rows % LANES == 0 and width % LANES == 0 and depth % 8 == 0
    full_x, full_y = rows * n_beam, width * n_det
    scale_x = -(1.5 / full_x) * LOG2E
    scale_y = -(1.5 / full_y) * LOG2E
    scale_sum = 1.0 / (scale_x * full_x)
    voxels = depth * rows * width
    turned = (n_species, rows, depth, width)
    cube = VMEM((n_energy, rows, depth, width), F32)
    plane = VMEM((rows, depth, width), F32)

    n_early = (n_energy + 3) // 4
    conc_x, emission, far_local, row_total, fixed = call(
        functools.partial(load_body, scale_y, scale_x),
        (VMEM(turned, F32), VMEM((n_early, rows, depth, width), F32), plane, plain(depth, rows),
         VMEM((n_species * n_energy + n_species, depth, width), F32)),
        (VMEM,) * 5,
        (HBM,) * 4,
        [
            SMEM(line.shape, F32),
            SMEM(cross.shape, F32),
            SMEM(index.shape, index.dtype),
            pltpu.SemaphoreType.DMA((3,)),
            pltpu.SemaphoreType.DMA((rows // CHUNK + 1,)),
        ],
        cost=(40 * voxels, 0, 16 * voxels),
    )(*(pltpu.with_memory_space_constraint(v, HBM) for v in (line, cross, index, conc)))

    far = beyond(row_total, "det", False)

    trans, emit, local_pair = call(
        functools.partial(local_body, scale_x),
        (cube, cube, plain(2, n_energy, depth, width)),
        (VMEM, VMEM, VMEM),
        (VMEM,) * 4,
        cost=(20 * voxels, 4 * voxels, 1024),
    )(fixed, conc_x, emission, far_local)

    wide = (n_energy, depth, width)
    far_wide, pair = call(
        functools.partial(line_body, n_det), (plane, plain(2, *wide)), (VMEM,) * 2, (VMEM,) * 3,
        cost=(8 * voxels, 0, 1024),
    )(far, emit, local_pair)

    fluor, rest = call(
        functools.partial(ahead_body, n_det), (cube, cube), (VMEM, VMEM), (VMEM, VMEM, VMEM),
        cost=(20 * voxels, 0, 1024),
    )(far_wide, trans, emit)

    others = []
    for r in range(1, n_beam):
        others.append(swap(pair, "beam", r))
    if others:
        others[-1], fluor, rest = lax.optimization_barrier((others[-1], fluor, rest))
    total, up, further = call(
        merge_body, (plain(1, *wide), plain(*wide), plain(*wide)), (VMEM,) * 3, (VMEM,) * n_beam,
        cost=(1 << 15, 1 << 13, 1024),
    )(pair, *others)

    if n_slab == 4 and n_beam > 1:
        even = swap(total, "slab", 1)
        odd = lax.ppermute(total, ("beam", "slab"), odd_pairs(n_beam, n_slab))
        near_lines = [total, even, odd]
        near_slabs = [0, 1, None]
        half = jnp.concatenate([total, even], axis=0)
        lines = [total, even, swap(half, "slab", 2)]
    else:
        lines = [total] + [swap(total, "slab", r) for r in range(1, n_slab)]
        near_slabs = [r for r in range(n_slab) if r & (r + 1) == 0]
        near_lines = [lines[r] for r in near_slabs]

    pixels = fan_offset.shape[0]
    gram, pull, fan_turned = call(
        functools.partial(fan_body, scale_sum, near_slabs), (plain(depth, depth * len(near_slabs)), plain(*wide), plain(pixels, depth * n_slab)),
        (VMEM,) * 3, (VMEM,) * 4, cost=(8 * depth * measured.size, 0, 4 * measured.size),
    )(fan_offset[None, :], fan_weight.T, measured, total)

    near, column_total, gain, shift = call(
        functools.partial(back_body, scale_sum, n_det),
        (plane, plain(depth, rows), plain(*wide), plain(n_species, depth, width)),
        (VMEM,) * 4,
        (VMEM,) * (5 + len(near_lines)),
        cost=(10 * voxels, 0, 1024),
    )(fixed, gram, pull, up, further, fluor, *near_lines[1:])

    nearer = beyond(column_total, "det", True)

    scale_line = scale_y * LN2 / scale_x
    out_sems = pltpu.SemaphoreType.DMA((len(out_ends(rows)),))
    mixed, near_last, grad = call(
        functools.partial(mix_body, scale_line, n_det),
        (VMEM(turned, F32), plane, HBM(conc.shape, F32)),
        (VMEM, VMEM, HBM),
        (VMEM,) * 6,
        [out_sems],
        cost=(40 * voxels, 0, 1024),
    )(fixed, gain, shift, rest, fluor, near)

    share = pixels // (n_beam * n_slab)
    return tuple(
        call(
            functools.partial(finish_body, scale_sum, scale_line, n_det),
            (plain(*conc.shape), plain(n_energy, share, width)),
            (HBM, HBM),
            (VMEM,) * 7 + (HBM,) + (VMEM,) * len(lines),
            [VMEM(turned, F32), VMEM((n_energy, share, width), F32), out_sems, pltpu.SemaphoreType.DMA],
            limit=16,
            cost=(10 * voxels, 0, 16 * voxels),
            aliases={7: 0},
        )(fixed, nearer, near, near_last, mixed, fan_turned, measured, grad, *lines)
    )


def solution(mesh):
    in_specs = (P(None, "slab", "beam", "det"), P(), P(), P(), P(), P(), P(None, None, "det"))
    out_specs = (P(None, "slab", "beam", "det"), P(None, ("beam", "slab"), "det"))
    return jax.shard_map(shards, mesh=mesh, in_specs=in_specs, out_specs=out_specs, check_vma=False)
```

```python
import functools
import math

import jax
import jax.numpy as jnp
from jax import lax
from jax.experimental import pallas as pl
from jax.experimental.pallas import tpu as pltpu
from jax.sharding import PartitionSpec as P


VMEM, SMEM, HBM = pltpu.VMEM, pltpu.SMEM, pltpu.HBM
F32, BF16 = jnp.float32, jnp.bfloat16
LANES = 128
CHUNK = 32
STEP = 16
LN2 = math.log(2.0)
LOG2E = 1.0 / LN2


def call(body, out_shape, out_spaces, in_spaces, scratch=(), limit=8, cost=None, aliases=None):
    flops, exps, size = cost
    return pl.pallas_call(
        body,
        out_shape=out_shape,
        in_specs=[pl.BlockSpec(memory_space=s) for s in in_spaces],
        out_specs=[pl.BlockSpec(memory_space=s) for s in out_spaces],
        scratch_shapes=list(scratch),
        input_output_aliases=aliases or {},
        compiler_params=pltpu.CompilerParams(vmem_limit_bytes=limit << 20),
        cost_estimate=pl.CostEstimate(flops=flops, transcendentals=exps, bytes_accessed=size),
    )


def plain(*shape):
    return jax.ShapeDtypeStruct(shape, F32)


def split(value):
    high = value.astype(BF16)
    low = (value - high.astype(F32)).astype(BF16)
    return jnp.concatenate([high, low], axis=1)


def lane_sums(width, beyond):
    row = lax.broadcasted_iota(jnp.int32, (width, 2 * width), 0)
    col = lax.broadcasted_iota(jnp.int32, (width, 2 * width), 1)
    part = (row > col) if beyond else (row < col)
    ones = jnp.where(part | (col >= width), 1.0, 0.0).astype(BF16)
    return jnp.concatenate([ones, ones], axis=0)


def selected(cross_ref, index_ref):
    n_energy = index_ref.shape[0]
    columns = [index_ref[e] for e in range(n_energy)]
    return [[cross_ref[s, columns[e]] for e in range(n_energy)] for s in range(cross_ref.shape[0])]


def planes(plane_ref, n_species, n_energy):
    cross = [[plane_ref[s * n_energy + e] for e in range(n_energy)] for s in range(n_species)]
    return cross, [plane_ref[n_species * n_energy + s] for s in range(n_species)]


def weighted(weights, values):
    total = weights[0] * values[0]
    for weight, value in zip(weights[1:], values[1:]):
        total = total + weight * value
    return total


def in_ends(rows):
    return [rows * part // 16 for part in (6, 10, 13, 15, 16)]


def load_body(
    scale, scale_x, line_hbm, cross_hbm, index_hbm, conc_hbm, conc_ref, emit_ref, beyond_ref, total_ref, plane_ref,
    line_ref, cross_ref, index_ref, small_sems, sems,
):
    n_species, depth, rows, width = conc_hbm.shape
    n_early = emit_ref.shape[0]
    ends = in_ends(rows)
    starts = [0] + ends[:-1]
    spans = [pl.ds(start, end - start) for start, end in zip(starts, ends)]

    small = [
        pltpu.make_async_copy(source, target, small_sems.at[i])
        for i, (source, target) in enumerate(
            [(line_hbm, line_ref), (cross_hbm, cross_ref), (index_hbm, index_ref)]
        )
    ]
    for copy in small:
        copy.start()
    for chunk, span in enumerate(spans):
        for z in range(depth):
            pltpu.make_async_copy(
                conc_hbm.at[:, z, span, :], conc_ref.at[:, span, z, :], sems.at[chunk]
            ).start()
    table = lane_sums(width, True)
    lane = lax.broadcasted_iota(jnp.int32, (depth, LANES), 1)
    for copy in small:
        copy.wait()
    line = [line_ref[s] * scale for s in range(n_species)]
    sigma = selected(cross_ref, index_ref)
    scalars = [v for row in sigma for v in row] + [line_ref[s] for s in range(n_species)]
    for i, value in enumerate(scalars):
        plane_ref[i] = jnp.full((depth, width), value)
    sigma = [[v * scale_x for v in row] for row in sigma]
    total = jnp.zeros((depth, LANES), F32)
    for chunk, (start, end) in enumerate(zip(starts, ends)):
        whole = conc_ref.at[:, spans[chunk]]
        pltpu.make_async_copy(whole, whole, sems.at[chunk]).wait()
        absorber = []
        for x in range(start, end):
            conc = [conc_ref[s, x] for s in range(n_species)]
            absorber.append(weighted(line, conc))
            for e in range(n_early):
                emit_ref[e, x] = weighted([sigma[s][e] for s in range(n_species)], conc)
        sums = jnp.dot(split(jnp.concatenate(absorber, axis=0)), table, preferred_element_type=F32)
        for q, x in enumerate(range(start, end)):
            here = sums[q * depth : (q + 1) * depth]
            beyond_ref[x] = here[:, :width]
            total = jnp.where(lane == x % LANES, here[:, width : width + LANES], total)
            if (x + 1) % LANES == 0:
                total_ref[:, x + 1 - LANES : x + 1] = total


def local_body(scale, plane_ref, conc_ref, early_ref, beyond_ref, trans_ref, emit_ref, pair_ref):
    n_energy, rows, depth, width = trans_ref.shape
    n_species, n_early = conc_ref.shape[0], early_ref.shape[0]
    sigma = [[v * scale for v in row] for row in planes(plane_ref, n_species, n_energy)[0]]

    def step(block, carry):
        path, sums = list(carry[:n_energy]), list(carry[n_energy:])
        for q in range(STEP):
            x = block * STEP + q
            beyond = beyond_ref[x]
            conc = [conc_ref[s, x] for s in range(n_species)]
            for e in range(n_energy):
                if e < n_early:
                    emission = early_ref[e, x]
                else:
                    emission = weighted([sigma[s][e] for s in range(n_species)], conc)
                trans = jnp.exp2(path[e] + beyond)
                trans_ref[e, x] = trans
                emit = emission * trans
                emit_ref[e, x] = emit
                path[e] = path[e] + emission
                sums[e] = sums[e] + emit
        return tuple(path + sums)

    zero = jnp.zeros((depth, width), F32)
    carry = lax.fori_loop(0, rows // STEP, step, (zero,) * (2 * n_energy))
    for e in range(n_energy):
        pair_ref[0, e] = carry[e]
        pair_ref[1, e] = carry[n_energy + e]


def columns(source_ref, change, width):
    depth, rows = source_ref.shape
    for part in range(rows // LANES):
        held = change(source_ref[:, part * LANES : (part + 1) * LANES])
        for q in range(LANES):
            yield part * LANES + q, jnp.broadcast_to(held[:, q : q + 1], (depth, width))


def line_body(count, far_ref, emit_ref, local_ref, far_out, pair_ref):
    n_energy, _, _, width = emit_ref.shape
    last = lax.axis_index("det") == count - 1

    @pl.when(last)
    def _():
        pair_ref[...] = local_ref[...]

    @pl.when(jnp.logical_not(last))
    def _():
        sums = [[None, None] for _ in range(n_energy)]
        for x, factor in columns(far_ref, jnp.exp2, width):
            far_out[x] = factor
            for e in range(n_energy):
                value = factor * emit_ref[e, x]
                sums[e][x % 2] = value if x < 2 else sums[e][x % 2] + value
        for e in range(n_energy):
            pair_ref[0, e] = local_ref[0, e]
            pair_ref[1, e] = sums[e][0] + sums[e][1]


def merge_body(*refs):
    pairs, (total_ref, up_ref, further_ref) = refs[:-3], refs[-3:]
    beam = lax.axis_index("beam")
    state = [(ref[0], ref[1]) for ref in pairs]
    up, further = jnp.zeros_like(state[0][0]), jnp.zeros_like(state[0][0])
    distance = 1
    while len(state) > 1:
        lower = (beam & distance) == 0
        merged = []
        for i in range(0, len(state), 2):
            (span, sums), (other_span, other_sums) = state[i], state[i + 1]
            fade = jnp.exp2(jnp.where(lower, span, other_span))
            late = fade * jnp.where(lower, other_sums, sums)
            if i == 0:
                further = jnp.where(lower, further + late, fade * further)
                up = jnp.where(lower, up, up + other_span)
            merged.append((span + other_span, jnp.where(lower, sums, other_sums) + late))
        state = merged
        distance *= 2
    total_ref[0] = state[0][1]
    up_ref[...] = up
    further_ref[...] = further


def ahead_body(count, far_ref, trans_ref, emit_ref, fluor_ref, rest_ref):
    n_energy, rows, depth, width = emit_ref.shape

    last = lax.axis_index("det") == count - 1

    def step(block, ahead):
        ahead = list(ahead)
        for q in range(STEP):
            x = rows - 1 - (block * STEP + q)
            far = jnp.where(last, 1.0, far_ref[x])
            for e in range(n_energy):
                fluor = far * emit_ref[e, x]
                fluor_ref[e, x] = fluor
                rest_ref[e, x] = far * trans_ref[e, x] + ahead[e]
                ahead[e] = ahead[e] + LN2 * fluor
        return tuple(ahead)

    zero = jnp.zeros((depth, width), F32)
    lax.fori_loop(0, rows // STEP, step, (zero,) * n_energy)


def fan_body(scale, near_slabs, offset_ref, weight_ref, measured_ref, own_ref, gram_ref, pull_ref, turned_ref):
    depth, n_slab = gram_ref.shape[0], turned_ref.shape[1] // gram_ref.shape[0]
    taps, pixels = weight_ref.shape
    own = lax.axis_index("slab")
    offset = jnp.broadcast_to(offset_ref[...], (depth, pixels))
    level = lax.broadcasted_iota(jnp.int32, (depth, pixels), 0) - offset
    taps = [jnp.broadcast_to(weight_ref[j : j + 1, :], (depth, pixels)).astype(F32) for j in range(taps)]

    def block(slab):
        place = level + slab * depth
        found = jnp.zeros((depth, pixels), F32)
        for j, tap in enumerate(taps):
            found = found + jnp.where(place == j, tap, 0.0)
        return found

    blocks = [block(own ^ r) for r in range(n_slab)]
    turned_ref[...] = jnp.concatenate(blocks, axis=0).T
    odd = own + jnp.where((own & 1) == 1, 1, -1)
    near = jnp.concatenate([block(odd) if r is None else blocks[r] for r in near_slabs], axis=0)
    gram = lax.dot_general(
        blocks[0].astype(BF16), near.astype(BF16), (((1,), (1,)), ((), ())), preferred_element_type=F32
    )
    gram_ref[...] = gram
    n_energy, _, width = pull_ref.shape
    sums = weigh(gram, [(0, own_ref, 0)], depth, n_energy, width)
    for e in range(n_energy):
        pull_ref[e] = sums[e] * scale - jnp.dot(
            blocks[0], measured_ref[e], precision=lax.Precision.HIGHEST, preferred_element_type=F32
        )


def weigh(weights, lines, depth, n_energy, width):
    height = weights.shape[0]
    sums = [[None, None] for _ in range(n_energy)]
    for order, (r, lines_ref, i) in enumerate(lines):
        for z in range(depth):
            place = r * depth + z
            weight = jnp.broadcast_to(weights[:, place : place + 1], (height, width))
            for e in range(n_energy):
                value = weight * lines_ref[i, e, z : z + 1, :]
                sums[e][z % 2] = value if order == 0 and z < 2 else sums[e][z % 2] + value
    return [a + b for a, b in sums]


def back_body(scale, count, plane_ref, gram_ref, pull_ref, up_ref, further_ref, fluor_ref, *refs):
    lines, (near_ref, total_ref, gain_ref, shift_ref) = refs[:-4], refs[-4:]
    n_energy, _, depth, width = fluor_ref.shape
    n_species = shift_ref.shape[0]
    sums = weigh(gram_ref[...], [(r + 1, ref, 0) for r, ref in enumerate(lines)], depth, n_energy, width)
    back = [sums[e] * scale + pull_ref[e] for e in range(n_energy)]
    gain = [back[e] * jnp.exp2(up_ref[e]) for e in range(n_energy)]
    sigma, _ = planes(plane_ref, n_species, n_energy)
    pushed = [LN2 * back[e] * further_ref[e] for e in range(n_energy)]
    for e in range(n_energy):
        gain_ref[e] = gain[e]
    for s in range(n_species):
        shift_ref[s] = weighted(sigma[s], pushed)
    last = jnp.logical_and(lax.axis_index("det") == count - 1, count > 1)

    @pl.when(jnp.logical_not(last))
    def _():
        column_sums(gain, fluor_ref, near_ref, total_ref)

    @pl.when(last)
    def _():
        total_ref[...] = jnp.zeros_like(total_ref)


def column_sums(gain, fluor_ref, near_ref, total_ref):
    n_energy, rows, depth, width = fluor_ref.shape
    table = lane_sums(width, False)
    lane = lax.broadcasted_iota(jnp.int32, (depth, LANES), 1)
    total = jnp.zeros((depth, LANES), F32)
    for start in range(0, rows, CHUNK):
        span = range(start, start + CHUNK)
        heavy = [weighted(gain, [fluor_ref[e, x] for e in range(n_energy)]) for x in span]
        found = jnp.dot(split(jnp.concatenate(heavy, axis=0)), table, preferred_element_type=F32)
        for q, x in enumerate(span):
            here = found[q * depth : (q + 1) * depth]
            near_ref[x] = here[:, :width]
            if total_ref is not None:
                total = jnp.where(lane == x % LANES, here[:, width : width + LANES], total)
        if total_ref is not None and (start + CHUNK) % LANES == 0:
            total_ref[:, start + CHUNK - LANES : start + CHUNK] = total


def out_copies(source_ref, out_hbm, sems, ends, chunk):
    start = ends[chunk - 1] if chunk else 0
    span = pl.ds(start, ends[chunk] - start)
    return [
        pltpu.make_async_copy(source_ref.at[:, span, z, :], out_hbm.at[:, z, span, :], sems.at[chunk])
        for z in range(out_hbm.shape[1])
    ]


def out_wait(source_ref, sems, ends, chunk):
    start = ends[chunk - 1] if chunk else 0
    whole = source_ref.at[:, pl.ds(start, ends[chunk] - start)]
    pltpu.make_async_copy(whole, whole, sems.at[chunk]).wait()


def out_ends(rows):
    return [rows * part // 16 for part in (1, 4, 8, 12, 16)]


def mix_body(
    scale_line, count, plane_ref, gain_ref, shift_ref, rest_ref, fluor_ref, near_ref,
    out_ref, last_ref, grad_hbm, sems,
):
    n_energy, rows, _, _ = rest_ref.shape
    n_species = out_ref.shape[0]
    sigma, line = planes(plane_ref, n_species, n_energy)
    mixed = [[sigma[s][e] * gain_ref[e] for e in range(n_energy)] for s in range(n_species)]
    shift = [shift_ref[s] for s in range(n_species)]
    place = lax.axis_index("det")

    @pl.when(place == 0)
    def _():
        ends = out_ends(rows)
        scaled = [v * scale_line for v in line]
        for x in range(rows):
            rest = [rest_ref[e, x] for e in range(n_energy)]
            before = near_ref[x]
            for s in range(n_species):
                out_ref[s, x] = weighted(mixed[s], rest) + (shift[s] + scaled[s] * before)
            if x + 1 in ends:
                for copy in out_copies(out_ref, grad_hbm, sems, ends, ends.index(x + 1)):
                    copy.start()
        for chunk in range(len(ends)):
            out_wait(out_ref, sems, ends, chunk)

    @pl.when(place != 0)
    def _():
        def step(block, carry):
            for q in range(STEP):
                x = block * STEP + q
                rest = [rest_ref[e, x] for e in range(n_energy)]
                for s in range(n_species):
                    out_ref[s, x] = weighted(mixed[s], rest) + shift[s]
            return carry

        lax.fori_loop(0, rows // STEP, step, 0)

    if count > 1:

        @pl.when(place == count - 1)
        def _():
            column_sums([gain_ref[e] for e in range(n_energy)], fluor_ref, last_ref, None)


def finish_body(
    scale, scale_line, count, plane_ref, nearer_ref, near_ref, last_ref, mix_ref, fan_ref, measured_ref, grad_in, *refs
):
    lines, (grad_hbm, residual_hbm, grad_ref, residual_ref, sems, residual_sem) = refs[:-6], refs[-6:]
    n_species, rows, depth, width = mix_ref.shape
    n_energy, share, _ = residual_ref.shape
    place = lax.axis_index("det")
    ends = out_ends(rows)

    @pl.when(place != 0)
    def _():
        line = [v * scale_line for v in planes(plane_ref, n_species, n_energy)[1]]
        last = place == count - 1
        for x, column in columns(nearer_ref, lambda v: v, width):
            before = jnp.where(last, last_ref[x], near_ref[x]) + column
            for s in range(n_species):
                grad_ref[s, x] = mix_ref[s, x] + line[s] * before
            if x + 1 in ends:
                for copy in out_copies(grad_ref, grad_hbm, sems, ends, ends.index(x + 1)):
                    copy.start()

    start = pl.multiple_of(lax.axis_index(("beam", "slab")) * share, share)
    pieces = [(ref, i) for ref in lines for i in range(ref.shape[0])]
    pieces = [(r, ref, i) for r, (ref, i) in enumerate(pieces)]
    sums = weigh(fan_ref[pl.ds(start, share), :], pieces, depth, n_energy, width)
    for e in range(n_energy):
        residual_ref[e] = sums[e] * scale - measured_ref[e, pl.ds(start, share), :]
    copy = pltpu.make_async_copy(residual_ref, residual_hbm, residual_sem)
    copy.start()

    @pl.when(place != 0)
    def _():
        for chunk in range(len(ends)):
            out_wait(grad_ref, sems, ends, chunk)

    copy.wait()


def odd_pairs(n_beam, n_slab):
    pairs = []
    for beam in range(n_beam):
        for slab in range(n_slab):
            other = slab + 1 if slab % 2 else slab - 1
            if 0 <= other < n_slab:
                target = beam * n_slab + other
            else:
                target = (beam ^ 1) * n_slab + slab
            pairs.append((beam * n_slab + slab, target))
    return pairs


def swap(value, axis, distance):
    return lax.ppermute(value, axis, [(i, i ^ distance) for i in range(lax.axis_size(axis))])


def beyond(value, axis, backward):
    count = lax.axis_size(axis)
    if count == 2:
        return swap(value, axis, 1)
    mine = lax.axis_index(axis)
    pieces = lax.all_gather(value, axis)
    places = jnp.arange(count)
    keep = (places < mine) if backward else (places > mine)
    return jnp.sum(jnp.where(keep.reshape((-1,) + (1,) * value.ndim), pieces, 0.0), axis=0)


def shards(conc, cross, line, index, fan_offset, fan_weight, measured):
    n_species, depth, rows, width = conc.shape
    n_energy = index.shape[0]
    n_beam, n_det, n_slab = (lax.axis_size(a) for a in ("beam", "det", "slab"))
    assert n_beam & (n_beam - 1) == 0 and n_slab & (n_slab - 1) == 0
    assert fan_weight.shape[1] <= depth + 1
    assert rows % LANES == 0 and width % LANES == 0 and depth % 8 == 0
    full_x, full_y = rows * n_beam, width * n_det
    scale_x = -(1.5 / full_x) * LOG2E
    scale_y = -(1.5 / full_y) * LOG2E
    scale_sum = 1.0 / (scale_x * full_x)
    voxels = depth * rows * width
    turned = (n_species, rows, depth, width)
    cube = VMEM((n_energy, rows, depth, width), F32)
    plane = VMEM((rows, depth, width), F32)

    n_early = (n_energy + 3) // 4
    conc_x, emission, far_local, row_total, fixed = call(
        functools.partial(load_body, scale_y, scale_x),
        (VMEM(turned, F32), VMEM((n_early, rows, depth, width), F32), plane, plain(depth, rows),
         VMEM((n_species * n_energy + n_species, depth, width), F32)),
        (VMEM,) * 5,
        (HBM,) * 4,
        [
            SMEM(line.shape, F32),
            SMEM(cross.shape, F32),
            SMEM(index.shape, index.dtype),
            pltpu.SemaphoreType.DMA((3,)),
            pltpu.SemaphoreType.DMA((len(in_ends(rows)),)),
        ],
        cost=(40 * voxels, 0, 16 * voxels),
    )(*(pltpu.with_memory_space_constraint(v, HBM) for v in (line, cross, index, conc)))

    far = beyond(row_total, "det", False)

    trans, emit, local_pair = call(
        functools.partial(local_body, scale_x),
        (cube, cube, plain(2, n_energy, depth, width)),
        (VMEM, VMEM, VMEM),
        (VMEM,) * 4,
        cost=(20 * voxels, 4 * voxels, 1024),
    )(fixed, conc_x, emission, far_local)

    wide = (n_energy, depth, width)
    far_wide, pair = call(
        functools.partial(line_body, n_det), (plane, plain(2, *wide)), (VMEM,) * 2, (VMEM,) * 3,
        cost=(8 * voxels, 0, 1024),
    )(far, emit, local_pair)

    fluor, rest = call(
        functools.partial(ahead_body, n_det), (cube, cube), (VMEM, VMEM), (VMEM, VMEM, VMEM),
        cost=(20 * voxels, 0, 1024),
    )(far_wide, trans, emit)

    others = []
    for r in range(1, n_beam):
        others.append(swap(pair, "beam", r))
    if others:
        others[-1], fluor, rest = lax.optimization_barrier((others[-1], fluor, rest))
    total, up, further = call(
        merge_body, (plain(1, *wide), plain(*wide), plain(*wide)), (VMEM,) * 3, (VMEM,) * n_beam,
        cost=(1 << 15, 1 << 13, 1024),
    )(pair, *others)

    if n_slab == 4 and n_beam > 1:
        even = swap(total, "slab", 1)
        odd = lax.ppermute(total, ("beam", "slab"), odd_pairs(n_beam, n_slab))
        near_lines = [total, even, odd]
        near_slabs = [0, 1, None]
        half = jnp.concatenate([total, even], axis=0)
        lines = [total, even, swap(half, "slab", 2)]
    else:
        lines = [total] + [swap(total, "slab", r) for r in range(1, n_slab)]
        near_slabs = [r for r in range(n_slab) if r & (r + 1) == 0]
        near_lines = [lines[r] for r in near_slabs]

    pixels = fan_offset.shape[0]
    gram, pull, fan_turned = call(
        functools.partial(fan_body, scale_sum, near_slabs), (plain(depth, depth * len(near_slabs)), plain(*wide), plain(pixels, depth * n_slab)),
        (VMEM,) * 3, (VMEM,) * 4, cost=(8 * depth * measured.size, 0, 4 * measured.size),
    )(fan_offset[None, :], fan_weight.T, measured, total)

    near, column_total, gain, shift = call(
        functools.partial(back_body, scale_sum, n_det),
        (plane, plain(depth, rows), plain(*wide), plain(n_species, depth, width)),
        (VMEM,) * 4,
        (VMEM,) * (5 + len(near_lines)),
        cost=(10 * voxels, 0, 1024),
    )(fixed, gram, pull, up, further, fluor, *near_lines[1:])

    nearer = beyond(column_total, "det", True)

    scale_line = scale_y * LN2 / scale_x
    out_sems = pltpu.SemaphoreType.DMA((len(out_ends(rows)),))
    mixed, near_last, grad = call(
        functools.partial(mix_body, scale_line, n_det),
        (VMEM(turned, F32), plane, HBM(conc.shape, F32)),
        (VMEM, VMEM, HBM),
        (VMEM,) * 6,
        [out_sems],
        cost=(40 * voxels, 0, 1024),
    )(fixed, gain, shift, rest, fluor, near)

    share = pixels // (n_beam * n_slab)
    return tuple(
        call(
            functools.partial(finish_body, scale_sum, scale_line, n_det),
            (plain(*conc.shape), plain(n_energy, share, width)),
            (HBM, HBM),
            (VMEM,) * 7 + (HBM,) + (VMEM,) * len(lines),
            [VMEM(turned, F32), VMEM((n_energy, share, width), F32), out_sems, pltpu.SemaphoreType.DMA],
            limit=16,
            cost=(10 * voxels, 0, 16 * voxels),
            aliases={7: 0},
        )(fixed, nearer, near, near_last, mixed, fan_turned, measured, grad, *lines)
    )


def solution(mesh):
    in_specs = (P(None, "slab", "beam", "det"), P(), P(), P(), P(), P(), P(None, None, "det"))
    out_specs = (P(None, "slab", "beam", "det"), P(None, ("beam", "slab"), "det"))
    return jax.shard_map(shards, mesh=mesh, in_specs=in_specs, out_specs=out_specs, check_vma=False)
```

```python
import functools
import math

import jax
import jax.numpy as jnp
from jax import lax
from jax.experimental import pallas as pl
from jax.experimental.pallas import tpu as pltpu
from jax.sharding import PartitionSpec as P


VMEM, SMEM, HBM = pltpu.VMEM, pltpu.SMEM, pltpu.HBM
F32, BF16 = jnp.float32, jnp.bfloat16
LANES = 128
CHUNK = 32
STEP = 16
LN2 = math.log(2.0)
LOG2E = 1.0 / LN2


def call(body, out_shape, out_spaces, in_spaces, scratch=(), limit=8, cost=None, aliases=None):
    flops, exps, size = cost
    return pl.pallas_call(
        body,
        out_shape=out_shape,
        in_specs=[pl.BlockSpec(memory_space=s) for s in in_spaces],
        out_specs=[pl.BlockSpec(memory_space=s) for s in out_spaces],
        scratch_shapes=list(scratch),
        input_output_aliases=aliases or {},
        compiler_params=pltpu.CompilerParams(vmem_limit_bytes=limit << 20),
        cost_estimate=pl.CostEstimate(flops=flops, transcendentals=exps, bytes_accessed=size),
    )


def plain(*shape):
    return jax.ShapeDtypeStruct(shape, F32)


def split(value):
    high = value.astype(BF16)
    low = (value - high.astype(F32)).astype(BF16)
    return jnp.concatenate([high, low], axis=1)


def lane_sums(width, beyond):
    row = lax.broadcasted_iota(jnp.int32, (width, 2 * width), 0)
    col = lax.broadcasted_iota(jnp.int32, (width, 2 * width), 1)
    part = (row > col) if beyond else (row < col)
    ones = jnp.where(part | (col >= width), 1.0, 0.0).astype(BF16)
    return jnp.concatenate([ones, ones], axis=0)


def selected(cross_ref, index_ref):
    n_energy = index_ref.shape[0]
    columns = [index_ref[e] for e in range(n_energy)]
    return [[cross_ref[s, columns[e]] for e in range(n_energy)] for s in range(cross_ref.shape[0])]


def planes(plane_ref, n_species, n_energy):
    cross = [[plane_ref[s * n_energy + e] for e in range(n_energy)] for s in range(n_species)]
    return cross, [plane_ref[n_species * n_energy + s] for s in range(n_species)]


def weighted(weights, values):
    total = weights[0] * values[0]
    for weight, value in zip(weights[1:], values[1:]):
        total = total + weight * value
    return total


def in_ends(rows):
    return [rows * part // 16 for part in (4, 8, 12, 16)]


def load_body(
    scale, scale_x, line_hbm, cross_hbm, index_hbm, conc_hbm, conc_ref, emit_ref, beyond_ref, total_ref, plane_ref,
    line_ref, cross_ref, index_ref, small_sems, sems,
):
    n_species, depth, rows, width = conc_hbm.shape
    n_early = emit_ref.shape[0]
    ends = in_ends(rows)
    starts = [0] + ends[:-1]
    spans = [pl.ds(start, end - start) for start, end in zip(starts, ends)]

    small = [
        pltpu.make_async_copy(source, target, small_sems.at[i])
        for i, (source, target) in enumerate(
            [(line_hbm, line_ref), (cross_hbm, cross_ref), (index_hbm, index_ref)]
        )
    ]
    for copy in small:
        copy.start()
    for chunk, span in enumerate(spans):
        for z in range(depth):
            pltpu.make_async_copy(
                conc_hbm.at[:, z, span, :], conc_ref.at[:, span, z, :], sems.at[chunk]
            ).start()
    table = lane_sums(width, True)
    lane = lax.broadcasted_iota(jnp.int32, (depth, LANES), 1)
    for copy in small:
        copy.wait()
    line = [line_ref[s] * scale for s in range(n_species)]
    sigma = selected(cross_ref, index_ref)
    scalars = [v for row in sigma for v in row] + [line_ref[s] for s in range(n_species)]
    for i, value in enumerate(scalars):
        plane_ref[i] = jnp.full((depth, width), value)
    sigma = [[v * scale_x for v in row] for row in sigma]
    total = jnp.zeros((depth, LANES), F32)
    for chunk, (start, end) in enumerate(zip(starts, ends)):
        whole = conc_ref.at[:, spans[chunk]]
        pltpu.make_async_copy(whole, whole, sems.at[chunk]).wait()
        absorber = []
        for x in range(start, end):
            conc = [conc_ref[s, x] for s in range(n_species)]
            absorber.append(weighted(line, conc))
            for e in range(n_early):
                emit_ref[e, x] = weighted([sigma[s][e] for s in range(n_species)], conc)
        sums = jnp.dot(split(jnp.concatenate(absorber, axis=0)), table, preferred_element_type=F32)
        for q, x in enumerate(range(start, end)):
            here = sums[q * depth : (q + 1) * depth]
            beyond_ref[x] = here[:, :width]
            total = jnp.where(lane == x % LANES, here[:, width : width + LANES], total)
            if (x + 1) % LANES == 0:
                total_ref[:, x + 1 - LANES : x + 1] = total


def local_body(scale, plane_ref, conc_ref, early_ref, beyond_ref, trans_ref, emit_ref, pair_ref):
    n_energy, rows, depth, width = trans_ref.shape
    n_species, n_early = conc_ref.shape[0], early_ref.shape[0]
    sigma = [[v * scale for v in row] for row in planes(plane_ref, n_species, n_energy)[0]]

    def step(block, carry):
        path, sums = list(carry[:n_energy]), list(carry[n_energy:])
        for q in range(STEP):
            x = block * STEP + q
            beyond = beyond_ref[x]
            conc = [conc_ref[s, x] for s in range(n_species)]
            for e in range(n_energy):
                if e < n_early:
                    emission = early_ref[e, x]
                else:
                    emission = weighted([sigma[s][e] for s in range(n_species)], conc)
                trans = jnp.exp2(path[e] + beyond)
                trans_ref[e, x] = trans
                emit = emission * trans
                emit_ref[e, x] = emit
                path[e] = path[e] + emission
                sums[e] = sums[e] + emit
        return tuple(path + sums)

    zero = jnp.zeros((depth, width), F32)
    carry = lax.fori_loop(0, rows // STEP, step, (zero,) * (2 * n_energy))
    for e in range(n_energy):
        pair_ref[0, e] = carry[e]
        pair_ref[1, e] = carry[n_energy + e]


def columns(source_ref, change, width):
    depth, rows = source_ref.shape
    for part in range(rows // LANES):
        held = change(source_ref[:, part * LANES : (part + 1) * LANES])
        for q in range(LANES):
            yield part * LANES + q, jnp.broadcast_to(held[:, q : q + 1], (depth, width))


def line_body(count, far_ref, emit_ref, local_ref, far_out, pair_ref):
    n_energy, _, _, width = emit_ref.shape
    last = lax.axis_index("det") == count - 1

    @pl.when(last)
    def _():
        pair_ref[...] = local_ref[...]

    @pl.when(jnp.logical_not(last))
    def _():
        sums = [[None, None] for _ in range(n_energy)]
        for x, factor in columns(far_ref, jnp.exp2, width):
            far_out[x] = factor
            for e in range(n_energy):
                value = factor * emit_ref[e, x]
                sums[e][x % 2] = value if x < 2 else sums[e][x % 2] + value
        for e in range(n_energy):
            pair_ref[0, e] = local_ref[0, e]
            pair_ref[1, e] = sums[e][0] + sums[e][1]


def merge_body(*refs):
    pairs, (total_ref, up_ref, further_ref) = refs[:-3], refs[-3:]
    beam = lax.axis_index("beam")
    state = [(ref[0], ref[1]) for ref in pairs]
    up, further = jnp.zeros_like(state[0][0]), jnp.zeros_like(state[0][0])
    distance = 1
    while len(state) > 1:
        lower = (beam & distance) == 0
        merged = []
        for i in range(0, len(state), 2):
            (span, sums), (other_span, other_sums) = state[i], state[i + 1]
            fade = jnp.exp2(jnp.where(lower, span, other_span))
            late = fade * jnp.where(lower, other_sums, sums)
            if i == 0:
                further = jnp.where(lower, further + late, fade * further)
                up = jnp.where(lower, up, up + other_span)
            merged.append((span + other_span, jnp.where(lower, sums, other_sums) + late))
        state = merged
        distance *= 2
    total_ref[0] = state[0][1]
    up_ref[...] = up
    further_ref[...] = further


def ahead_body(count, far_ref, trans_ref, emit_ref, fluor_ref, rest_ref):
    n_energy, rows, depth, width = emit_ref.shape

    last = lax.axis_index("det") == count - 1

    def step(block, ahead):
        ahead = list(ahead)
        for q in range(STEP):
            x = rows - 1 - (block * STEP + q)
            far = jnp.where(last, 1.0, far_ref[x])
            for e in range(n_energy):
                fluor = far * emit_ref[e, x]
                fluor_ref[e, x] = fluor
                rest_ref[e, x] = far * trans_ref[e, x] + ahead[e]
                ahead[e] = ahead[e] + LN2 * fluor
        return tuple(ahead)

    zero = jnp.zeros((depth, width), F32)
    lax.fori_loop(0, rows // STEP, step, (zero,) * n_energy)


def fan_body(scale, near_slabs, offset_ref, weight_ref, measured_ref, own_ref, gram_ref, pull_ref, turned_ref):
    depth, n_slab = gram_ref.shape[0], turned_ref.shape[1] // gram_ref.shape[0]
    taps, pixels = weight_ref.shape
    own = lax.axis_index("slab")
    offset = jnp.broadcast_to(offset_ref[...], (depth, pixels))
    level = lax.broadcasted_iota(jnp.int32, (depth, pixels), 0) - offset
    taps = [jnp.broadcast_to(weight_ref[j : j + 1, :], (depth, pixels)).astype(F32) for j in range(taps)]

    def block(slab):
        place = level + slab * depth
        found = jnp.zeros((depth, pixels), F32)
        for j, tap in enumerate(taps):
            found = found + jnp.where(place == j, tap, 0.0)
        return found

    blocks = [block(own ^ r) for r in range(n_slab)]
    turned_ref[...] = jnp.concatenate(blocks, axis=0).T
    odd = own + jnp.where((own & 1) == 1, 1, -1)
    near = jnp.concatenate([block(odd) if r is None else blocks[r] for r in near_slabs], axis=0)
    gram = lax.dot_general(
        blocks[0].astype(BF16), near.astype(BF16), (((1,), (1,)), ((), ())), preferred_element_type=F32
    )
    gram_ref[...] = gram
    n_energy, _, width = pull_ref.shape
    sums = weigh(gram, [(0, own_ref, 0)], depth, n_energy, width)
    for e in range(n_energy):
        pull_ref[e] = sums[e] * scale - jnp.dot(
            blocks[0], measured_ref[e], precision=lax.Precision.HIGHEST, preferred_element_type=F32
        )


def weigh(weights, lines, depth, n_energy, width):
    height = weights.shape[0]
    sums = [[None, None] for _ in range(n_energy)]
    for order, (r, lines_ref, i) in enumerate(lines):
        for z in range(depth):
            place = r * depth + z
            weight = jnp.broadcast_to(weights[:, place : place + 1], (height, width))
            for e in range(n_energy):
                value = weight * lines_ref[i, e, z : z + 1, :]
                sums[e][z % 2] = value if order == 0 and z < 2 else sums[e][z % 2] + value
    return [a + b for a, b in sums]


def back_body(scale, count, plane_ref, gram_ref, pull_ref, up_ref, further_ref, fluor_ref, *refs):
    lines, (near_ref, total_ref, gain_ref, shift_ref) = refs[:-4], refs[-4:]
    n_energy, _, depth, width = fluor_ref.shape
    n_species = shift_ref.shape[0]
    sums = weigh(gram_ref[...], [(r + 1, ref, 0) for r, ref in enumerate(lines)], depth, n_energy, width)
    back = [sums[e] * scale + pull_ref[e] for e in range(n_energy)]
    gain = [back[e] * jnp.exp2(up_ref[e]) for e in range(n_energy)]
    sigma, _ = planes(plane_ref, n_species, n_energy)
    pushed = [LN2 * back[e] * further_ref[e] for e in range(n_energy)]
    for e in range(n_energy):
        gain_ref[e] = gain[e]
    for s in range(n_species):
        shift_ref[s] = weighted(sigma[s], pushed)
    last = jnp.logical_and(lax.axis_index("det") == count - 1, count > 1)

    @pl.when(jnp.logical_not(last))
    def _():
        column_sums(gain, fluor_ref, near_ref, total_ref)

    @pl.when(last)
    def _():
        total_ref[...] = jnp.zeros_like(total_ref)


def column_sums(gain, fluor_ref, near_ref, total_ref):
    n_energy, rows, depth, width = fluor_ref.shape
    table = lane_sums(width, False)
    lane = lax.broadcasted_iota(jnp.int32, (depth, LANES), 1)
    total = jnp.zeros((depth, LANES), F32)
    for start in range(0, rows, CHUNK):
        span = range(start, start + CHUNK)
        heavy = [weighted(gain, [fluor_ref[e, x] for e in range(n_energy)]) for x in span]
        found = jnp.dot(split(jnp.concatenate(heavy, axis=0)), table, preferred_element_type=F32)
        for q, x in enumerate(span):
            here = found[q * depth : (q + 1) * depth]
            near_ref[x] = here[:, :width]
            if total_ref is not None:
                total = jnp.where(lane == x % LANES, here[:, width : width + LANES], total)
        if total_ref is not None and (start + CHUNK) % LANES == 0:
            total_ref[:, start + CHUNK - LANES : start + CHUNK] = total


def out_copies(source_ref, out_hbm, sems, ends, chunk):
    start = ends[chunk - 1] if chunk else 0
    span = pl.ds(start, ends[chunk] - start)
    return [
        pltpu.make_async_copy(source_ref.at[:, span, z, :], out_hbm.at[:, z, span, :], sems.at[chunk])
        for z in range(out_hbm.shape[1])
    ]


def out_wait(source_ref, sems, ends, chunk):
    start = ends[chunk - 1] if chunk else 0
    whole = source_ref.at[:, pl.ds(start, ends[chunk] - start)]
    pltpu.make_async_copy(whole, whole, sems.at[chunk]).wait()


def out_ends(rows):
    return [rows * part // 16 for part in (1, 4, 8, 12, 16)]


def mix_body(
    scale_line, count, plane_ref, gain_ref, shift_ref, rest_ref, fluor_ref, near_ref,
    out_ref, last_ref, grad_hbm, sems,
):
    n_energy, rows, _, _ = rest_ref.shape
    n_species = out_ref.shape[0]
    sigma, line = planes(plane_ref, n_species, n_energy)
    mixed = [[sigma[s][e] * gain_ref[e] for e in range(n_energy)] for s in range(n_species)]
    shift = [shift_ref[s] for s in range(n_species)]
    place = lax.axis_index("det")

    @pl.when(place == 0)
    def _():
        ends = out_ends(rows)
        scaled = [v * scale_line for v in line]
        for x in range(rows):
            rest = [rest_ref[e, x] for e in range(n_energy)]
            before = near_ref[x]
            for s in range(n_species):
                out_ref[s, x] = weighted(mixed[s], rest) + (shift[s] + scaled[s] * before)
            if x + 1 in ends:
                for copy in out_copies(out_ref, grad_hbm, sems, ends, ends.index(x + 1)):
                    copy.start()
        for chunk in range(len(ends)):
            out_wait(out_ref, sems, ends, chunk)

    @pl.when(place != 0)
    def _():
        def step(block, carry):
            for q in range(STEP):
                x = block * STEP + q
                rest = [rest_ref[e, x] for e in range(n_energy)]
                for s in range(n_species):
                    out_ref[s, x] = weighted(mixed[s], rest) + shift[s]
            return carry

        lax.fori_loop(0, rows // STEP, step, 0)

    if count > 1:

        @pl.when(place == count - 1)
        def _():
            column_sums([gain_ref[e] for e in range(n_energy)], fluor_ref, last_ref, None)


def residual_copy(scale, fan_ref, measured_ref, lines, residual_ref, residual_hbm, sem):
    n_energy, share, width = residual_ref.shape
    start = pl.multiple_of(lax.axis_index(("beam", "slab")) * share, share)
    pieces = [(ref, i) for ref in lines for i in range(ref.shape[0])]
    pieces = [(r, ref, i) for r, (ref, i) in enumerate(pieces)]
    depth = fan_ref.shape[1] // len(pieces)
    sums = weigh(fan_ref[pl.ds(start, share), :], pieces, depth, n_energy, width)
    for e in range(n_energy):
        residual_ref[e] = sums[e] * scale - measured_ref[e, pl.ds(start, share), :]
    copy = pltpu.make_async_copy(residual_ref, residual_hbm, sem)
    copy.start()
    return copy


def signal_body(scale, fan_ref, measured_ref, *refs):
    lines, (residual_hbm, residual_ref, sem) = refs[:-3], refs[-3:]

    @pl.when(lax.axis_index("det") == 0)
    def _():
        residual_copy(scale, fan_ref, measured_ref, lines, residual_ref, residual_hbm, sem).wait()


def finish_body(
    scale, scale_line, count, plane_ref, nearer_ref, near_ref, last_ref, mix_ref, fan_ref, measured_ref,
    grad_in, residual_in, *refs,
):
    lines, (grad_hbm, residual_hbm, grad_ref, residual_ref, sems, residual_sem) = refs[:-6], refs[-6:]
    n_species, rows, _, width = mix_ref.shape
    n_energy = residual_ref.shape[0]
    place = lax.axis_index("det")
    ends = out_ends(rows)

    @pl.when(place != 0)
    def _():
        line = [v * scale_line for v in planes(plane_ref, n_species, n_energy)[1]]
        last = place == count - 1
        for x, column in columns(nearer_ref, lambda v: v, width):
            before = jnp.where(last, last_ref[x], near_ref[x]) + column
            for s in range(n_species):
                grad_ref[s, x] = mix_ref[s, x] + line[s] * before
            if x + 1 in ends:
                for copy in out_copies(grad_ref, grad_hbm, sems, ends, ends.index(x + 1)):
                    copy.start()
        copy = residual_copy(scale, fan_ref, measured_ref, lines, residual_ref, residual_hbm, residual_sem)
        for chunk in range(len(ends)):
            out_wait(grad_ref, sems, ends, chunk)
        copy.wait()


def odd_pairs(n_beam, n_slab):
    pairs = []
    for beam in range(n_beam):
        for slab in range(n_slab):
            other = slab + 1 if slab % 2 else slab - 1
            if 0 <= other < n_slab:
                target = beam * n_slab + other
            else:
                target = (beam ^ 1) * n_slab + slab
            pairs.append((beam * n_slab + slab, target))
    return pairs


def swap(value, axis, distance):
    return lax.ppermute(value, axis, [(i, i ^ distance) for i in range(lax.axis_size(axis))])


def beyond(value, axis, backward):
    count = lax.axis_size(axis)
    if count == 2:
        return swap(value, axis, 1)
    mine = lax.axis_index(axis)
    pieces = lax.all_gather(value, axis)
    places = jnp.arange(count)
    keep = (places < mine) if backward else (places > mine)
    return jnp.sum(jnp.where(keep.reshape((-1,) + (1,) * value.ndim), pieces, 0.0), axis=0)


def shards(conc, cross, line, index, fan_offset, fan_weight, measured):
    n_species, depth, rows, width = conc.shape
    n_energy = index.shape[0]
    n_beam, n_det, n_slab = (lax.axis_size(a) for a in ("beam", "det", "slab"))
    assert n_beam & (n_beam - 1) == 0 and n_slab & (n_slab - 1) == 0
    assert fan_weight.shape[1] <= depth + 1
    assert rows % LANES == 0 and width % LANES == 0 and depth % 8 == 0
    full_x, full_y = rows * n_beam, width * n_det
    scale_x = -(1.5 / full_x) * LOG2E
    scale_y = -(1.5 / full_y) * LOG2E
    scale_sum = 1.0 / (scale_x * full_x)
    voxels = depth * rows * width
    turned = (n_species, rows, depth, width)
    cube = VMEM((n_energy, rows, depth, width), F32)
    plane = VMEM((rows, depth, width), F32)

    n_early = (n_energy + 3) // 4
    conc_x, emission, far_local, row_total, fixed = call(
        functools.partial(load_body, scale_y, scale_x),
        (VMEM(turned, F32), VMEM((n_early, rows, depth, width), F32), plane, plain(depth, rows),
         VMEM((n_species * n_energy + n_species, depth, width), F32)),
        (VMEM,) * 5,
        (HBM,) * 4,
        [
            SMEM(line.shape, F32),
            SMEM(cross.shape, F32),
            SMEM(index.shape, index.dtype),
            pltpu.SemaphoreType.DMA((3,)),
            pltpu.SemaphoreType.DMA((len(in_ends(rows)),)),
        ],
        cost=(40 * voxels, 0, 16 * voxels),
    )(*(pltpu.with_memory_space_constraint(v, HBM) for v in (line, cross, index, conc)))

    far = beyond(row_total, "det", False)

    trans, emit, local_pair = call(
        functools.partial(local_body, scale_x),
        (cube, cube, plain(2, n_energy, depth, width)),
        (VMEM, VMEM, VMEM),
        (VMEM,) * 4,
        cost=(20 * voxels, 4 * voxels, 1024),
    )(fixed, conc_x, emission, far_local)

    wide = (n_energy, depth, width)
    far_wide, pair = call(
        functools.partial(line_body, n_det), (plane, plain(2, *wide)), (VMEM,) * 2, (VMEM,) * 3,
        cost=(8 * voxels, 0, 1024),
    )(far, emit, local_pair)

    fluor, rest = call(
        functools.partial(ahead_body, n_det), (cube, cube), (VMEM, VMEM), (VMEM, VMEM, VMEM),
        cost=(20 * voxels, 0, 1024),
    )(far_wide, trans, emit)

    others = []
    for r in range(1, n_beam):
        others.append(swap(pair, "beam", r))
    if others:
        others[-1], fluor, rest = lax.optimization_barrier((others[-1], fluor, rest))
    total, up, further = call(
        merge_body, (plain(1, *wide), plain(*wide), plain(*wide)), (VMEM,) * 3, (VMEM,) * n_beam,
        cost=(1 << 15, 1 << 13, 1024),
    )(pair, *others)

    if n_slab == 4 and n_beam > 1:
        even = swap(total, "slab", 1)
        odd = lax.ppermute(total, ("beam", "slab"), odd_pairs(n_beam, n_slab))
        near_lines = [total, even, odd]
        near_slabs = [0, 1, None]
        half = jnp.concatenate([total, even], axis=0)
        lines = [total, even, swap(half, "slab", 2)]
    else:
        lines = [total] + [swap(total, "slab", r) for r in range(1, n_slab)]
        near_slabs = [r for r in range(n_slab) if r & (r + 1) == 0]
        near_lines = [lines[r] for r in near_slabs]

    pixels = fan_offset.shape[0]
    gram, pull, fan_turned = call(
        functools.partial(fan_body, scale_sum, near_slabs), (plain(depth, depth * len(near_slabs)), plain(*wide), plain(pixels, depth * n_slab)),
        (VMEM,) * 3, (VMEM,) * 4, cost=(8 * depth * measured.size, 0, 4 * measured.size),
    )(fan_offset[None, :], fan_weight.T, measured, total)

    near, column_total, gain, shift = call(
        functools.partial(back_body, scale_sum, n_det),
        (plane, plain(depth, rows), plain(*wide), plain(n_species, depth, width)),
        (VMEM,) * 4,
        (VMEM,) * (5 + len(near_lines)),
        cost=(10 * voxels, 0, 1024),
    )(fixed, gram, pull, up, further, fluor, *near_lines[1:])

    nearer = beyond(column_total, "det", True)

    scale_line = scale_y * LN2 / scale_x
    out_sems = pltpu.SemaphoreType.DMA((len(out_ends(rows)),))
    mixed, near_last, grad = call(
        functools.partial(mix_body, scale_line, n_det),
        (VMEM(turned, F32), plane, HBM(conc.shape, F32)),
        (VMEM, VMEM, HBM),
        (VMEM,) * 6,
        [out_sems],
        cost=(40 * voxels, 0, 1024),
    )(fixed, gain, shift, rest, fluor, near)

    share = pixels // (n_beam * n_slab)
    residual_scratch = [VMEM((n_energy, share, width), F32), pltpu.SemaphoreType.DMA]
    residual = call(
        functools.partial(signal_body, scale_sum),
        (HBM((n_energy, share, width), F32),),
        (HBM,),
        (VMEM,) * (2 + len(lines)),
        residual_scratch,
        cost=(1 << 16, 0, 1024),
    )(fan_turned, measured, *lines)[0]

    return tuple(
        call(
            functools.partial(finish_body, scale_sum, scale_line, n_det),
            (plain(*conc.shape), plain(n_energy, share, width)),
            (HBM, HBM),
            (VMEM,) * 7 + (HBM,) * 2 + (VMEM,) * len(lines),
            [VMEM(turned, F32), residual_scratch[0], out_sems, residual_scratch[1]],
            limit=16,
            cost=(10 * voxels, 0, 16 * voxels),
            aliases={7: 0, 8: 1},
        )(fixed, nearer, near, near_last, mixed, fan_turned, measured, grad, residual, *lines)
    )


def solution(mesh):
    in_specs = (P(None, "slab", "beam", "det"), P(), P(), P(), P(), P(), P(None, None, "det"))
    out_specs = (P(None, "slab", "beam", "det"), P(None, ("beam", "slab"), "det"))
    return jax.shard_map(shards, mesh=mesh, in_specs=in_specs, out_specs=out_specs, check_vma=False)
```
